32 devices in a mesh: seq: 8 (over z, x), tp: 4 (over y, core).
Axes of the slice: x: 2, y: 2, z: 4, core: 2. Of those that a mesh axis runs over, the one named last changes fastest.
Arguments:
- tokens: bfloat16 [2048, 1536], P('seq'), may hold values from -6 to 6
- norm1_gain: bfloat16 [1536], replicated, may hold values from 0.25 to 1.75
- w_query: bfloat16 [1536, 1536], P('tp'), may hold values from -0.15625 to 0.15625
- key_weight: bfloat16 [512, 1536], P('tp'), may hold values from -0.4375 to 0.4375
- value_weight: bfloat16 [512, 1536], P('tp'), may hold values from -0.15625 to 0.15625
- rotated_key_cache: bfloat16 [4, 8, 524288], P(None, 'tp', 'seq'), may hold values from -60 to 60
- stored_value_cache: bfloat16 [4, 8, 524288], P(None, 'tp', 'seq'), may hold values from -6 to 6
- cache_len: int32 [4], replicated, may hold values from 1 to 8192, 16384 in all
- w_out: bfloat16 [1536, 1536], P('tp'), may hold values from -0.15625 to 0.15625
- norm2_gain: bfloat16 [1536], replicated, may hold values from 0.25 to 1.75
- w_router: bfloat16 [1536, 40], replicated, may hold values from -0.0546875 to 0.0546875
- expert_ids: int32 [2048, 8], P('seq'), may hold values from 0 to 39, all different within a row
- w_gate_up: bfloat16 [40, 2, 1536, 512], P('tp', None, 'seq'), may hold values from -0.15625 to 0.15625
- w_down: bfloat16 [40, 512, 1536], P('tp', 'seq'), may hold values from -0.5 to 0.5
Outputs:
- attn_out: bfloat16 [2048, 1536], P('seq')
- expert_out: bfloat16 [2048, 1536], P('seq')
The draws below stay inside these ranges and needn't reach their ends.
Inputs may be any that keep to these rules, and one draw needn't show every extreme that they name: `cache_len`: request lengths of 1 to 8192; one request fills all 8192 positions. `expert_ids`: each row names 8 different experts; every expert is named.
All inputs are finite; a program needn't handle non-finite values.
Results may differ from the reference program's by a relative error of at most 0.03.
Values may be sent and summed in bfloat16 or wider, within the bound.
A program may use at most 192 MiB of HBM per device.

```python
import math
import jax
import jax.numpy as jnp
import numpy as np
from jax import lax

MODEL_WIDTH = 1536
QUERY_HEADS = 24
KEY_VALUE_HEADS = 8
HEAD_SIZE = 64
EXPERTS = 40
FFE = 512
TOPK = 8
FRESH_TOKENS = 512
CACHE_LENGTH = 8192
REQUEST_COUNT = 4
TOKENS = 2048


def draw_rotated_key_cache(key, part):
    array_shape = (REQUEST_COUNT, KEY_VALUE_HEADS, CACHE_LENGTH, HEAD_SIZE)
    base_values = jnp.clip(3.0 * jax.random.normal(key, array_shape, jnp.float32), -18.0, 18.0)
    magnitude = jax.random.uniform(jax.random.fold_in(key, 31), (REQUEST_COUNT, KEY_VALUE_HEADS, 1, HEAD_SIZE), jnp.float32, 45.0, 57.0)
    signs = jnp.where(jax.random.bernoulli(jax.random.fold_in(key, 37), 0.5, (REQUEST_COUNT, KEY_VALUE_HEADS, 1, HEAD_SIZE)), 1.0, -1.0)
    loud_key = magnitude * signs
    spot = jax.random.randint(jax.random.fold_in(key, 41), (REQUEST_COUNT, 1, 1, 1), 2, CACHE_LENGTH - 1)
    where_pos = jnp.arange(CACHE_LENGTH, dtype=jnp.int32)[None, None, :, None]
    first_loud = (where_pos == 0) | (where_pos == spot)
    second_loud = (where_pos == 1) | (where_pos == spot + 1)
    factor = jnp.where(first_loud, 1.0, jnp.where(second_loud, 1.02, 0.0))
    mixed = jnp.where(factor > 0.0, loud_key * factor, base_values)
    return mixed.reshape(REQUEST_COUNT, KEY_VALUE_HEADS, CACHE_LENGTH * HEAD_SIZE).astype(jnp.bfloat16)


def block_scale(rng, dims, split, least, high):
    def one(axis_at, parts):
        heights = jax.random.uniform(jax.random.fold_in(jax.random.fold_in(rng, 6), axis_at), (parts,), jnp.float32, least / len(split), high / len(split))
        return jnp.repeat(jnp.exp(heights), dims[axis_at] // parts).reshape((-1,) + (1,) * (len(dims) - axis_at - 1))

    factor_of = one(*split[0])
    for cut in split[1:]:
        factor_of = factor_of * one(*cut)
    return factor_of


def different_ones(stream_key, rows, count, top, lift):
    sequence = jax.random.permutation(jax.random.fold_in(stream_key, 1), count)
    boost = sequence
    for power in range(3):
        boost = boost * boost // count
    boost = boost * lift // count
    chance = jax.random.randint(jax.random.fold_in(stream_key, 2), (rows, count), 0, 4096) + boost
    sure = jax.random.permutation(jax.random.fold_in(stream_key, 3), rows)[jnp.arange(count) % rows]
    chance = jnp.where(jnp.arange(rows)[:, None] == sure[None, :], 1 << 14, chance)
    merit = chance * count + jnp.arange(count)
    return lax.top_k(merit.astype(jnp.int32), top)[1].astype(jnp.int32)


def split_up(amount, total, most, slope):
    loads = [(1 << 20) // math.isqrt(standing ** slope) + 1 for standing in range(2, amount + 1)]
    rest, counts = total - most - (amount - 1), [1] * (amount - 1)
    while rest > 0:
        movable = [i for i in range(amount - 1) if counts[i] < most]
        pool, budget = sum([loads[i] for i in movable]), rest
        for i in movable:
            more = min(most - counts[i], max(1, budget * loads[i] // pool), rest)
            counts[i] = counts[i] + more
            rest = rest - more
    return np.array([most] + counts)


def uneven_parts(stream_key, count, total, bound, skew):
    if count == 2:
        one = jax.random.randint(stream_key, (), max(1, total - bound), min(bound, total - 1) + 1)
        return jnp.stack([one, total - one])
    sizes = jnp.asarray(split_up(count, total, bound, skew), jnp.int32)
    twos = (count - 1) // 2
    source_of, taker = sizes[1:1 + 2 * twos:2], sizes[2:2 + 2 * twos:2]
    slack = jnp.minimum(source_of - 1, bound - taker)
    passed = jax.random.randint(jax.random.fold_in(stream_key, 1), (twos,), 0, 1 << 20) % (slack + 1)
    sizes = sizes.at[1:1 + 2 * twos:2].set(source_of - passed).at[2:2 + 2 * twos:2].set(taker + passed)
    return sizes[jax.random.permutation(jax.random.fold_in(stream_key, 2), count)]


def gaussian(key, dims, deviation, limit, shards=(), kind=jnp.bfloat16):
    values = deviation * jax.random.normal(key, dims, jnp.float32)
    if shards:
        values = values * block_scale(key, dims, shards, -0.22, 0.18)
    return jnp.clip(values, -limit, limit).astype(kind)


def setup_inputs(seed: int = 0) -> dict:
    splits = jax.random.split(jax.random.key(seed), 15)
    tokens = gaussian(splits[0], (TOKENS, MODEL_WIDTH), 1.0, 6.0, ((0, 8),))
    norm1_gain = jnp.clip(1.0 + 0.15 * jax.random.normal(splits[1], (MODEL_WIDTH,), jnp.float32), 0.25, 1.75).astype(jnp.bfloat16)
    w_query = gaussian(splits[2], (QUERY_HEADS * HEAD_SIZE, MODEL_WIDTH), MODEL_WIDTH ** -0.5, 0.15625, ((0, 4),))
    key_weight = gaussian(splits[3], (KEY_VALUE_HEADS * HEAD_SIZE, MODEL_WIDTH), (MODEL_WIDTH // 9) ** -0.5, 0.4375, ((0, 4),))
    value_weight = gaussian(splits[4], (KEY_VALUE_HEADS * HEAD_SIZE, MODEL_WIDTH), MODEL_WIDTH ** -0.5, 0.15625, ((0, 4),))
    rotated_key_cache = draw_rotated_key_cache(jax.random.fold_in(splits[14], 71), 0)
    stored_value_cache = gaussian(splits[6], (REQUEST_COUNT, KEY_VALUE_HEADS, CACHE_LENGTH * HEAD_SIZE), 1.0, 6.0, ((1, 4), (2, 8)))
    cache_len = uneven_parts(splits[7], REQUEST_COUNT, REQUEST_COUNT * CACHE_LENGTH // 2, CACHE_LENGTH, 2).astype(jnp.int32)
    w_out = gaussian(splits[8], (QUERY_HEADS * HEAD_SIZE, MODEL_WIDTH), (QUERY_HEADS * HEAD_SIZE) ** -0.5, 0.15625, ((0, 4),))
    norm2_gain = jnp.clip(1.0 + 0.15 * jax.random.normal(splits[9], (MODEL_WIDTH,), jnp.float32), 0.25, 1.75).astype(jnp.bfloat16)
    w_router = gaussian(splits[10], (MODEL_WIDTH, EXPERTS), (MODEL_WIDTH * 8) ** -0.5, 0.0546875)
    expert_ids = different_ones(splits[11], TOKENS, EXPERTS, TOPK, 3276)
    w_gate_up = gaussian(splits[12], (EXPERTS, 2, MODEL_WIDTH, FFE), MODEL_WIDTH ** -0.5, 0.15625, ((0, 4), (2, 8)))
    w_down = gaussian(splits[13], (EXPERTS, FFE, MODEL_WIDTH), (FFE // 4) ** -0.5, 0.5, ((0, 4), (1, 8)))
    return {"tokens": tokens, "norm1_gain": norm1_gain, "w_query": w_query, "key_weight": key_weight, "value_weight": value_weight, "rotated_key_cache": rotated_key_cache, "stored_value_cache": stored_value_cache, "cache_len": cache_len, "w_out": w_out, "norm2_gain": norm2_gain, "w_router": w_router, "expert_ids": expert_ids, "w_gate_up": w_gate_up, "w_down": w_down}


EPS = 1e-05
THETA = 10000.0

def rms_norm(values, gain):
    mean_square = lax.optimization_barrier(jnp.mean(values * values, axis=-1, keepdims=True))
    return values * lax.rsqrt(mean_square + EPS) * gain.astype(values.dtype)

def apply_rotary(values, positions):
    half_dim = values.shape[-1] // 2
    exponent = jnp.arange(half_dim, dtype=jnp.float32) * (2.0 / values.shape[-1])
    freqs = THETA ** (-exponent)
    angles = positions[:, None] * freqs[None, :]
    cosine = jnp.cos(angles)[:, None, :]
    sine = jnp.sin(angles)[:, None, :]
    first = values[..., :half_dim]
    second = values[..., half_dim:]
    return jnp.concatenate([first * cosine - second * sine, second * cosine + first * sine], axis=-1)

def apply_projection(normalized_input, weight):
    return jnp.einsum('td,fd->tf', normalized_input, weight, preferred_element_type=jnp.float32)

def reference(tokens, norm1_gain, w_query, key_weight, value_weight, rotated_key_cache, stored_value_cache, cache_len, w_out, norm2_gain, w_router, expert_ids, w_gate_up, w_down):
    token_count = tokens.shape[0]
    query_group = QUERY_HEADS // KEY_VALUE_HEADS
    scale = HEAD_SIZE ** (-0.5)
    inputs = tokens.astype(jnp.float32)
    normalized_input = rms_norm(inputs, norm1_gain).astype(jnp.bfloat16)
    row_ids = jnp.arange(token_count, dtype=jnp.int32)
    owners = row_ids // FRESH_TOKENS
    positions = (cache_len[owners] + row_ids % FRESH_TOKENS).astype(jnp.int32)
    angle_position = positions.astype(jnp.float32)
    query_vector = apply_rotary(apply_projection(normalized_input, w_query).reshape(token_count, QUERY_HEADS, HEAD_SIZE), angle_position).astype(jnp.bfloat16)
    fresh_key = apply_rotary(apply_projection(normalized_input, key_weight).reshape(token_count, KEY_VALUE_HEADS, HEAD_SIZE), angle_position).astype(jnp.bfloat16)
    fresh_value = apply_projection(normalized_input, value_weight).astype(jnp.bfloat16).reshape(token_count, KEY_VALUE_HEADS, HEAD_SIZE)
    cache_pos = jnp.arange(CACHE_LENGTH, dtype=jnp.int32)

    def one_request(request_index):
        length = lax.dynamic_index_in_dim(cache_len, request_index, 0, keepdims=False)
        start_position = (request_index * FRESH_TOKENS).astype(jnp.int32)
        query_rows = lax.dynamic_slice_in_dim(query_vector, start_position, FRESH_TOKENS, 0).reshape(FRESH_TOKENS, KEY_VALUE_HEADS, query_group, HEAD_SIZE).astype(jnp.float32)
        query_pos = length + jnp.arange(FRESH_TOKENS, dtype=jnp.int32)
        prior_keys = jnp.transpose(lax.dynamic_index_in_dim(rotated_key_cache, request_index, 0, keepdims=False).reshape(KEY_VALUE_HEADS, CACHE_LENGTH, HEAD_SIZE), (1, 0, 2))
        prior_values = jnp.transpose(lax.dynamic_index_in_dim(stored_value_cache, request_index, 0, keepdims=False).reshape(KEY_VALUE_HEADS, CACHE_LENGTH, HEAD_SIZE), (1, 0, 2))
        keys = jnp.concatenate([prior_keys, lax.dynamic_slice_in_dim(fresh_key, start_position, FRESH_TOKENS, 0)], axis=0).astype(jnp.float32)
        values = jnp.concatenate([prior_values, lax.dynamic_slice_in_dim(fresh_value, start_position, FRESH_TOKENS, 0)], axis=0).astype(jnp.float32)
        key_pos = jnp.concatenate([cache_pos, query_pos])
        usable = jnp.concatenate([cache_pos < length, jnp.ones((FRESH_TOKENS,), dtype=bool)])
        allowed = usable[None, :] & (key_pos[None, :] <= query_pos[:, None])

        def single_head(head):
            head_q = lax.dynamic_index_in_dim(query_rows, head, 1, keepdims=False)
            head_k = lax.dynamic_index_in_dim(keys, head, 1, keepdims=False)
            head_v = lax.dynamic_index_in_dim(values, head, 1, keepdims=False)
            scores = jnp.einsum('ngd,kd->gnk', head_q, head_k) * scale
            scores = jnp.where(allowed[None], scores, -jnp.inf)
            peak = lax.optimization_barrier(jnp.max(scores, axis=-1, keepdims=True))
            weights = jnp.where(allowed[None], jnp.exp(scores - peak), 0.0)
            total = lax.optimization_barrier(jnp.sum(weights, axis=-1))
            mixed = jnp.einsum('gnk,kd->ngd', weights.astype(jnp.bfloat16).astype(jnp.float32), head_v)
            return mixed / jnp.transpose(total, (1, 0))[:, :, None]
        head_list = lax.map(single_head, jnp.arange(KEY_VALUE_HEADS, dtype=jnp.int32))
        return jnp.transpose(head_list, (1, 0, 2, 3)).reshape(FRESH_TOKENS, QUERY_HEADS * HEAD_SIZE).astype(jnp.bfloat16)
    attention = lax.map(one_request, jnp.arange(REQUEST_COUNT, dtype=jnp.int32)).reshape(token_count, QUERY_HEADS * HEAD_SIZE)
    attn = jnp.dot(attention, w_out, preferred_element_type=jnp.float32)
    attn_out = attn.astype(jnp.bfloat16)
    normed2 = rms_norm(inputs + attn, norm2_gain).astype(jnp.bfloat16)
    logits = jnp.dot(normed2, w_router, preferred_element_type=jnp.float32)
    chosen = jnp.take_along_axis(logits, expert_ids, axis=1)
    gates = jax.nn.softmax(chosen, axis=-1)
    picked = expert_ids[:, :, None] == jnp.arange(EXPERTS, dtype=jnp.int32)[None, None, :]
    share = lax.optimization_barrier(jnp.sum(jnp.where(picked, gates[:, :, None], 0.0), axis=1))

    def one_expert(running, expert):
        both = lax.dynamic_index_in_dim(w_gate_up, expert, 0, keepdims=False)
        gate = jnp.dot(normed2, both[0], preferred_element_type=jnp.float32)
        upward = jnp.dot(normed2, both[1], preferred_element_type=jnp.float32)
        column = lax.dynamic_index_in_dim(share, expert, 1, keepdims=True)
        hidden = (jax.nn.silu(gate) * upward * column).astype(jnp.bfloat16)
        down = lax.dynamic_index_in_dim(w_down, expert, 0, keepdims=False)
        return (running + jnp.dot(hidden, down, preferred_element_type=jnp.float32), None)
    moe, unused = lax.scan(one_expert, jnp.zeros((token_count, MODEL_WIDTH), jnp.float32), jnp.arange(EXPERTS, dtype=jnp.int32))
    return (attn_out, moe.astype(jnp.bfloat16))
```

```python
import functools

import jax
import jax.numpy as jnp
from jax import lax
from jax.experimental import pallas as pl
from jax.experimental.pallas import tpu as pltpu
from jax.sharding import PartitionSpec as P

HEAD_SIZE = 64
FRESH_TOKENS = 512


EPS = 1e-05
THETA = 10000.0
NEGATIVE = -1e30


def rms_norm(values, gain):
    mean_square = jnp.mean(values * values, axis=-1, keepdims=True)
    return values * lax.rsqrt(mean_square + EPS) * gain.astype(values.dtype)


def apply_rotary(values, positions):
    half_dim = values.shape[-1] // 2
    exponent = jnp.arange(half_dim, dtype=jnp.float32) * (2.0 / values.shape[-1])
    freqs = THETA ** (-exponent)
    angles = positions[:, None] * freqs[None, :]
    cosine = jnp.cos(angles)[:, None, :]
    sine = jnp.sin(angles)[:, None, :]
    first = values[..., :half_dim]
    second = values[..., half_dim:]
    return jnp.concatenate(
        [first * cosine - second * sine, second * cosine + first * sine], axis=-1
    )


def apply_projection(normalized_input, weight):
    return jnp.einsum("td,fd->tf", normalized_input, weight, preferred_element_type=jnp.float32)


def lookup(table, index):
    hits = index[:, None] == jnp.arange(table.shape[0], dtype=jnp.int32)[None, :]
    return jnp.sum(jnp.where(hits, table[None, :], 0), axis=1)


def attend_kernel(group, info, q_ref, k_ref, v_ref, fk_ref, fv_ref, out_ref, peak_ref, sum_ref, acc_ref):
    heads, rows = acc_ref.shape[0], acc_ref.shape[1]
    pairs = k_ref.shape[2]
    columns = q_ref.shape[1]
    dest = pl.program_id(0)
    me = info[0]
    per = FRESH_TOKENS // rows
    length = info[1 + dest // per]
    base = me * (2 * pairs)
    col = lax.broadcasted_iota(jnp.int32, (columns, 128), 0)
    lane = lax.broadcasted_iota(jnp.int32, (columns, 128), 1)
    out_lane = lax.broadcasted_iota(jnp.int32, (rows, 128), 1)
    has_cache = base < length
    has_fresh = (dest // per == me // per) & (dest >= me)
    nt = (((1,), (1,)), ((), ()))

    def pick(g, odd):
        hit = (col == g * HEAD_SIZE + lane - odd * HEAD_SIZE) & (lane // HEAD_SIZE == odd)
        select = jnp.where(hit, HEAD_SIZE ** (-0.5), 0.0).astype(jnp.bfloat16)
        return jnp.dot(q_ref[...], select, preferred_element_type=jnp.float32).astype(jnp.bfloat16)

    @pl.when(jnp.logical_not(has_cache))
    def _():
        peak_ref[...] = jnp.full_like(peak_ref, NEGATIVE)
        sum_ref[...] = jnp.zeros_like(sum_ref)
        acc_ref[...] = jnp.zeros_like(acc_ref)

    @pl.when(has_cache)
    def _():
        even_pos = base + 2 * lax.broadcasted_iota(jnp.int32, (1, pairs), 1)
        even_bias = jnp.where(even_pos < length, 0.0, NEGATIVE)
        odd_bias = jnp.where(even_pos + 1 < length, 0.0, NEGATIVE)
        @pl.loop(0, heads // group)
        def _(j):
            for i in range(group):
                g = j * group + i
                keys = k_ref[0, j]
                values = v_ref[0, j]
                even = lax.dot_general(pick(g, 0), keys, nt, preferred_element_type=jnp.float32) + even_bias
                odd = lax.dot_general(pick(g, 1), keys, nt, preferred_element_type=jnp.float32) + odd_bias
                peak = jnp.max(jnp.maximum(even, odd), axis=1, keepdims=True)
                even = jnp.exp(even - peak)
                odd = jnp.exp(odd - peak)
                total = jnp.sum(even + odd, axis=1, keepdims=True)
                mix_even = jnp.dot(even.astype(jnp.bfloat16), values, preferred_element_type=jnp.float32)
                mix_odd = jnp.dot(odd.astype(jnp.bfloat16), values, preferred_element_type=jnp.float32)
                mixed = jnp.where(out_lane < HEAD_SIZE, mix_even, mix_odd)
                peak_ref[g] = jnp.broadcast_to(peak, (rows, 128))
                sum_ref[g] = jnp.broadcast_to(total, (rows, 128))
                acc_ref[g] = mixed

    @pl.when(has_fresh)
    def _():
        row_q = dest * rows + lax.broadcasted_iota(jnp.int32, (rows, rows), 0)
        row_k = me * rows + lax.broadcasted_iota(jnp.int32, (rows, rows), 1)
        bias = jnp.where(row_k <= row_q, 0.0, NEGATIVE)
        @pl.loop(0, heads // group)
        def _(j):
            for i in range(group):
                g = j * group + i
                score = lax.dot_general(pick(g, 0), fk_ref[j], nt, preferred_element_type=jnp.float32) + bias
                old = peak_ref[g][:, :1]
                peak = jnp.maximum(old, jnp.max(score, axis=1, keepdims=True))
                weight = jnp.exp(score - peak)
                factor = jnp.exp(old - peak)
                total = sum_ref[g][:, :1] * factor + jnp.sum(weight, axis=1, keepdims=True)
                mix = jnp.dot(weight.astype(jnp.bfloat16), fv_ref[j], preferred_element_type=jnp.float32)
                acc_ref[g] = acc_ref[g] * factor + mix
                peak_ref[g] = jnp.broadcast_to(peak, (rows, 128))
                sum_ref[g] = jnp.broadcast_to(total, (rows, 128))

    tail = jnp.zeros((rows, 128), jnp.float32)
    left = None
    for g in range(heads):
        acc = acc_ref[g]
        acc = acc + pltpu.roll(acc, HEAD_SIZE, 1)
        total = sum_ref[g]
        some = total > 0.0
        safe = jnp.where(some, total, 1.0)
        level = jnp.where(some, peak_ref[g] + jnp.log(safe), NEGATIVE)
        high = level.astype(jnp.bfloat16).astype(jnp.float32)
        middle = (level - high).astype(jnp.bfloat16).astype(jnp.float32)
        low = level - high - middle
        tail = jnp.where(out_lane == g, high, tail)
        tail = jnp.where(out_lane == heads + g, middle, tail)
        tail = jnp.where(out_lane == 2 * heads + g, low, tail)
        result = acc / safe
        if g % 2 == 0:
            left = result
        if g % 2 == 1 or g == heads - 1:
            block = jnp.where(out_lane < HEAD_SIZE, left, result)
            out_ref[0, :, g // 2 * 128 : g // 2 * 128 + 128] = block.astype(out_ref.dtype)
    out_ref[0, :, out_ref.shape[2] - 128 :] = tail.astype(out_ref.dtype)


def attend(info, query, keys, values, fresh_key, fresh_value, rows, local_q):
    local_kv, pairs = keys.shape[1], keys.shape[2]
    group = local_q // local_kv
    per = FRESH_TOKENS // rows
    dests = query.shape[0] // rows
    cache_spec = pl.BlockSpec((1, local_kv, pairs, 128), lambda d, info: (d // per, 0, 0, 0))
    fresh_spec = pl.BlockSpec((local_kv, rows, 128), lambda d, info: (0, 0, 0))
    columns = (local_q + 1) // 2 * 128 + 128
    return pl.pallas_call(
        functools.partial(attend_kernel, group),
        grid_spec=pltpu.PrefetchScalarGridSpec(
            num_scalar_prefetch=1,
            grid=(dests,),
            in_specs=[
                pl.BlockSpec((rows, local_q * HEAD_SIZE), lambda d, info: (d, 0)),
                cache_spec,
                cache_spec,
                fresh_spec,
                fresh_spec,
            ],
            out_specs=pl.BlockSpec((1, rows, columns), lambda d, info: (d, 0, 0)),
            scratch_shapes=[pltpu.VMEM((local_q, rows, 128), jnp.float32)] * 3,
        ),
        out_shape=jax.ShapeDtypeStruct((dests, rows, columns), jnp.bfloat16),
        compiler_params=pltpu.CompilerParams(vmem_limit_bytes=40 * 1024 * 1024),
        cost_estimate=pl.CostEstimate(
            flops=8 * query.size * pairs * 2, bytes_accessed=16 << 20, transcendentals=query.size * pairs // 32
        ),
    )(info, query, keys, values, fresh_key, fresh_value)


def pack_kernel(w_ref, out_ref):
    experts = w_ref.shape[0]
    lane = lax.broadcasted_iota(jnp.int32, (w_ref.shape[2], 128), 1)
    low = lane < 64
    for pair in range(experts // 2):
        for part in range(2):
            one = w_ref[2 * pair, part].astype(jnp.float32)
            two = w_ref[2 * pair + 1, part].astype(jnp.float32)
            at = pair * 256 + part * 128
            out_ref[0, :, at : at + 128] = jnp.where(low, one, pltpu.roll(two, 64, 1)).astype(out_ref.dtype)
            out_ref[1, :, at : at + 128] = jnp.where(low, pltpu.roll(one, 64, 1), two).astype(out_ref.dtype)


def pack_gate_up(w_gate_up):
    experts, _, rows, hidden = w_gate_up.shape
    owners = hidden // 64
    return pl.pallas_call(
        pack_kernel,
        grid=(owners // 2,),
        in_specs=[pl.BlockSpec((experts, 2, rows, 128), lambda i: (0, 0, 0, i))],
        out_specs=pl.BlockSpec((2, rows, experts * 128), lambda i: (i, 0, 0)),
        out_shape=jax.ShapeDtypeStruct((owners, rows, experts * 128), w_gate_up.dtype),
        compiler_params=pltpu.CompilerParams(vmem_limit_bytes=24 * 1024 * 1024),
        cost_estimate=pl.CostEstimate(flops=w_gate_up.size, bytes_accessed=4 * w_gate_up.size, transcendentals=0),
    )(w_gate_up)


def nearest(z, j):
    up = jnp.where(z == 1, jnp.where(j == 0, 1, jnp.where(j == 1, 0, j)), j)
    down = jnp.where(z == 2, jnp.where(j == 0, 2, jnp.where(j == 1, 3, 3 - j)), 3 - j)
    return jnp.where(z < 2, up, down)


def expert_kernel(
    own_ref, ids_ref, router_ref, gate_up_ref, down_ref, out_ref,
    blocks, hidden, other_half, own_half, from_core, from_y, kept, passed, from_x, partial, from_z, final,
    sem_away, sem_side, sem_core, got_link, got_core,
    sem_a, got_a, sem_b, got_b, sem_c, got_c, sem_d, got_d, sem_e, got_e,
):
    rows, width = own_ref.shape
    units = down_ref.shape[0]
    half, quarter = width // 2, width // 4
    s, t = lax.axis_index("seq"), lax.axis_index("tp")
    z, x = s // 2, s % 2
    y, c = t // 2, t % 2
    mesh_id = pl.DeviceIdType.MESH
    side = (z * 2 + 1 - x, t)
    across = (s, (1 - y) * 2 + c)
    twin = (s, y * 2 + 1 - c)
    mine = pl.ds(pl.multiple_of(c * half, 128), half)
    others = pl.ds(pl.multiple_of((1 - c) * half, 128), half)
    f32 = jnp.float32

    barrier = pltpu.get_barrier_semaphore()
    for peer in (side, across, twin):
        pl.semaphore_signal(barrier, inc=1, device_id=peer, device_id_type=mesh_id)
    for step in range(1, 4):
        pl.semaphore_signal(barrier, inc=1, device_id=((z + step) % 4 * 2 + x, t), device_id_type=mesh_id)
    blocks[s] = own_ref[...]
    pl.semaphore_wait(barrier, 6)

    def away(b, direction):
        return pltpu.make_async_remote_copy(
            blocks.at[b, :, mine], blocks.at[b, :, mine], sem_away.at[b, (direction + 1) // 2], got_link.at[b],
            device_id=((z + direction) * 2 + x, t), device_id_type=mesh_id)

    def sideways(b):
        return pltpu.make_async_remote_copy(
            blocks.at[b, :, mine], blocks.at[b, :, mine], sem_side.at[b], got_link.at[b],
            device_id=side, device_id_type=mesh_id)

    def to_twin(b):
        return pltpu.make_async_remote_copy(
            blocks.at[b, :, mine], blocks.at[b, :, mine], sem_core.at[b], got_core.at[b],
            device_id=twin, device_id_type=mesh_id)

    def copy_a(i):
        return pltpu.make_async_remote_copy(
            other_half.at[i], from_core.at[i], sem_a.at[i], got_a.at[i], device_id=twin, device_id_type=mesh_id)

    def copy_b(i):
        cut = pl.ds(pl.multiple_of((1 - y) * quarter, 128), quarter)
        return pltpu.make_async_remote_copy(
            own_half.at[i, :, cut], from_y.at[i], sem_b.at[i], got_b.at[i], device_id=across, device_id_type=mesh_id)

    def copy_c(j):
        return pltpu.make_async_remote_copy(
            passed.at[j], from_x.at[j], sem_c.at[j], got_c.at[j], device_id=side, device_id_type=mesh_id)

    def copy_d(j):
        return pltpu.make_async_remote_copy(
            partial.at[j], from_z.at[z], sem_d.at[j], got_d.at[z],
            device_id=(nearest(z, j) * 2 + x, t), device_id_type=mesh_id)

    def arrive_d(z_from):
        return pltpu.make_async_remote_copy(
            partial.at[0], from_z.at[z_from], sem_d.at[0], got_d.at[z_from],
            device_id=side, device_id_type=mesh_id)

    for direction in (-1, 1):
        @pl.when((z + direction >= 0) & (z + direction < 4))
        def _():
            away(s, direction).start()
    sideways(s).start()

    def block_of(i):
        k = i % 2
        return nearest(z, i // 2) * 2 + jnp.where(k == 0, x, 1 - x)

    expert_of = lanes_of(rows).astype(f32)
    as_columns = jnp.where(lax.broadcasted_iota(jnp.int32, (ids_ref.shape[1], 128), 0) == lanes_of(ids_ref.shape[1]), 1.0, 0.0).astype(jnp.bfloat16)
    expert_lane = lax.broadcasted_iota(jnp.int32, (128, units), 0)
    expert_unit = lax.broadcasted_iota(jnp.int32, (128, units), 1)

    def step(i, carry):
        @pl.when(i < 8)
        def _():
            b = block_of(i)
            zj = nearest(z, i // 2)

            @pl.when(i > 0)
            def _():
                sideways(b).wait_recv()
                to_twin(b).start()

            @pl.when((i > 0) & (i % 2 == 0))
            def _():
                for direction in (-1, 1):
                    @pl.when(((z - zj) * direction > 0) & (z + direction >= 0) & (z + direction < 4))
                    def _():
                        away(b, direction).start()
                sideways(b).start()

            @pl.when(i > 0)
            def _():
                to_twin(b).wait_recv()

            tokens = blocks[b]
            logits = jnp.dot(tokens, router_ref[...], preferred_element_type=f32)
            named = lax.dot_general(ids_ref[b], as_columns, (((0,), (0,)), ((), ())), preferred_element_type=f32)
            chosen = named[:, 0:1] == expert_of
            for k in range(1, 8):
                chosen = chosen | (named[:, k : k + 1] == expert_of)
            logits = jnp.where(chosen, logits, NEGATIVE)
            gates = jnp.where(chosen, jnp.exp(logits - jnp.max(logits, axis=1, keepdims=True)), 0.0)
            share = gates / jnp.sum(gates, axis=1, keepdims=True)
            high = share.astype(jnp.bfloat16)
            low = (share - high.astype(f32)).astype(jnp.bfloat16)
            spread = jnp.where(expert_lane == t * (units // 64) + expert_unit // 64, 1.0, 0.0).astype(jnp.bfloat16)
            shares = jnp.dot(high, spread, preferred_element_type=f32) + jnp.dot(low, spread, preferred_element_type=f32)
            for p in range(units // 128):
                both = jnp.dot(tokens, gate_up_ref[:, p * 256 : p * 256 + 256], preferred_element_type=f32)
                gate, up = both[:, :128], both[:, 128:]
                value = gate / (1.0 + jnp.exp(-gate)) * up * shares[:, p * 128 : p * 128 + 128]
                hidden[:, p * 128 : p * 128 + 128] = value.astype(jnp.bfloat16)
            other_half[i] = jnp.dot(hidden[...], down_ref[:, others], preferred_element_type=f32).astype(jnp.bfloat16)
            copy_a(i).start()
            own_half[i] = jnp.dot(hidden[...], down_ref[:, mine], preferred_element_type=f32).astype(jnp.bfloat16)

        @pl.when((i >= 1) & (i < 9))
        def _():
            n = i - 1
            copy_a(n).wait_recv()
            own_half[n] = (own_half[n].astype(f32) + from_core[n].astype(f32)).astype(jnp.bfloat16)
            copy_b(n).start()

        @pl.when((i >= 2) & (i < 10))
        def _():
            n = i - 2
            copy_b(n).wait_recv()
            cut = pl.ds(pl.multiple_of(y * quarter, 128), quarter)
            total = (own_half[n, :, cut].astype(f32) + from_y[n].astype(f32)).astype(jnp.bfloat16)

            @pl.when(n % 2 == 0)
            def _():
                kept[n // 2] = total

            @pl.when(n % 2 == 1)
            def _():
                passed[n // 2] = total
                copy_c(n // 2).start()

        @pl.when((i >= 4) & (i % 2 == 0))
        def _():
            j = (i - 4) // 2
            copy_c(j).wait_recv()
            partial[j] = (kept[j].astype(f32) + from_x[j].astype(f32)).astype(jnp.bfloat16)

            @pl.when(j > 0)
            def _():
                copy_d(j).start()
        return carry

    lax.fori_loop(0, 11, step, 0)

    total = partial[0].astype(f32)
    for step_z in range(1, 4):
        z_from = (z + step_z) % 4
        arrive_d(z_from).wait_recv()
        total = total + from_z[z_from].astype(f32)

    def copy_e(n, to):
        at = c * half + y * quarter if n == 0 else c * half
        size = quarter if n == 0 else half
        cut = pl.ds(pl.multiple_of(at, 128), size)
        return pltpu.make_async_remote_copy(
            final.at[:, cut], final.at[:, cut], sem_e.at[n], got_e.at[n], device_id=to, device_id_type=mesh_id)

    final[:, pl.ds(pl.multiple_of(c * half + y * quarter, 128), quarter)] = total.astype(jnp.bfloat16)
    copy_e(0, across).start()
    copy_e(0, across).wait_recv()
    copy_e(1, twin).start()
    copy_e(1, twin).wait_recv()
    out_ref[...] = final[...]

    def drain(i, carry):
        b = block_of(i)
        zj = nearest(z, i // 2)

        @pl.when(i > 0)
        def _():
            to_twin(b).wait_send()

        @pl.when(i % 2 == 0)
        def _():
            sideways(b).wait_send()
            for direction in (-1, 1):
                @pl.when(((z - zj) * direction >= 0) & (z + direction >= 0) & (z + direction < 4))
                def _():
                    away(b, direction).wait_send()
            copy_c(i // 2).wait_send()

            @pl.when(i > 0)
            def _():
                copy_d(i // 2).wait_send()

        copy_a(i).wait_send()
        copy_b(i).wait_send()
        return carry

    lax.fori_loop(0, 8, drain, 0)
    copy_e(0, across).wait_send()
    copy_e(1, twin).wait_send()


def expert_branch(normed2, ids, router, gate_up, down):
    rows, width = normed2.shape
    units = down.shape[0]
    half, quarter = width // 2, width // 4
    bf16 = jnp.bfloat16
    dma = pltpu.SemaphoreType.DMA
    return pl.pallas_call(
        expert_kernel,
        out_shape=jax.ShapeDtypeStruct((rows, width), bf16),
        in_specs=[pl.BlockSpec(memory_space=pltpu.VMEM)] * 5,
        out_specs=pl.BlockSpec(memory_space=pltpu.VMEM),
        scratch_shapes=[
            pltpu.VMEM((8, rows, width), bf16),
            pltpu.VMEM((rows, units), bf16),
            pltpu.VMEM((8, rows, half), bf16),
            pltpu.VMEM((8, rows, half), bf16),
            pltpu.VMEM((8, rows, half), bf16),
            pltpu.VMEM((8, rows, quarter), bf16),
            pltpu.VMEM((4, rows, quarter), bf16),
            pltpu.VMEM((4, rows, quarter), bf16),
            pltpu.VMEM((4, rows, quarter), bf16),
            pltpu.VMEM((4, rows, quarter), bf16),
            pltpu.VMEM((4, rows, quarter), bf16),
            pltpu.VMEM((rows, width), bf16),
            dma((8, 2)), dma((8,)), dma((8,)), dma((8,)), dma((8,)),
            dma((8,)), dma((8,)), dma((8,)), dma((8,)), dma((4,)), dma((4,)), dma((4,)), dma((4,)), dma((2,)), dma((2,)),
        ],
        compiler_params=pltpu.CompilerParams(
            collective_id=0, has_side_effects=True, vmem_limit_bytes=56 * 1024 * 1024
        ),
        cost_estimate=pl.CostEstimate(
            flops=16 * rows * width * units * 3, bytes_accessed=16 << 20, transcendentals=8 * rows * units
        ),
    )(normed2, ids, router, gate_up, down)


def lanes_of(rows):
    return lax.broadcasted_iota(jnp.int32, (rows, 128), 1)


def read_levels(tail, heads):
    return tail + pltpu.roll(tail, 128 - heads, 1) + pltpu.roll(tail, 128 - 2 * heads, 1)


def write_levels(level, heads):
    lane = lanes_of(level.shape[0])
    high = level.astype(jnp.bfloat16).astype(jnp.float32)
    middle = (level - high).astype(jnp.bfloat16).astype(jnp.float32)
    low = level - high - middle
    tail = jnp.where(lane < 3 * heads, pltpu.roll(low, 2 * heads, 1), 0.0)
    tail = jnp.where(lane < 2 * heads, pltpu.roll(middle, heads, 1), tail)
    return jnp.where(lane < heads, high, tail)


def merge(pieces, heads):
    lane = lanes_of(pieces[0].shape[0])
    levels = [read_levels(piece[:, heads * 64 :].astype(jnp.float32), heads) for piece in pieces]
    peak = functools.reduce(jnp.maximum, levels)
    weights = [jnp.exp(level - peak) for level in levels]
    total = functools.reduce(jnp.add, weights)
    weights = [weight / total for weight in weights]
    tiles = []
    for tile in range(heads // 2):
        mixed = None
        for piece, weight in zip(pieces, weights):
            factor = jnp.where(lane < 64, weight[:, 2 * tile : 2 * tile + 1], weight[:, 2 * tile + 1 : 2 * tile + 2])
            term = piece[:, tile * 128 : tile * 128 + 128].astype(jnp.float32) * factor
            mixed = term if mixed is None else mixed + term
        tiles.append(mixed)
    return tiles, peak + jnp.log(total)


def attention_kernel(
    lens_ref, q_ref, k_ref, v_ref, fk_ref, fv_ref, w_out_ref, tokens_ref, gain_ref, attn_ref, normed_ref, ids_ref,
    queries, keys, values, mixed, level_tail, sent, held, from_x, merged, from_z, parting, half_sum, got_twin, got_across, joined,
    sem_qz, sem_qx, got_q, sem_x, got_x, sem_z, got_z, sem_t, got_t,
):
    rows, features = tokens_ref.shape[0], q_ref.shape[1]
    heads = features // 64
    group = heads // k_ref.shape[1]
    pairs = k_ref.shape[2]
    width = tokens_ref.shape[1]
    half = width // 2
    s, t = lax.axis_index("seq"), lax.axis_index("tp")
    z, x = s // 2, s % 2
    y, c = t // 2, t % 2
    mesh_id = pl.DeviceIdType.MESH
    side = (z * 2 + 1 - x, t)
    across = (s, (1 - y) * 2 + c)
    twin = (s, y * 2 + 1 - c)
    mine = pl.ds(pl.multiple_of(c * half, 128), half)
    others = pl.ds(pl.multiple_of((1 - c) * half, 128), half)
    f32, bf16 = jnp.float32, jnp.bfloat16
    nt = (((1,), (1,)), ((), ()))

    barrier = pltpu.get_barrier_semaphore()
    for peer in (side, across, twin):
        pl.semaphore_signal(barrier, inc=1, device_id=peer, device_id_type=mesh_id)
    for step in range(1, 4):
        pl.semaphore_signal(barrier, inc=1, device_id=((z + step) % 4 * 2 + x, t), device_id_type=mesh_id)
    queries[s] = q_ref[...]
    pl.semaphore_wait(barrier, 6)

    def query_z(j):
        return pltpu.make_async_remote_copy(
            queries.at[s], queries.at[s], sem_qz.at[j], got_q.at[s],
            device_id=(nearest(z, j) * 2 + x, t), device_id_type=mesh_id)

    def query_x(r):
        b = r * 2 + x
        return pltpu.make_async_remote_copy(
            queries.at[b], queries.at[b], sem_qx.at[r], got_q.at[b], device_id=side, device_id_type=mesh_id)

    def arrived_q(b):
        return pltpu.make_async_remote_copy(
            queries.at[b], queries.at[b], sem_qx.at[0], got_q.at[b], device_id=side, device_id_type=mesh_id)

    def part_x(i):
        return pltpu.make_async_remote_copy(
            sent.at[i], from_x.at[i], sem_x.at[i], got_x.at[i], device_id=side, device_id_type=mesh_id)

    def part_z(i):
        return pltpu.make_async_remote_copy(
            merged.at[i], from_z.at[z], sem_z.at[i], got_z.at[z],
            device_id=(nearest(z, i + 1) * 2 + x, t), device_id_type=mesh_id)

    def arrived_z(z_from):
        return pltpu.make_async_remote_copy(
            merged.at[0], from_z.at[z_from], sem_z.at[0], got_z.at[z_from], device_id=side, device_id_type=mesh_id)

    for j in range(1, 4):
        query_z(j).start()
    query_x(z).start()

    base = s * (2 * pairs)
    lane = lanes_of(pairs)
    row_lane = lanes_of(rows)
    below = lane < 64

    def spread(block, fill, scale):
        plain = block.astype(f32)
        if scale != 1.0:
            plain = plain * scale
        turned = pltpu.roll(plain, 64, 1)
        keep = lanes_of(block.shape[0]) < 64
        return (
            (jnp.where(keep, plain, fill).astype(bf16), jnp.where(keep, turned, fill).astype(bf16)),
            (jnp.where(keep, fill, turned).astype(bf16), jnp.where(keep, fill, plain).astype(bf16)),
        )

    def attend(r, fresh, between):
        length = lens_ref[r]
        slot = lax.broadcasted_iota(jnp.int32, (1, 2 * pairs), 1)
        position = base + 2 * (slot % pairs) + slot // pairs
        bias = jnp.where(position < length, 0.0, NEGATIVE)
        for j in range(heads // group):
            if j == 1:
                between()
            key_two = spread(k_ref[r, j], 0.0, 0.125)
            value_two = spread(v_ref[r, j], 1.0, 1.0)
            for parity in range(2):
                keys[parity, :pairs] = key_two[parity][0]
                keys[parity, pairs : 2 * pairs] = key_two[parity][1]
                values[parity, :pairs] = value_two[parity][0]
                values[parity, pairs : 2 * pairs] = value_two[parity][1]
            if fresh:
                new_keys = spread(fk_ref[j], 0.0, 0.125)
                new_values = spread(fv_ref[j], 1.0, 1.0)
            for g in range(j * group, (j + 1) * group):
                parity = g % 2
                for part in range(2):
                    query = queries[r * 2 + part, :rows, g // 2 * 128 : g // 2 * 128 + 128]
                    score = lax.dot_general(query, keys[parity], nt, preferred_element_type=f32) + bias
                    peak = jnp.max(score, axis=1, keepdims=True)
                    if fresh:
                        new_key = new_keys[0][0] if parity == 0 else new_keys[1][0]
                        new_value = new_values[0][0] if parity == 0 else new_values[1][0]
                        row_q = part * rows + lax.broadcasted_iota(jnp.int32, (rows, rows), 0)
                        row_k = x * rows + lax.broadcasted_iota(jnp.int32, (rows, rows), 1)
                        new_score = lax.dot_general(query, new_key, nt, preferred_element_type=f32)
                        new_score = new_score + jnp.where(row_k <= row_q, 0.0, NEGATIVE)
                        peak = jnp.maximum(peak, jnp.max(new_score, axis=1, keepdims=True))
                    weight = jnp.exp(score - peak).astype(bf16)
                    total = jnp.dot(weight, values[parity], preferred_element_type=f32)
                    if fresh:
                        weight = jnp.exp(new_score - peak).astype(bf16)
                        total = total + jnp.dot(weight, new_value, preferred_element_type=f32)
                    turned = pltpu.roll(total, 64, 1)
                    if parity == 0:
                        sums = jnp.where(row_lane < 64, turned, total)
                    else:
                        sums = jnp.where(row_lane < 64, total, turned)
                    level = peak + jnp.log(sums)
                    result = total / sums
                    at = pl.ds(part * rows, rows)
                    if g == 0:
                        level_tail[at, :] = level
                    else:
                        level_tail[at, :] = jnp.where(row_lane == g, level, level_tail[at, :])
                    tile = pl.ds(g // 2 * 128, 128)
                    if parity == 0:
                        mixed[at, tile] = result
                    else:
                        mixed[at, tile] = jnp.where(row_lane < 64, mixed[at, tile], result)

    def hand_over(i):
        own = pl.ds(pl.multiple_of(x * rows, rows), rows)
        away = pl.ds(pl.multiple_of((1 - x) * rows, rows), rows)
        sent[i, :, :features] = mixed[away, :].astype(bf16)
        sent[i, :, features:] = write_levels(level_tail[away, :], heads).astype(bf16)
        part_x(i).start()
        held[i, :, :features] = mixed[own, :].astype(bf16)
        held[i, :, features:] = write_levels(level_tail[own, :], heads).astype(bf16)

    def merge_x(i):
        part_x(i).wait_recv()
        tiles, level = merge([held[i], from_x[i]], heads)
        for n, tile in enumerate(tiles):
            merged[i, :, n * 128 : n * 128 + 128] = tile.astype(bf16)
        merged[i, :, features:] = write_levels(level, heads).astype(bf16)

    def forward(i):
        r = nearest(z, i + 1)
        arrived_q(r * 2 + x).wait_recv()
        query_x(r).start()

    forward(0)

    def step(i, carry):
        r = nearest(z, i + 1)
        arrived_q(r * 2 + 1 - x).wait_recv()

        def between():
            @pl.when(i < 2)
            def _():
                forward(i + 1)

        attend(r, False, between)
        hand_over(i)

        @pl.when(i > 0)
        def _():
            merge_x(i - 1)
            part_z(i - 1).start()
        return carry

    lax.fori_loop(0, 3, step, 0)
    arrived_q(z * 2 + 1 - x).wait_recv()

    def between():
        merge_x(2)
        part_z(2).start()

    attend(z, True, between)
    hand_over(3)
    merge_x(3)
    pieces = [merged[3]]
    for step_z in range(1, 4):
        z_from = (z + step_z) % 4
        arrived_z(z_from).wait_recv()
        pieces.append(from_z[z_from])
    tiles, _ = merge(pieces, heads)
    heads_out = jnp.concatenate([tile.astype(bf16) for tile in tiles], axis=1)

    def exchange(n, source, target, to):
        return pltpu.make_async_remote_copy(
            source, target, sem_t.at[n], got_t.at[n], device_id=to, device_id_type=mesh_id)

    parting[...] = jnp.dot(heads_out, w_out_ref[:, others], preferred_element_type=f32).astype(bf16)
    first = exchange(0, parting, got_twin, twin)
    first.start()
    own = jnp.dot(heads_out, w_out_ref[:, mine], preferred_element_type=f32)
    first.wait_recv()
    half_sum[...] = (own + got_twin[...].astype(f32)).astype(bf16)
    second = exchange(1, half_sum, got_across, across)
    second.start()
    second.wait_recv()
    joined[:, mine] = (half_sum[...].astype(f32) + got_across[...].astype(f32)).astype(bf16)
    third = exchange(2, joined.at[:, mine], joined.at[:, mine], twin)
    third.start()
    third.wait_recv()
    attn_ref[...] = joined[...]
    stream = tokens_ref[...].astype(f32) + joined[...].astype(f32)
    normed = rms_norm(stream, gain_ref[...])
    normed_ref[...] = normed.astype(bf16)
    for b in range(8):
        ids_ref[b] = queries[b, rows:, :rows]

    for j in range(1, 4):
        query_z(j).wait_send()
    for j in range(4):
        query_x(nearest(z, j)).wait_send()
        part_x(j).wait_send()
    for j in range(3):
        part_z(j).wait_send()
    first.wait_send()
    second.wait_send()
    third.wait_send()


def attention_branch(lens, query, keys, values, fresh_key, fresh_value, w_out, tokens, gain):
    features = query.shape[1]
    rows, width = tokens.shape
    extra = query.shape[0] - rows
    requests, local_kv, pairs, _ = keys.shape
    bf16, f32 = jnp.bfloat16, jnp.float32
    dma = pltpu.SemaphoreType.DMA
    vmem = pl.BlockSpec(memory_space=pltpu.VMEM)
    scores = requests * FRESH_TOKENS * (features // 64) * 2 * pairs
    return pl.pallas_call(
        attention_kernel,
        out_shape=[jax.ShapeDtypeStruct((rows, width), bf16)] * 2 + [jax.ShapeDtypeStruct((8, extra, rows), bf16)],
        in_specs=[pl.BlockSpec(memory_space=pltpu.SMEM)] + [vmem] * 8,
        out_specs=[vmem] * 3,
        scratch_shapes=[
            pltpu.VMEM((8, rows + extra, features), bf16),
            pltpu.VMEM((2, 2 * pairs, 128), bf16),
            pltpu.VMEM((2, 2 * pairs, 128), bf16),
            pltpu.VMEM((2 * rows, features), f32),
            pltpu.VMEM((2 * rows, 128), f32),
            pltpu.VMEM((4, rows, features + 128), bf16),
            pltpu.VMEM((4, rows, features + 128), bf16),
            pltpu.VMEM((4, rows, features + 128), bf16),
            pltpu.VMEM((4, rows, features + 128), bf16),
            pltpu.VMEM((4, rows, features + 128), bf16),
            pltpu.VMEM((rows, width // 2), bf16),
            pltpu.VMEM((rows, width // 2), bf16),
            pltpu.VMEM((rows, width // 2), bf16),
            pltpu.VMEM((rows, width // 2), bf16),
            pltpu.VMEM((rows, width), bf16),
            dma((4,)), dma((4,)), dma((8,)), dma((4,)), dma((4,)), dma((4,)), dma((4,)), dma((3,)), dma((3,)),
        ],
        compiler_params=pltpu.CompilerParams(
            collective_id=1, has_side_effects=True, vmem_limit_bytes=56 * 1024 * 1024
        ),
        cost_estimate=pl.CostEstimate(flops=64 * 4 * scores, bytes_accessed=16 << 20, transcendentals=scores),
    )(lens, query, keys, values, fresh_key, fresh_value, w_out, tokens, gain)


def swap_cores(values):
    count = lax.axis_size("tp")
    return lax.ppermute(values, "tp", [(i, i ^ 1) for i in range(count)])


def sum_halves(mine, others):
    received = swap_cores(others.astype(jnp.bfloat16)).astype(jnp.float32)
    return (mine + received).astype(jnp.bfloat16)


def sum_chips(values):
    count = lax.axis_size("tp")
    step = 2
    total = values.astype(jnp.float32)
    while step < count:
        sent = total.astype(jnp.bfloat16)
        received = lax.ppermute(sent, "tp", [(i, i ^ step) for i in range(count)])
        total = sent.astype(jnp.float32) + received.astype(jnp.float32)
        step = step * 2
    return total.astype(jnp.bfloat16)


def join_halves(values, core):
    other = swap_cores(values)
    first = jnp.where(core == 0, values, other)
    second = jnp.where(core == 0, other, values)
    return jnp.concatenate([first, second], axis=1)


def per_device(
    tokens,
    norm1_gain,
    w_query,
    key_weight,
    value_weight,
    rotated_key_cache,
    stored_value_cache,
    cache_len,
    w_out,
    norm2_gain,
    w_router,
    expert_ids,
    w_gate_up,
    w_down,
):
    tok_rows, width = tokens.shape
    seq_pos = lax.axis_index("seq")
    tp_pos = lax.axis_index("tp")
    local_q = w_query.shape[0] // HEAD_SIZE
    local_kv = key_weight.shape[0] // HEAD_SIZE
    requests = rotated_key_cache.shape[0]
    span = rotated_key_cache.shape[2] // HEAD_SIZE
    inputs = tokens.astype(jnp.float32)
    devices = lax.axis_size("seq")
    local_experts, _, own_width, hidden_size = w_gate_up.shape
    own_hidden = hidden_size // devices
    normalized_input = rms_norm(inputs, norm1_gain).astype(jnp.bfloat16)
    row_ids = seq_pos * tok_rows + jnp.arange(tok_rows, dtype=jnp.int32)
    owners = row_ids // FRESH_TOKENS
    positions = lookup(cache_len, owners) + row_ids % FRESH_TOKENS
    angle_position = positions.astype(jnp.float32)
    query_vector = apply_rotary(
        apply_projection(normalized_input, w_query).reshape(tok_rows, local_q, HEAD_SIZE),
        angle_position,
    ).astype(jnp.bfloat16)
    units = local_experts * own_hidden
    by_owner = jnp.transpose(
        w_gate_up.reshape(local_experts, 2, own_width, devices, own_hidden), (3, 2, 1, 0, 4)
    ).reshape(width, 2 * units)
    fresh_key = apply_rotary(
        apply_projection(normalized_input, key_weight).reshape(tok_rows, local_kv, HEAD_SIZE),
        angle_position,
    ).astype(jnp.bfloat16)
    fresh_value = (
        apply_projection(normalized_input, value_weight)
        .astype(jnp.bfloat16)
        .reshape(tok_rows, local_kv, HEAD_SIZE)
    )
    all_query = lax.all_gather(
        query_vector.reshape(tok_rows, local_q * HEAD_SIZE), "seq", axis=0, tiled=True
    )
    all_query, by_owner = lax.optimization_barrier((all_query, by_owner))
    own_gate_up = lax.all_to_all(by_owner, "seq", 0, 0, tiled=True)
    paired = (requests, local_kv, span // 2, 2 * HEAD_SIZE)
    pad = ((0, 0), (0, 0), (0, HEAD_SIZE))
    parts = attend(
        jnp.concatenate([seq_pos[None].astype(jnp.int32), cache_len]),
        all_query,
        rotated_key_cache.reshape(paired),
        stored_value_cache.reshape(paired),
        jnp.pad(jnp.transpose(fresh_key, (1, 0, 2)), pad),
        jnp.pad(jnp.transpose(fresh_value, (1, 0, 2)), pad),
        tok_rows,
        local_q,
    )
    parts, own_gate_up = lax.optimization_barrier((parts, own_gate_up))
    parts = lax.all_to_all(parts, "seq", 0, 0, tiled=True)
    parts = parts.astype(jnp.float32)
    features = local_q * HEAD_SIZE
    tails = parts.shape[2] - 128
    pieces = parts[:, :, tails : tails + 3 * local_q]
    level = pieces[..., :local_q] + pieces[..., local_q : 2 * local_q] + pieces[..., 2 * local_q :]
    factor = jnp.exp(level - jnp.max(level, axis=0, keepdims=True))
    factor = factor / jnp.sum(factor, axis=0, keepdims=True)
    feature_head = jnp.arange(features, dtype=jnp.int32) // HEAD_SIZE
    widen = (jnp.arange(local_q, dtype=jnp.int32)[:, None] == feature_head[None, :]).astype(jnp.float32)
    factor = jnp.einsum("sth,hf->stf", factor, widen, precision=lax.Precision.HIGHEST)
    heads_out = jnp.sum(parts[:, :, :features] * factor, axis=0).astype(jnp.bfloat16)
    attn_part = jnp.dot(heads_out, w_out, preferred_element_type=jnp.float32)
    core = tp_pos % 2
    half = width // 2
    attn = sum_halves(
        lax.dynamic_slice_in_dim(attn_part, core * half, half, 1),
        lax.dynamic_slice_in_dim(attn_part, (1 - core) * half, half, 1),
    )
    attn = join_halves(sum_chips(attn), core).astype(jnp.float32)
    attn_out = attn.astype(jnp.bfloat16)
    normed2 = rms_norm(inputs + attn, norm2_gain).astype(jnp.bfloat16)
    logits = jnp.dot(normed2, w_router, preferred_element_type=jnp.float32)
    experts_all = w_router.shape[1]
    picked_all = expert_ids[:, :, None] == jnp.arange(experts_all, dtype=jnp.int32)[None, None, :]
    chosen = jnp.sum(jnp.where(picked_all, logits[:, None, :], 0.0), axis=-1)
    gates = jax.nn.softmax(chosen, axis=-1)
    local_ids = tp_pos * local_experts + jnp.arange(local_experts, dtype=jnp.int32)
    picked = expert_ids[:, :, None] == local_ids[None, None, :]
    share = jnp.sum(jnp.where(picked, gates[:, :, None], 0.0), axis=1)
    share_high = lax.reduce_precision(share, 8, 7)
    packed = jnp.concatenate(
        [
            lax.dynamic_slice_in_dim(normed2, core * half, half, 1),
            share_high.astype(jnp.bfloat16),
            (share - share_high).astype(jnp.bfloat16),
            jnp.zeros((tok_rows, 128 - 2 * local_experts), jnp.bfloat16),
        ],
        axis=1,
    )
    packed = lax.all_gather(packed, "seq", axis=0, tiled=True)
    others = swap_cores(packed[:, :half])
    unit_expert = jnp.arange(units, dtype=jnp.int32) // own_hidden
    lanes = jnp.arange(128, dtype=jnp.int32)
    spread = (lanes[:, None] % local_experts == unit_expert[None, :]) & (lanes[:, None] < 2 * local_experts)
    share_all = jnp.dot(packed[:, half:], spread.astype(jnp.bfloat16), preferred_element_type=jnp.float32)
    gate_up_mine = lax.dynamic_slice_in_dim(own_gate_up, core * half, half, 0)
    gate_up_others = lax.dynamic_slice_in_dim(own_gate_up, (1 - core) * half, half, 0)
    both = jnp.dot(packed[:, :half], gate_up_mine, preferred_element_type=jnp.float32)
    both = both + jnp.dot(others, gate_up_others, preferred_element_type=jnp.float32)
    hidden = (jax.nn.silu(both[:, :units]) * both[:, units:] * share_all).astype(jnp.bfloat16)
    down = w_down.reshape(units, width)
    down_mine = lax.dynamic_slice_in_dim(down, core * half, half, 1)
    down_others = lax.dynamic_slice_in_dim(down, (1 - core) * half, half, 1)
    moe_half = sum_halves(
        jnp.dot(hidden, down_mine, preferred_element_type=jnp.float32),
        jnp.dot(hidden, down_others, preferred_element_type=jnp.float32),
    )
    moe_half = lax.psum_scatter(moe_half, "seq", scatter_dimension=0, tiled=True)
    expert_out = join_halves(sum_chips(moe_half.astype(jnp.float32)), core)
    return (attn_out, expert_out)


def per_device_block(
    tokens,
    norm1_gain,
    w_query,
    key_weight,
    value_weight,
    rotated_key_cache,
    stored_value_cache,
    cache_len,
    w_out,
    norm2_gain,
    w_router,
    expert_ids,
    w_gate_up,
    w_down,
):
    tok_rows, width = tokens.shape
    seq_pos = lax.axis_index("seq")
    tp_pos = lax.axis_index("tp")
    local_q = w_query.shape[0] // HEAD_SIZE
    local_kv = key_weight.shape[0] // HEAD_SIZE
    requests = rotated_key_cache.shape[0]
    span = rotated_key_cache.shape[2] // HEAD_SIZE
    inputs = tokens.astype(jnp.float32)
    devices = lax.axis_size("seq")
    local_experts, _, own_width, hidden_size = w_gate_up.shape
    own_hidden = hidden_size // devices
    normalized_input = rms_norm(inputs, norm1_gain).astype(jnp.bfloat16)
    row_ids = seq_pos * tok_rows + jnp.arange(tok_rows, dtype=jnp.int32)
    owners = row_ids // FRESH_TOKENS
    positions = lookup(cache_len, owners) + row_ids % FRESH_TOKENS
    angle_position = positions.astype(jnp.float32)
    query_vector = apply_rotary(
        apply_projection(normalized_input, w_query).reshape(tok_rows, local_q, HEAD_SIZE),
        angle_position,
    ).astype(jnp.bfloat16)
    units = local_experts * own_hidden
    by_owner = pack_gate_up(w_gate_up)
    fresh_key = apply_rotary(
        apply_projection(normalized_input, key_weight).reshape(tok_rows, local_kv, HEAD_SIZE),
        angle_position,
    ).astype(jnp.bfloat16)
    fresh_value = (
        apply_projection(normalized_input, value_weight)
        .astype(jnp.bfloat16)
        .reshape(tok_rows, local_kv, HEAD_SIZE)
    )
    own_gate_up = lax.all_to_all(by_owner, "seq", 0, 0, tiled=True).reshape(width, 2 * units)
    ids = jnp.pad(expert_ids.T.astype(jnp.bfloat16), ((0, 8), (0, local_q * HEAD_SIZE - tok_rows)))
    paired = (requests, local_kv, span // 2, 2 * HEAD_SIZE)
    pad = ((0, 0), (0, 0), (0, HEAD_SIZE))
    attn_out, normed2, all_ids = attention_branch(
        cache_len,
        jnp.concatenate([query_vector.reshape(tok_rows, local_q * HEAD_SIZE), ids]),
        rotated_key_cache.reshape(paired),
        stored_value_cache.reshape(paired),
        jnp.pad(jnp.transpose(fresh_key, (1, 0, 2)), pad),
        jnp.pad(jnp.transpose(fresh_value, (1, 0, 2)), pad),
        w_out,
        tokens,
        norm2_gain[None, :],
    )
    router = jnp.pad(w_router, ((0, 0), (0, 128 - w_router.shape[1])))
    expert_out = expert_branch(normed2, all_ids, router, own_gate_up, w_down.reshape(units, width))
    return (attn_out, expert_out)


def solution(mesh):
    block = mesh.shape["seq"] == 8 and mesh.shape["tp"] == 4
    return jax.shard_map(
        per_device_block if block else per_device,
        mesh=mesh,
        in_specs=(
            P("seq", None),
            P(),
            P("tp", None),
            P("tp", None),
            P("tp", None),
            P(None, "tp", "seq"),
            P(None, "tp", "seq"),
            P(),
            P("tp", None),
            P(),
            P(),
            P("seq", None),
            P("tp", None, "seq", None),
            P("tp", "seq", None),
        ),
        out_specs=(P("seq", None), P("seq", None)),
        check_vma=False,
    )
```

```python
import functools

import jax
import jax.numpy as jnp
from jax import lax
from jax.experimental import pallas as pl
from jax.experimental.pallas import tpu as pltpu
from jax.sharding import PartitionSpec as P

HEAD_SIZE = 64
FRESH_TOKENS = 512


EPS = 1e-05
THETA = 10000.0
NEGATIVE = -1e30


def rms_norm(values, gain):
    mean_square = jnp.mean(values * values, axis=-1, keepdims=True)
    return values * lax.rsqrt(mean_square + EPS) * gain.astype(values.dtype)


def apply_rotary(values, positions):
    half_dim = values.shape[-1] // 2
    exponent = jnp.arange(half_dim, dtype=jnp.float32) * (2.0 / values.shape[-1])
    freqs = THETA ** (-exponent)
    angles = positions[:, None] * freqs[None, :]
    cosine = jnp.cos(angles)[:, None, :]
    sine = jnp.sin(angles)[:, None, :]
    first = values[..., :half_dim]
    second = values[..., half_dim:]
    return jnp.concatenate(
        [first * cosine - second * sine, second * cosine + first * sine], axis=-1
    )


def apply_projection(normalized_input, weight):
    return jnp.einsum("td,fd->tf", normalized_input, weight, preferred_element_type=jnp.float32)


def lookup(table, index):
    hits = index[:, None] == jnp.arange(table.shape[0], dtype=jnp.int32)[None, :]
    return jnp.sum(jnp.where(hits, table[None, :], 0), axis=1)


def attend_kernel(group, info, q_ref, k_ref, v_ref, fk_ref, fv_ref, out_ref, peak_ref, sum_ref, acc_ref):
    heads, rows = acc_ref.shape[0], acc_ref.shape[1]
    pairs = k_ref.shape[2]
    columns = q_ref.shape[1]
    dest = pl.program_id(0)
    me = info[0]
    per = FRESH_TOKENS // rows
    length = info[1 + dest // per]
    base = me * (2 * pairs)
    col = lax.broadcasted_iota(jnp.int32, (columns, 128), 0)
    lane = lax.broadcasted_iota(jnp.int32, (columns, 128), 1)
    out_lane = lax.broadcasted_iota(jnp.int32, (rows, 128), 1)
    has_cache = base < length
    has_fresh = (dest // per == me // per) & (dest >= me)
    nt = (((1,), (1,)), ((), ()))

    def pick(g, odd):
        hit = (col == g * HEAD_SIZE + lane - odd * HEAD_SIZE) & (lane // HEAD_SIZE == odd)
        select = jnp.where(hit, HEAD_SIZE ** (-0.5), 0.0).astype(jnp.bfloat16)
        return jnp.dot(q_ref[...], select, preferred_element_type=jnp.float32).astype(jnp.bfloat16)

    @pl.when(jnp.logical_not(has_cache))
    def _():
        peak_ref[...] = jnp.full_like(peak_ref, NEGATIVE)
        sum_ref[...] = jnp.zeros_like(sum_ref)
        acc_ref[...] = jnp.zeros_like(acc_ref)

    @pl.when(has_cache)
    def _():
        even_pos = base + 2 * lax.broadcasted_iota(jnp.int32, (1, pairs), 1)
        even_bias = jnp.where(even_pos < length, 0.0, NEGATIVE)
        odd_bias = jnp.where(even_pos + 1 < length, 0.0, NEGATIVE)
        @pl.loop(0, heads // group)
        def _(j):
            for i in range(group):
                g = j * group + i
                keys = k_ref[0, j]
                values = v_ref[0, j]
                even = lax.dot_general(pick(g, 0), keys, nt, preferred_element_type=jnp.float32) + even_bias
                odd = lax.dot_general(pick(g, 1), keys, nt, preferred_element_type=jnp.float32) + odd_bias
                peak = jnp.max(jnp.maximum(even, odd), axis=1, keepdims=True)
                even = jnp.exp(even - peak)
                odd = jnp.exp(odd - peak)
                total = jnp.sum(even + odd, axis=1, keepdims=True)
                mix_even = jnp.dot(even.astype(jnp.bfloat16), values, preferred_element_type=jnp.float32)
                mix_odd = jnp.dot(odd.astype(jnp.bfloat16), values, preferred_element_type=jnp.float32)
                mixed = jnp.where(out_lane < HEAD_SIZE, mix_even, mix_odd)
                peak_ref[g] = jnp.broadcast_to(peak, (rows, 128))
                sum_ref[g] = jnp.broadcast_to(total, (rows, 128))
                acc_ref[g] = mixed

    @pl.when(has_fresh)
    def _():
        row_q = dest * rows + lax.broadcasted_iota(jnp.int32, (rows, rows), 0)
        row_k = me * rows + lax.broadcasted_iota(jnp.int32, (rows, rows), 1)
        bias = jnp.where(row_k <= row_q, 0.0, NEGATIVE)
        @pl.loop(0, heads // group)
        def _(j):
            for i in range(group):
                g = j * group + i
                score = lax.dot_general(pick(g, 0), fk_ref[j], nt, preferred_element_type=jnp.float32) + bias
                old = peak_ref[g][:, :1]
                peak = jnp.maximum(old, jnp.max(score, axis=1, keepdims=True))
                weight = jnp.exp(score - peak)
                factor = jnp.exp(old - peak)
                total = sum_ref[g][:, :1] * factor + jnp.sum(weight, axis=1, keepdims=True)
                mix = jnp.dot(weight.astype(jnp.bfloat16), fv_ref[j], preferred_element_type=jnp.float32)
                acc_ref[g] = acc_ref[g] * factor + mix
                peak_ref[g] = jnp.broadcast_to(peak, (rows, 128))
                sum_ref[g] = jnp.broadcast_to(total, (rows, 128))

    tail = jnp.zeros((rows, 128), jnp.float32)
    left = None
    for g in range(heads):
        acc = acc_ref[g]
        acc = acc + pltpu.roll(acc, HEAD_SIZE, 1)
        total = sum_ref[g]
        some = total > 0.0
        safe = jnp.where(some, total, 1.0)
        level = jnp.where(some, peak_ref[g] + jnp.log(safe), NEGATIVE)
        high = level.astype(jnp.bfloat16).astype(jnp.float32)
        middle = (level - high).astype(jnp.bfloat16).astype(jnp.float32)
        low = level - high - middle
        tail = jnp.where(out_lane == g, high, tail)
        tail = jnp.where(out_lane == heads + g, middle, tail)
        tail = jnp.where(out_lane == 2 * heads + g, low, tail)
        result = acc / safe
        if g % 2 == 0:
            left = result
        if g % 2 == 1 or g == heads - 1:
            block = jnp.where(out_lane < HEAD_SIZE, left, result)
            out_ref[0, :, g // 2 * 128 : g // 2 * 128 + 128] = block.astype(out_ref.dtype)
    out_ref[0, :, out_ref.shape[2] - 128 :] = tail.astype(out_ref.dtype)


def attend(info, query, keys, values, fresh_key, fresh_value, rows, local_q):
    local_kv, pairs = keys.shape[1], keys.shape[2]
    group = local_q // local_kv
    per = FRESH_TOKENS // rows
    dests = query.shape[0] // rows
    cache_spec = pl.BlockSpec((1, local_kv, pairs, 128), lambda d, info: (d // per, 0, 0, 0))
    fresh_spec = pl.BlockSpec((local_kv, rows, 128), lambda d, info: (0, 0, 0))
    columns = (local_q + 1) // 2 * 128 + 128
    return pl.pallas_call(
        functools.partial(attend_kernel, group),
        grid_spec=pltpu.PrefetchScalarGridSpec(
            num_scalar_prefetch=1,
            grid=(dests,),
            in_specs=[
                pl.BlockSpec((rows, local_q * HEAD_SIZE), lambda d, info: (d, 0)),
                cache_spec,
                cache_spec,
                fresh_spec,
                fresh_spec,
            ],
            out_specs=pl.BlockSpec((1, rows, columns), lambda d, info: (d, 0, 0)),
            scratch_shapes=[pltpu.VMEM((local_q, rows, 128), jnp.float32)] * 3,
        ),
        out_shape=jax.ShapeDtypeStruct((dests, rows, columns), jnp.bfloat16),
        compiler_params=pltpu.CompilerParams(vmem_limit_bytes=40 * 1024 * 1024),
        cost_estimate=pl.CostEstimate(
            flops=8 * query.size * pairs * 2, bytes_accessed=16 << 20, transcendentals=query.size * pairs // 32
        ),
    )(info, query, keys, values, fresh_key, fresh_value)


def pack_kernel(w_ref, out_ref):
    experts = w_ref.shape[0]
    lane = lax.broadcasted_iota(jnp.int32, (w_ref.shape[2], 128), 1)
    low = lane < 64
    for pair in range(experts // 2):
        for part in range(2):
            one = w_ref[2 * pair, part].astype(jnp.float32)
            two = w_ref[2 * pair + 1, part].astype(jnp.float32)
            at = pair * 256 + part * 128
            out_ref[0, :, at : at + 128] = jnp.where(low, one, pltpu.roll(two, 64, 1)).astype(out_ref.dtype)
            out_ref[1, :, at : at + 128] = jnp.where(low, pltpu.roll(one, 64, 1), two).astype(out_ref.dtype)


def pack_gate_up(w_gate_up):
    experts, _, rows, hidden = w_gate_up.shape
    owners = hidden // 64
    return pl.pallas_call(
        pack_kernel,
        grid=(owners // 2,),
        in_specs=[pl.BlockSpec((experts, 2, rows, 128), lambda i: (0, 0, 0, i))],
        out_specs=pl.BlockSpec((2, rows, experts * 128), lambda i: (i, 0, 0)),
        out_shape=jax.ShapeDtypeStruct((owners, rows, experts * 128), w_gate_up.dtype),
        compiler_params=pltpu.CompilerParams(vmem_limit_bytes=24 * 1024 * 1024),
        cost_estimate=pl.CostEstimate(flops=w_gate_up.size, bytes_accessed=4 * w_gate_up.size, transcendentals=0),
    )(w_gate_up)


def nearest(z, j):
    up = jnp.where(z == 1, jnp.where(j == 0, 1, jnp.where(j == 1, 0, j)), j)
    down = jnp.where(z == 2, jnp.where(j == 0, 2, jnp.where(j == 1, 3, 3 - j)), 3 - j)
    return jnp.where(z < 2, up, down)


def lanes_of(rows):
    return lax.broadcasted_iota(jnp.int32, (rows, 128), 1)


def read_levels(tail, heads):
    return tail + pltpu.roll(tail, 128 - heads, 1) + pltpu.roll(tail, 128 - 2 * heads, 1)


def write_levels(level, heads):
    lane = lanes_of(level.shape[0])
    high = level.astype(jnp.bfloat16).astype(jnp.float32)
    middle = (level - high).astype(jnp.bfloat16).astype(jnp.float32)
    low = level - high - middle
    tail = jnp.where(lane < 3 * heads, pltpu.roll(low, 2 * heads, 1), 0.0)
    tail = jnp.where(lane < 2 * heads, pltpu.roll(middle, heads, 1), tail)
    return jnp.where(lane < heads, high, tail)


def merge(pieces, heads):
    lane = lanes_of(pieces[0].shape[0])
    levels = [read_levels(piece[:, heads * 64 :].astype(jnp.float32), heads) for piece in pieces]
    peak = functools.reduce(jnp.maximum, levels)
    weights = [jnp.exp(level - peak) for level in levels]
    total = functools.reduce(jnp.add, weights)
    weights = [weight / total for weight in weights]
    tiles = []
    for tile in range(heads // 2):
        mixed = None
        for piece, weight in zip(pieces, weights):
            factor = jnp.where(lane < 64, weight[:, 2 * tile : 2 * tile + 1], weight[:, 2 * tile + 1 : 2 * tile + 2])
            term = piece[:, tile * 128 : tile * 128 + 128].astype(jnp.float32) * factor
            mixed = term if mixed is None else mixed + term
        tiles.append(mixed)
    return tiles, peak + jnp.log(total)


def layer_kernel(
    lens_ref, q_ref, k_ref, v_ref, fk_ref, fv_ref, w_out_ref, tokens_ref, gain_ref, packed_ref, router_ref, down_ref,
    attn_ref, out_ref,
    queries, keys, values, mixed, level_tail, sent, held, peer_x, merged, peer_z, parting, half_sum, got_twin, got_across, joined,
    gate_up_ref, blocks, hidden, other_half, own_half, from_core, from_y, kept, passed, from_x, partial, from_z, final,
    sem_qz, sem_qx, got_q, sem_x, got_x, sem_z, got_z, sem_t, got_t, sem_w, got_w, sem_own,
    sem_away, sem_side, sem_core, got_link, got_core,
    sem_a, got_a, sem_b, got_b, sem_c, got_c, sem_d, got_d, sem_e, got_e,
):
    units = down_ref.shape[0]
    quarter = tokens_ref.shape[1] // 4
    rows, features = tokens_ref.shape[0], q_ref.shape[1]
    heads = features // 64
    group = heads // k_ref.shape[1]
    pairs = k_ref.shape[2]
    width = tokens_ref.shape[1]
    half = width // 2
    s, t = lax.axis_index("seq"), lax.axis_index("tp")
    z, x = s // 2, s % 2
    y, c = t // 2, t % 2
    mesh_id = pl.DeviceIdType.MESH
    side = (z * 2 + 1 - x, t)
    across = (s, (1 - y) * 2 + c)
    twin = (s, y * 2 + 1 - c)
    mine = pl.ds(pl.multiple_of(c * half, 128), half)
    others = pl.ds(pl.multiple_of((1 - c) * half, 128), half)
    f32, bf16 = jnp.float32, jnp.bfloat16
    nt = (((1,), (1,)), ((), ()))

    barrier = pltpu.get_barrier_semaphore()
    for peer in (side, across, twin):
        pl.semaphore_signal(barrier, inc=1, device_id=peer, device_id_type=mesh_id)
    for step in range(1, 8):
        @pl.when((s + step) % 8 != s // 2 * 2 + 1 - x)
        def _():
            pl.semaphore_signal(barrier, inc=1, device_id=((s + step) % 8, t), device_id_type=mesh_id)
    queries[s] = q_ref[...]
    pl.semaphore_wait(barrier, 9)

    def weight_copy(n):
        to = (s + 1 + n % 7) % 8
        cut = n // 7
        depth = packed_ref.shape[1]
        part = depth // 4
        source = pl.ds(pl.multiple_of(cut * part, 16), part)
        target = pl.ds(pl.multiple_of(s * depth + cut * part, 16), part)
        return pltpu.make_async_remote_copy(
            packed_ref.at[to, source], gate_up_ref.at[target], sem_w.at[n], got_w.at[s, cut],
            device_id=(to, t), device_id_type=mesh_id)

    def arrived_w(origin, cut):
        part = packed_ref.shape[1] // 4
        target = pl.ds(pl.multiple_of(origin * packed_ref.shape[1] + cut * part, 16), part)
        return pltpu.make_async_remote_copy(
            packed_ref.at[0, :part], gate_up_ref.at[target], sem_w.at[0], got_w.at[origin, cut],
            device_id=side, device_id_type=mesh_id)

    own_weights = pltpu.make_async_copy(
        packed_ref.at[s],
        gate_up_ref.at[pl.ds(pl.multiple_of(s * packed_ref.shape[1], 16), packed_ref.shape[1])],
        sem_own.at[0])
    own_weights.start()

    def pump(n):
        weight_copy(n).start()

    def query_z(r, direction):
        b = r * 2 + x
        return pltpu.make_async_remote_copy(
            queries.at[b], queries.at[b], sem_qz.at[r, (direction + 1) // 2], got_q.at[b],
            device_id=((z + direction) * 2 + x, t), device_id_type=mesh_id)

    def query_x(r):
        b = r * 2 + x
        return pltpu.make_async_remote_copy(
            queries.at[b], queries.at[b], sem_qx.at[r], got_q.at[b], device_id=side, device_id_type=mesh_id)

    def arrived_q(b):
        return pltpu.make_async_remote_copy(
            queries.at[b], queries.at[b], sem_qx.at[0], got_q.at[b], device_id=side, device_id_type=mesh_id)

    def part_x(i):
        return pltpu.make_async_remote_copy(
            sent.at[i], peer_x.at[i], sem_x.at[i], got_x.at[i], device_id=side, device_id_type=mesh_id)

    def part_z(i):
        return pltpu.make_async_remote_copy(
            merged.at[i], peer_z.at[z], sem_z.at[i], got_z.at[z],
            device_id=(nearest(z, i + 1) * 2 + x, t), device_id_type=mesh_id)

    def arrived_z(z_from):
        return pltpu.make_async_remote_copy(
            merged.at[0], peer_z.at[z_from], sem_z.at[0], got_z.at[z_from], device_id=side, device_id_type=mesh_id)

    for direction in (-1, 1):
        @pl.when((z + direction >= 0) & (z + direction < 4))
        def _():
            query_z(z, direction).start()
    query_x(z).start()

    base = s * (2 * pairs)
    lane = lanes_of(pairs)
    row_lane = lanes_of(rows)
    below = lane < 64

    def spread(block, fill, scale):
        plain = block.astype(f32)
        if scale != 1.0:
            plain = plain * scale
        turned = pltpu.roll(plain, 64, 1)
        keep = lanes_of(block.shape[0]) < 64
        return (
            (jnp.where(keep, plain, fill).astype(bf16), jnp.where(keep, turned, fill).astype(bf16)),
            (jnp.where(keep, fill, turned).astype(bf16), jnp.where(keep, fill, plain).astype(bf16)),
        )

    def attend(r, fresh, between, pumped):
        length = lens_ref[r]
        slot = lax.broadcasted_iota(jnp.int32, (1, 2 * pairs), 1)
        position = base + 2 * (slot % pairs) + slot // pairs
        bias = jnp.where(position < length, 0.0, NEGATIVE)
        for j in range(heads // group):
            if j == 1:
                between()
            key_two = spread(k_ref[r, j], 0.0, 0.125)
            value_two = spread(v_ref[r, j], 1.0, 1.0)
            for parity in range(2):
                keys[parity, :pairs] = key_two[parity][0]
                keys[parity, pairs : 2 * pairs] = key_two[parity][1]
                values[parity, :pairs] = value_two[parity][0]
                values[parity, pairs : 2 * pairs] = value_two[parity][1]
            if fresh:
                new_keys = spread(fk_ref[j], 0.0, 0.125)
                new_values = spread(fv_ref[j], 1.0, 1.0)
            for g in range(j * group, (j + 1) * group):
                parity = g % 2
                for part in range(2):
                    query = queries[r * 2 + part, :rows, g // 2 * 128 : g // 2 * 128 + 128]
                    score = lax.dot_general(query, keys[parity], nt, preferred_element_type=f32) + bias
                    peak = jnp.max(score, axis=1, keepdims=True)
                    if fresh:
                        new_key = new_keys[0][0] if parity == 0 else new_keys[1][0]
                        new_value = new_values[0][0] if parity == 0 else new_values[1][0]
                        row_q = part * rows + lax.broadcasted_iota(jnp.int32, (rows, rows), 0)
                        row_k = x * rows + lax.broadcasted_iota(jnp.int32, (rows, rows), 1)
                        new_score = lax.dot_general(query, new_key, nt, preferred_element_type=f32)
                        new_score = new_score + jnp.where(row_k <= row_q, 0.0, NEGATIVE)
                        peak = jnp.maximum(peak, jnp.max(new_score, axis=1, keepdims=True))
                    weight = jnp.exp(score - peak).astype(bf16)
                    total = jnp.dot(weight, values[parity], preferred_element_type=f32)
                    if fresh:
                        weight = jnp.exp(new_score - peak).astype(bf16)
                        total = total + jnp.dot(weight, new_value, preferred_element_type=f32)
                    turned = pltpu.roll(total, 64, 1)
                    if parity == 0:
                        sums = jnp.where(row_lane < 64, turned, total)
                    else:
                        sums = jnp.where(row_lane < 64, total, turned)
                    level = peak + jnp.log(sums)
                    result = total / sums
                    at = pl.ds(part * rows, rows)
                    if g == 0:
                        level_tail[at, :] = level
                    else:
                        level_tail[at, :] = jnp.where(row_lane == g, level, level_tail[at, :])
                    tile = pl.ds(g // 2 * 128, 128)
                    if parity == 0:
                        mixed[at, tile] = result
                    else:
                        mixed[at, tile] = jnp.where(row_lane < 64, mixed[at, tile], result)
                if parity == 1:
                    pump(pumped + g // 2)

    def hand_over(i):
        own = pl.ds(pl.multiple_of(x * rows, rows), rows)
        away = pl.ds(pl.multiple_of((1 - x) * rows, rows), rows)
        sent[i, :, :features] = mixed[away, :].astype(bf16)
        sent[i, :, features:] = write_levels(level_tail[away, :], heads).astype(bf16)
        part_x(i).start()
        held[i, :, :features] = mixed[own, :].astype(bf16)
        held[i, :, features:] = write_levels(level_tail[own, :], heads).astype(bf16)

    def merge_x(i):
        part_x(i).wait_recv()
        tiles, level = merge([held[i], peer_x[i]], heads)
        for n, tile in enumerate(tiles):
            merged[i, :, n * 128 : n * 128 + 128] = tile.astype(bf16)
        merged[i, :, features:] = write_levels(level, heads).astype(bf16)

    def forward(i):
        r = nearest(z, i + 1)
        arrived_q(r * 2 + x).wait_recv()
        for direction in (-1, 1):
            @pl.when(((z - r) * direction > 0) & (z + direction >= 0) & (z + direction < 4))
            def _():
                query_z(r, direction).start()
        query_x(r).start()

    forward(0)
    forward(1)

    def step(i, carry):
        r = nearest(z, i + 1)
        arrived_q(r * 2 + 1 - x).wait_recv()

        def between():
            @pl.when(i == 0)
            def _():
                forward(2)

        attend(r, False, between, 3 * i)
        hand_over(i)

        @pl.when(i > 0)
        def _():
            merge_x(i - 1)
            part_z(i - 1).start()
        return carry

    lax.fori_loop(0, 3, step, 0)
    arrived_q(z * 2 + 1 - x).wait_recv()

    def between():
        merge_x(2)
        part_z(2).start()

    attend(z, True, between, 9)
    hand_over(3)
    merge_x(3)
    pieces = [merged[3]]
    for step_z in range(1, 4):
        z_from = (z + step_z) % 4
        arrived_z(z_from).wait_recv()
        pieces.append(peer_z[z_from])
    tiles, _ = merge(pieces, heads)
    heads_out = jnp.concatenate([tile.astype(bf16) for tile in tiles], axis=1)

    def exchange(n, source, target, to):
        return pltpu.make_async_remote_copy(
            source, target, sem_t.at[n], got_t.at[n], device_id=to, device_id_type=mesh_id)

    parting[...] = jnp.dot(heads_out, w_out_ref[:, others], preferred_element_type=f32).astype(bf16)
    first = exchange(0, parting, got_twin, twin)
    first.start()
    pump(12)
    own = jnp.dot(heads_out, w_out_ref[:, mine], preferred_element_type=f32)
    first.wait_recv()
    half_sum[...] = (own + got_twin[...].astype(f32)).astype(bf16)
    second = exchange(1, half_sum, got_across, across)
    second.start()
    pump(13)
    pump(14)
    second.wait_recv()
    joined[:, mine] = (half_sum[...].astype(f32) + got_across[...].astype(f32)).astype(bf16)
    third = exchange(2, joined.at[:, mine], joined.at[:, mine], twin)
    third.start()
    pump(15)
    third.wait_recv()
    attn_ref[...] = joined[...]
    stream = tokens_ref[...].astype(f32) + joined[...].astype(f32)
    normed = rms_norm(stream, gain_ref[...])
    blocks[s] = normed.astype(bf16)

    def away(b, direction):
        return pltpu.make_async_remote_copy(
            blocks.at[b, :, mine], blocks.at[b, :, mine], sem_away.at[b, (direction + 1) // 2], got_link.at[b],
            device_id=((z + direction) * 2 + x, t), device_id_type=mesh_id)

    def sideways(b):
        return pltpu.make_async_remote_copy(
            blocks.at[b, :, mine], blocks.at[b, :, mine], sem_side.at[b], got_link.at[b],
            device_id=side, device_id_type=mesh_id)

    def to_twin(b):
        return pltpu.make_async_remote_copy(
            blocks.at[b, :, mine], blocks.at[b, :, mine], sem_core.at[b], got_core.at[b],
            device_id=twin, device_id_type=mesh_id)

    def copy_a(i):
        return pltpu.make_async_remote_copy(
            other_half.at[i], from_core.at[i], sem_a.at[i], got_a.at[i], device_id=twin, device_id_type=mesh_id)

    def copy_b(i):
        cut = pl.ds(pl.multiple_of((1 - y) * quarter, 128), quarter)
        return pltpu.make_async_remote_copy(
            own_half.at[i, :, cut], from_y.at[i], sem_b.at[i], got_b.at[i], device_id=across, device_id_type=mesh_id)

    def copy_c(j):
        return pltpu.make_async_remote_copy(
            passed.at[j], from_x.at[j], sem_c.at[j], got_c.at[j], device_id=side, device_id_type=mesh_id)

    def copy_d(j):
        return pltpu.make_async_remote_copy(
            partial.at[j], from_z.at[z], sem_d.at[j], got_d.at[z],
            device_id=(nearest(z, 3 - j) * 2 + x, t), device_id_type=mesh_id)

    def arrive_d(z_from):
        return pltpu.make_async_remote_copy(
            partial.at[0], from_z.at[z_from], sem_d.at[0], got_d.at[z_from],
            device_id=side, device_id_type=mesh_id)

    for direction in (-1, 1):
        @pl.when((z + direction >= 0) & (z + direction < 4))
        def _():
            away(s, direction).start()
    sideways(s).start()

    def block_of(i):
        k = i % 2
        return nearest(z, i // 2) * 2 + jnp.where(k == 0, x, 1 - x)

    pump(16)
    pump(17)

    def take_z(j):
        b = nearest(z, j) * 2 + x
        sideways(b).wait_recv()
        for direction in (-1, 1):
            @pl.when(((z - nearest(z, j)) * direction > 0) & (z + direction >= 0) & (z + direction < 4))
            def _():
                away(b, direction).start()
        sideways(b).start()
        to_twin(b).start()

    def take_x(j):
        b = nearest(z, j) * 2 + 1 - x
        sideways(b).wait_recv()
        to_twin(b).start()

    n = 18
    for j in range(4):
        if j < 3:
            take_z(j + 1)
            for _ in range(3):
                pump(n)
                n += 1
        if j == 3:
            pump(n)
        take_x(j)
    for n in range(28):
        weight_copy(n).wait_send()
    own_weights.wait()
    for step_s in range(1, 8):
        for cut in range(4):
            arrived_w((s + step_s) % 8, cut).wait_recv()

    expert_of = lanes_of(rows).astype(f32)
    as_columns = jnp.where(lax.broadcasted_iota(jnp.int32, ((queries.shape[1] - rows), 128), 0) == lanes_of((queries.shape[1] - rows)), 1.0, 0.0).astype(jnp.bfloat16)
    expert_lane = lax.broadcasted_iota(jnp.int32, (128, units), 0)
    expert_unit = lax.broadcasted_iota(jnp.int32, (128, units), 1)

    def compute(i, carry):
        @pl.when(i < 8)
        def _():
            b = nearest(z, 3 - i // 2) * 2 + jnp.where(i % 2 == 0, 1 - x, x)

            @pl.when(i < 7)
            def _():
                to_twin(b).wait_recv()

            tokens = blocks[b]
            logits = jnp.dot(tokens, router_ref[...], preferred_element_type=f32)
            named = lax.dot_general(queries[b, rows:, :rows], as_columns, (((0,), (0,)), ((), ())), preferred_element_type=f32)
            chosen = named[:, 0:1] == expert_of
            for k in range(1, 8):
                chosen = chosen | (named[:, k : k + 1] == expert_of)
            logits = jnp.where(chosen, logits, NEGATIVE)
            gates = jnp.where(chosen, jnp.exp(logits - jnp.max(logits, axis=1, keepdims=True)), 0.0)
            share = gates / jnp.sum(gates, axis=1, keepdims=True)
            high = share.astype(jnp.bfloat16)
            low = (share - high.astype(f32)).astype(jnp.bfloat16)
            spread = jnp.where(expert_lane == t * (units // 64) + expert_unit // 64, 1.0, 0.0).astype(jnp.bfloat16)
            shares = jnp.dot(high, spread, preferred_element_type=f32) + jnp.dot(low, spread, preferred_element_type=f32)
            for p in range(units // 128):
                both = jnp.dot(tokens, gate_up_ref[:, p * 256 : p * 256 + 256], preferred_element_type=f32)
                gate, up = both[:, :128], both[:, 128:]
                value = gate / (1.0 + jnp.exp(-gate)) * up * shares[:, p * 128 : p * 128 + 128]
                hidden[:, p * 128 : p * 128 + 128] = value.astype(jnp.bfloat16)
            other_half[i] = jnp.dot(hidden[...], down_ref[:, others], preferred_element_type=f32).astype(jnp.bfloat16)
            copy_a(i).start()
            own_half[i] = jnp.dot(hidden[...], down_ref[:, mine], preferred_element_type=f32).astype(jnp.bfloat16)

        @pl.when((i >= 1) & (i < 9))
        def _():
            n = i - 1
            copy_a(n).wait_recv()
            own_half[n] = (own_half[n].astype(f32) + from_core[n].astype(f32)).astype(jnp.bfloat16)
            copy_b(n).start()

        @pl.when((i >= 4) & (i < 12))
        def _():
            n = i - 4
            copy_b(n).wait_recv()
            cut = pl.ds(pl.multiple_of(y * quarter, 128), quarter)
            total = (own_half[n, :, cut].astype(f32) + from_y[n].astype(f32)).astype(jnp.bfloat16)

            @pl.when(n % 2 == 1)
            def _():
                kept[n // 2] = total

            @pl.when(n % 2 == 0)
            def _():
                passed[n // 2] = total
                copy_c(n // 2).start()

        @pl.when((i >= 6) & (i % 2 == 0))
        def _():
            j = i // 2 - 3
            copy_c(j).wait_recv()
            partial[j] = (kept[j].astype(f32) + from_x[j].astype(f32)).astype(jnp.bfloat16)

            @pl.when(j < 3)
            def _():
                copy_d(j).start()
        return carry

    lax.fori_loop(0, 13, compute, 0)

    total = partial[3].astype(f32)
    for step_z in range(1, 4):
        z_from = (z + step_z) % 4
        arrive_d(z_from).wait_recv()
        total = total + from_z[z_from].astype(f32)

    def copy_e(n, to):
        at = c * half + y * quarter if n == 0 else c * half
        size = quarter if n == 0 else half
        cut = pl.ds(pl.multiple_of(at, 128), size)
        return pltpu.make_async_remote_copy(
            final.at[:, cut], final.at[:, cut], sem_e.at[n], got_e.at[n], device_id=to, device_id_type=mesh_id)

    final[:, pl.ds(pl.multiple_of(c * half + y * quarter, 128), quarter)] = total.astype(jnp.bfloat16)
    copy_e(0, across).start()
    copy_e(0, across).wait_recv()
    copy_e(1, twin).start()
    copy_e(1, twin).wait_recv()
    out_ref[...] = final[...]

    def drain(i, carry):
        b = block_of(i)
        zj = nearest(z, i // 2)

        @pl.when(i > 0)
        def _():
            to_twin(b).wait_send()

        @pl.when(i % 2 == 0)
        def _():
            sideways(b).wait_send()
            for direction in (-1, 1):
                @pl.when(((z - zj) * direction >= 0) & (z + direction >= 0) & (z + direction < 4))
                def _():
                    away(b, direction).wait_send()
            copy_c(i // 2).wait_send()

            @pl.when(i < 6)
            def _():
                copy_d(i // 2).wait_send()

        copy_a(i).wait_send()
        copy_b(i).wait_send()
        return carry

    lax.fori_loop(0, 8, drain, 0)
    copy_e(0, across).wait_send()
    copy_e(1, twin).wait_send()
    for j in range(4):
        query_x(nearest(z, j)).wait_send()
        part_x(j).wait_send()
        for direction in (-1, 1):
            @pl.when(((z - nearest(z, j)) * direction >= 0) & (z + direction >= 0) & (z + direction < 4))
            def _():
                query_z(nearest(z, j), direction).wait_send()
    for j in range(3):
        part_z(j).wait_send()
    first.wait_send()
    second.wait_send()
    third.wait_send()


def layer(lens, query, keys, values, fresh_key, fresh_value, w_out, tokens, gain, packed, router, down):
    features = query.shape[1]
    rows, width = tokens.shape
    extra = query.shape[0] - rows
    requests, local_kv, pairs, _ = keys.shape
    units = down.shape[0]
    half, quarter = width // 2, width // 4
    bf16, f32 = jnp.bfloat16, jnp.float32
    dma = pltpu.SemaphoreType.DMA
    vmem = pl.BlockSpec(memory_space=pltpu.VMEM)
    scores = requests * FRESH_TOKENS * (features // 64) * 2 * pairs
    return pl.pallas_call(
        layer_kernel,
        out_shape=[jax.ShapeDtypeStruct((rows, width), bf16)] * 2,
        in_specs=[pl.BlockSpec(memory_space=pltpu.SMEM)] + [vmem] * 8 + [pl.BlockSpec(memory_space=pl.ANY)] + [vmem] * 2,
        out_specs=[vmem] * 2,
        scratch_shapes=[
            pltpu.VMEM((8, rows + extra, features), bf16),
            pltpu.VMEM((2, 2 * pairs, 128), bf16),
            pltpu.VMEM((2, 2 * pairs, 128), bf16),
            pltpu.VMEM((2 * rows, features), f32),
            pltpu.VMEM((2 * rows, 128), f32),
            pltpu.VMEM((4, rows, features + 128), bf16),
            pltpu.VMEM((4, rows, features + 128), bf16),
            pltpu.VMEM((4, rows, features + 128), bf16),
            pltpu.VMEM((4, rows, features + 128), bf16),
            pltpu.VMEM((4, rows, features + 128), bf16),
            pltpu.VMEM((rows, width // 2), bf16),
            pltpu.VMEM((rows, width // 2), bf16),
            pltpu.VMEM((rows, width // 2), bf16),
            pltpu.VMEM((rows, width // 2), bf16),
            pltpu.VMEM((rows, width), bf16),
            pltpu.VMEM((width, 2 * units), bf16),
            pltpu.VMEM((8, rows, width), bf16),
            pltpu.VMEM((rows, units), bf16),
            pltpu.VMEM((8, rows, half), bf16),
            pltpu.VMEM((8, rows, half), bf16),
            pltpu.VMEM((8, rows, half), bf16),
            pltpu.VMEM((8, rows, quarter), bf16),
            pltpu.VMEM((4, rows, quarter), bf16),
            pltpu.VMEM((4, rows, quarter), bf16),
            pltpu.VMEM((4, rows, quarter), bf16),
            pltpu.VMEM((4, rows, quarter), bf16),
            pltpu.VMEM((4, rows, quarter), bf16),
            pltpu.VMEM((rows, width), bf16),
            dma((4, 2)), dma((4,)), dma((8,)), dma((4,)), dma((4,)), dma((4,)), dma((4,)), dma((3,)), dma((3,)), dma((28,)), dma((8, 4)), dma((1,)),
            dma((8, 2)), dma((8,)), dma((8,)), dma((8,)), dma((8,)),
            dma((8,)), dma((8,)), dma((8,)), dma((8,)), dma((4,)), dma((4,)), dma((4,)), dma((4,)), dma((2,)), dma((2,)),
        ],
        compiler_params=pltpu.CompilerParams(
            collective_id=0, has_side_effects=True, vmem_limit_bytes=60 * 1024 * 1024
        ),
        cost_estimate=pl.CostEstimate(flops=64 * 4 * scores, bytes_accessed=16 << 20, transcendentals=scores),
    )(lens, query, keys, values, fresh_key, fresh_value, w_out, tokens, gain, packed, router, down)


def swap_cores(values):
    count = lax.axis_size("tp")
    return lax.ppermute(values, "tp", [(i, i ^ 1) for i in range(count)])


def sum_halves(mine, others):
    received = swap_cores(others.astype(jnp.bfloat16)).astype(jnp.float32)
    return (mine + received).astype(jnp.bfloat16)


def sum_chips(values):
    count = lax.axis_size("tp")
    step = 2
    total = values.astype(jnp.float32)
    while step < count:
        sent = total.astype(jnp.bfloat16)
        received = lax.ppermute(sent, "tp", [(i, i ^ step) for i in range(count)])
        total = sent.astype(jnp.float32) + received.astype(jnp.float32)
        step = step * 2
    return total.astype(jnp.bfloat16)


def join_halves(values, core):
    other = swap_cores(values)
    first = jnp.where(core == 0, values, other)
    second = jnp.where(core == 0, other, values)
    return jnp.concatenate([first, second], axis=1)


def per_device(
    tokens,
    norm1_gain,
    w_query,
    key_weight,
    value_weight,
    rotated_key_cache,
    stored_value_cache,
    cache_len,
    w_out,
    norm2_gain,
    w_router,
    expert_ids,
    w_gate_up,
    w_down,
):
    tok_rows, width = tokens.shape
    seq_pos = lax.axis_index("seq")
    tp_pos = lax.axis_index("tp")
    local_q = w_query.shape[0] // HEAD_SIZE
    local_kv = key_weight.shape[0] // HEAD_SIZE
    requests = rotated_key_cache.shape[0]
    span = rotated_key_cache.shape[2] // HEAD_SIZE
    inputs = tokens.astype(jnp.float32)
    devices = lax.axis_size("seq")
    local_experts, _, own_width, hidden_size = w_gate_up.shape
    own_hidden = hidden_size // devices
    normalized_input = rms_norm(inputs, norm1_gain).astype(jnp.bfloat16)
    row_ids = seq_pos * tok_rows + jnp.arange(tok_rows, dtype=jnp.int32)
    owners = row_ids // FRESH_TOKENS
    positions = lookup(cache_len, owners) + row_ids % FRESH_TOKENS
    angle_position = positions.astype(jnp.float32)
    query_vector = apply_rotary(
        apply_projection(normalized_input, w_query).reshape(tok_rows, local_q, HEAD_SIZE),
        angle_position,
    ).astype(jnp.bfloat16)
    units = local_experts * own_hidden
    by_owner = jnp.transpose(
        w_gate_up.reshape(local_experts, 2, own_width, devices, own_hidden), (3, 2, 1, 0, 4)
    ).reshape(width, 2 * units)
    fresh_key = apply_rotary(
        apply_projection(normalized_input, key_weight).reshape(tok_rows, local_kv, HEAD_SIZE),
        angle_position,
    ).astype(jnp.bfloat16)
    fresh_value = (
        apply_projection(normalized_input, value_weight)
        .astype(jnp.bfloat16)
        .reshape(tok_rows, local_kv, HEAD_SIZE)
    )
    all_query = lax.all_gather(
        query_vector.reshape(tok_rows, local_q * HEAD_SIZE), "seq", axis=0, tiled=True
    )
    all_query, by_owner = lax.optimization_barrier((all_query, by_owner))
    own_gate_up = lax.all_to_all(by_owner, "seq", 0, 0, tiled=True)
    paired = (requests, local_kv, span // 2, 2 * HEAD_SIZE)
    pad = ((0, 0), (0, 0), (0, HEAD_SIZE))
    parts = attend(
        jnp.concatenate([seq_pos[None].astype(jnp.int32), cache_len]),
        all_query,
        rotated_key_cache.reshape(paired),
        stored_value_cache.reshape(paired),
        jnp.pad(jnp.transpose(fresh_key, (1, 0, 2)), pad),
        jnp.pad(jnp.transpose(fresh_value, (1, 0, 2)), pad),
        tok_rows,
        local_q,
    )
    parts, own_gate_up = lax.optimization_barrier((parts, own_gate_up))
    parts = lax.all_to_all(parts, "seq", 0, 0, tiled=True)
    parts = parts.astype(jnp.float32)
    features = local_q * HEAD_SIZE
    tails = parts.shape[2] - 128
    pieces = parts[:, :, tails : tails + 3 * local_q]
    level = pieces[..., :local_q] + pieces[..., local_q : 2 * local_q] + pieces[..., 2 * local_q :]
    factor = jnp.exp(level - jnp.max(level, axis=0, keepdims=True))
    factor = factor / jnp.sum(factor, axis=0, keepdims=True)
    feature_head = jnp.arange(features, dtype=jnp.int32) // HEAD_SIZE
    widen = (jnp.arange(local_q, dtype=jnp.int32)[:, None] == feature_head[None, :]).astype(jnp.float32)
    factor = jnp.einsum("sth,hf->stf", factor, widen, precision=lax.Precision.HIGHEST)
    heads_out = jnp.sum(parts[:, :, :features] * factor, axis=0).astype(jnp.bfloat16)
    attn_part = jnp.dot(heads_out, w_out, preferred_element_type=jnp.float32)
    core = tp_pos % 2
    half = width // 2
    attn = sum_halves(
        lax.dynamic_slice_in_dim(attn_part, core * half, half, 1),
        lax.dynamic_slice_in_dim(attn_part, (1 - core) * half, half, 1),
    )
    attn = join_halves(sum_chips(attn), core).astype(jnp.float32)
    attn_out = attn.astype(jnp.bfloat16)
    normed2 = rms_norm(inputs + attn, norm2_gain).astype(jnp.bfloat16)
    logits = jnp.dot(normed2, w_router, preferred_element_type=jnp.float32)
    experts_all = w_router.shape[1]
    picked_all = expert_ids[:, :, None] == jnp.arange(experts_all, dtype=jnp.int32)[None, None, :]
    chosen = jnp.sum(jnp.where(picked_all, logits[:, None, :], 0.0), axis=-1)
    gates = jax.nn.softmax(chosen, axis=-1)
    local_ids = tp_pos * local_experts + jnp.arange(local_experts, dtype=jnp.int32)
    picked = expert_ids[:, :, None] == local_ids[None, None, :]
    share = jnp.sum(jnp.where(picked, gates[:, :, None], 0.0), axis=1)
    share_high = lax.reduce_precision(share, 8, 7)
    packed = jnp.concatenate(
        [
            lax.dynamic_slice_in_dim(normed2, core * half, half, 1),
            share_high.astype(jnp.bfloat16),
            (share - share_high).astype(jnp.bfloat16),
            jnp.zeros((tok_rows, 128 - 2 * local_experts), jnp.bfloat16),
        ],
        axis=1,
    )
    packed = lax.all_gather(packed, "seq", axis=0, tiled=True)
    others = swap_cores(packed[:, :half])
    unit_expert = jnp.arange(units, dtype=jnp.int32) // own_hidden
    lanes = jnp.arange(128, dtype=jnp.int32)
    spread = (lanes[:, None] % local_experts == unit_expert[None, :]) & (lanes[:, None] < 2 * local_experts)
    share_all = jnp.dot(packed[:, half:], spread.astype(jnp.bfloat16), preferred_element_type=jnp.float32)
    gate_up_mine = lax.dynamic_slice_in_dim(own_gate_up, core * half, half, 0)
    gate_up_others = lax.dynamic_slice_in_dim(own_gate_up, (1 - core) * half, half, 0)
    both = jnp.dot(packed[:, :half], gate_up_mine, preferred_element_type=jnp.float32)
    both = both + jnp.dot(others, gate_up_others, preferred_element_type=jnp.float32)
    hidden = (jax.nn.silu(both[:, :units]) * both[:, units:] * share_all).astype(jnp.bfloat16)
    down = w_down.reshape(units, width)
    down_mine = lax.dynamic_slice_in_dim(down, core * half, half, 1)
    down_others = lax.dynamic_slice_in_dim(down, (1 - core) * half, half, 1)
    moe_half = sum_halves(
        jnp.dot(hidden, down_mine, preferred_element_type=jnp.float32),
        jnp.dot(hidden, down_others, preferred_element_type=jnp.float32),
    )
    moe_half = lax.psum_scatter(moe_half, "seq", scatter_dimension=0, tiled=True)
    expert_out = join_halves(sum_chips(moe_half.astype(jnp.float32)), core)
    return (attn_out, expert_out)


def per_device_block(
    tokens,
    norm1_gain,
    w_query,
    key_weight,
    value_weight,
    rotated_key_cache,
    stored_value_cache,
    cache_len,
    w_out,
    norm2_gain,
    w_router,
    expert_ids,
    w_gate_up,
    w_down,
):
    tok_rows, width = tokens.shape
    seq_pos = lax.axis_index("seq")
    tp_pos = lax.axis_index("tp")
    local_q = w_query.shape[0] // HEAD_SIZE
    local_kv = key_weight.shape[0] // HEAD_SIZE
    requests = rotated_key_cache.shape[0]
    span = rotated_key_cache.shape[2] // HEAD_SIZE
    inputs = tokens.astype(jnp.float32)
    devices = lax.axis_size("seq")
    local_experts, _, own_width, hidden_size = w_gate_up.shape
    own_hidden = hidden_size // devices
    normalized_input = rms_norm(inputs, norm1_gain).astype(jnp.bfloat16)
    row_ids = seq_pos * tok_rows + jnp.arange(tok_rows, dtype=jnp.int32)
    owners = row_ids // FRESH_TOKENS
    positions = lookup(cache_len, owners) + row_ids % FRESH_TOKENS
    angle_position = positions.astype(jnp.float32)
    query_vector = apply_rotary(
        apply_projection(normalized_input, w_query).reshape(tok_rows, local_q, HEAD_SIZE),
        angle_position,
    ).astype(jnp.bfloat16)
    units = local_experts * own_hidden
    by_owner = pack_gate_up(w_gate_up)
    fresh_key = apply_rotary(
        apply_projection(normalized_input, key_weight).reshape(tok_rows, local_kv, HEAD_SIZE),
        angle_position,
    ).astype(jnp.bfloat16)
    fresh_value = (
        apply_projection(normalized_input, value_weight)
        .astype(jnp.bfloat16)
        .reshape(tok_rows, local_kv, HEAD_SIZE)
    )
    ids = jnp.pad(expert_ids.T.astype(jnp.bfloat16), ((0, 8), (0, local_q * HEAD_SIZE - tok_rows)))
    paired = (requests, local_kv, span // 2, 2 * HEAD_SIZE)
    pad = ((0, 0), (0, 0), (0, HEAD_SIZE))
    router = jnp.pad(w_router, ((0, 0), (0, 128 - w_router.shape[1])))
    return layer(
        cache_len,
        jnp.concatenate([query_vector.reshape(tok_rows, local_q * HEAD_SIZE), ids]),
        rotated_key_cache.reshape(paired),
        stored_value_cache.reshape(paired),
        jnp.pad(jnp.transpose(fresh_key, (1, 0, 2)), pad),
        jnp.pad(jnp.transpose(fresh_value, (1, 0, 2)), pad),
        w_out,
        tokens,
        norm2_gain[None, :],
        by_owner,
        router,
        w_down.reshape(units, width),
    )


def solution(mesh):
    block = mesh.shape["seq"] == 8 and mesh.shape["tp"] == 4
    return jax.shard_map(
        per_device_block if block else per_device,
        mesh=mesh,
        in_specs=(
            P("seq", None),
            P(),
            P("tp", None),
            P("tp", None),
            P("tp", None),
            P(None, "tp", "seq"),
            P(None, "tp", "seq"),
            P(),
            P("tp", None),
            P(),
            P(),
            P("seq", None),
            P("tp", None, "seq", None),
            P("tp", "seq", None),
        ),
        out_specs=(P("seq", None), P("seq", None)),
        check_vma=False,
    )
```

```python
import functools

import jax
import jax.numpy as jnp
from jax import lax
from jax.experimental import pallas as pl
from jax.experimental.pallas import tpu as pltpu
from jax.sharding import PartitionSpec as P

HEAD_SIZE = 64
FRESH_TOKENS = 512


EPS = 1e-05
THETA = 10000.0
NEGATIVE = -1e30
WEIGHT_PLAN = (0, 1, 1, 3)


def rms_norm(values, gain):
    mean_square = jnp.mean(values * values, axis=-1, keepdims=True)
    return values * lax.rsqrt(mean_square + EPS) * gain.astype(values.dtype)


def apply_rotary(values, positions):
    half_dim = values.shape[-1] // 2
    exponent = jnp.arange(half_dim, dtype=jnp.float32) * (2.0 / values.shape[-1])
    freqs = THETA ** (-exponent)
    angles = positions[:, None] * freqs[None, :]
    cosine = jnp.cos(angles)[:, None, :]
    sine = jnp.sin(angles)[:, None, :]
    first = values[..., :half_dim]
    second = values[..., half_dim:]
    return jnp.concatenate(
        [first * cosine - second * sine, second * cosine + first * sine], axis=-1
    )


def apply_projection(normalized_input, weight):
    return jnp.einsum("td,fd->tf", normalized_input, weight, preferred_element_type=jnp.float32)


def lookup(table, index):
    hits = index[:, None] == jnp.arange(table.shape[0], dtype=jnp.int32)[None, :]
    return jnp.sum(jnp.where(hits, table[None, :], 0), axis=1)


def attend_kernel(group, info, q_ref, k_ref, v_ref, fk_ref, fv_ref, out_ref, peak_ref, sum_ref, acc_ref):
    heads, rows = acc_ref.shape[0], acc_ref.shape[1]
    pairs = k_ref.shape[2]
    columns = q_ref.shape[1]
    dest = pl.program_id(0)
    me = info[0]
    per = FRESH_TOKENS // rows
    length = info[1 + dest // per]
    base = me * (2 * pairs)
    col = lax.broadcasted_iota(jnp.int32, (columns, 128), 0)
    lane = lax.broadcasted_iota(jnp.int32, (columns, 128), 1)
    out_lane = lax.broadcasted_iota(jnp.int32, (rows, 128), 1)
    has_cache = base < length
    has_fresh = (dest // per == me // per) & (dest >= me)
    nt = (((1,), (1,)), ((), ()))

    def pick(g, odd):
        hit = (col == g * HEAD_SIZE + lane - odd * HEAD_SIZE) & (lane // HEAD_SIZE == odd)
        select = jnp.where(hit, HEAD_SIZE ** (-0.5), 0.0).astype(jnp.bfloat16)
        return jnp.dot(q_ref[...], select, preferred_element_type=jnp.float32).astype(jnp.bfloat16)

    @pl.when(jnp.logical_not(has_cache))
    def _():
        peak_ref[...] = jnp.full_like(peak_ref, NEGATIVE)
        sum_ref[...] = jnp.zeros_like(sum_ref)
        acc_ref[...] = jnp.zeros_like(acc_ref)

    @pl.when(has_cache)
    def _():
        even_pos = base + 2 * lax.broadcasted_iota(jnp.int32, (1, pairs), 1)
        even_bias = jnp.where(even_pos < length, 0.0, NEGATIVE)
        odd_bias = jnp.where(even_pos + 1 < length, 0.0, NEGATIVE)
        @pl.loop(0, heads // group)
        def _(j):
            for i in range(group):
                g = j * group + i
                keys = k_ref[0, j]
                values = v_ref[0, j]
                even = lax.dot_general(pick(g, 0), keys, nt, preferred_element_type=jnp.float32) + even_bias
                odd = lax.dot_general(pick(g, 1), keys, nt, preferred_element_type=jnp.float32) + odd_bias
                peak = jnp.max(jnp.maximum(even, odd), axis=1, keepdims=True)
                even = jnp.exp(even - peak)
                odd = jnp.exp(odd - peak)
                total = jnp.sum(even + odd, axis=1, keepdims=True)
                mix_even = jnp.dot(even.astype(jnp.bfloat16), values, preferred_element_type=jnp.float32)
                mix_odd = jnp.dot(odd.astype(jnp.bfloat16), values, preferred_element_type=jnp.float32)
                mixed = jnp.where(out_lane < HEAD_SIZE, mix_even, mix_odd)
                peak_ref[g] = jnp.broadcast_to(peak, (rows, 128))
                sum_ref[g] = jnp.broadcast_to(total, (rows, 128))
                acc_ref[g] = mixed

    @pl.when(has_fresh)
    def _():
        row_q = dest * rows + lax.broadcasted_iota(jnp.int32, (rows, rows), 0)
        row_k = me * rows + lax.broadcasted_iota(jnp.int32, (rows, rows), 1)
        bias = jnp.where(row_k <= row_q, 0.0, NEGATIVE)
        @pl.loop(0, heads // group)
        def _(j):
            for i in range(group):
                g = j * group + i
                score = lax.dot_general(pick(g, 0), fk_ref[j], nt, preferred_element_type=jnp.float32) + bias
                old = peak_ref[g][:, :1]
                peak = jnp.maximum(old, jnp.max(score, axis=1, keepdims=True))
                weight = jnp.exp(score - peak)
                factor = jnp.exp(old - peak)
                total = sum_ref[g][:, :1] * factor + jnp.sum(weight, axis=1, keepdims=True)
                mix = jnp.dot(weight.astype(jnp.bfloat16), fv_ref[j], preferred_element_type=jnp.float32)
                acc_ref[g] = acc_ref[g] * factor + mix
                peak_ref[g] = jnp.broadcast_to(peak, (rows, 128))
                sum_ref[g] = jnp.broadcast_to(total, (rows, 128))

    tail = jnp.zeros((rows, 128), jnp.float32)
    left = None
    for g in range(heads):
        acc = acc_ref[g]
        acc = acc + pltpu.roll(acc, HEAD_SIZE, 1)
        total = sum_ref[g]
        some = total > 0.0
        safe = jnp.where(some, total, 1.0)
        level = jnp.where(some, peak_ref[g] + jnp.log(safe), NEGATIVE)
        high = level.astype(jnp.bfloat16).astype(jnp.float32)
        middle = (level - high).astype(jnp.bfloat16).astype(jnp.float32)
        low = level - high - middle
        tail = jnp.where(out_lane == g, high, tail)
        tail = jnp.where(out_lane == heads + g, middle, tail)
        tail = jnp.where(out_lane == 2 * heads + g, low, tail)
        result = acc / safe
        if g % 2 == 0:
            left = result
        if g % 2 == 1 or g == heads - 1:
            block = jnp.where(out_lane < HEAD_SIZE, left, result)
            out_ref[0, :, g // 2 * 128 : g // 2 * 128 + 128] = block.astype(out_ref.dtype)
    out_ref[0, :, out_ref.shape[2] - 128 :] = tail.astype(out_ref.dtype)


def attend(info, query, keys, values, fresh_key, fresh_value, rows, local_q):
    local_kv, pairs = keys.shape[1], keys.shape[2]
    group = local_q // local_kv
    per = FRESH_TOKENS // rows
    dests = query.shape[0] // rows
    cache_spec = pl.BlockSpec((1, local_kv, pairs, 128), lambda d, info: (d // per, 0, 0, 0))
    fresh_spec = pl.BlockSpec((local_kv, rows, 128), lambda d, info: (0, 0, 0))
    columns = (local_q + 1) // 2 * 128 + 128
    return pl.pallas_call(
        functools.partial(attend_kernel, group),
        grid_spec=pltpu.PrefetchScalarGridSpec(
            num_scalar_prefetch=1,
            grid=(dests,),
            in_specs=[
                pl.BlockSpec((rows, local_q * HEAD_SIZE), lambda d, info: (d, 0)),
                cache_spec,
                cache_spec,
                fresh_spec,
                fresh_spec,
            ],
            out_specs=pl.BlockSpec((1, rows, columns), lambda d, info: (d, 0, 0)),
            scratch_shapes=[pltpu.VMEM((local_q, rows, 128), jnp.float32)] * 3,
        ),
        out_shape=jax.ShapeDtypeStruct((dests, rows, columns), jnp.bfloat16),
        compiler_params=pltpu.CompilerParams(vmem_limit_bytes=40 * 1024 * 1024),
        cost_estimate=pl.CostEstimate(
            flops=8 * query.size * pairs * 2, bytes_accessed=16 << 20, transcendentals=query.size * pairs // 32
        ),
    )(info, query, keys, values, fresh_key, fresh_value)


def nearest(z, j):
    up = jnp.where(z == 1, jnp.where(j == 0, 1, jnp.where(j == 1, 0, j)), j)
    down = jnp.where(z == 2, jnp.where(j == 0, 2, jnp.where(j == 1, 3, 3 - j)), 3 - j)
    return jnp.where(z < 2, up, down)


def lanes_of(rows):
    return lax.broadcasted_iota(jnp.int32, (rows, 128), 1)


def unit_rows(count):
    return jnp.where(lax.broadcasted_iota(jnp.int32, (count, 128), 0) == lanes_of(count), 1.0, 0.0).astype(jnp.bfloat16)


def read_levels(packed, heads):
    split = lax.dot_general(packed, unit_rows(16), (((0,), (0,)), ((), ())), preferred_element_type=jnp.float32)
    return split + pltpu.roll(split, 128 - heads, 1)


def write_levels(level, heads):
    lane = lanes_of(level.shape[0])
    high = level.astype(jnp.bfloat16).astype(jnp.float32)
    low = level - high
    split = jnp.where(lane < heads, high, jnp.where(lane < 2 * heads, pltpu.roll(low, heads, 1), 0.0))
    nt = (((1,), (1,)), ((), ()))
    return lax.dot_general(unit_rows(16), split.astype(jnp.bfloat16), nt, preferred_element_type=jnp.float32)


def merge(pieces, heads):
    rows = pieces[0].shape[0] - 16
    lane = lanes_of(rows)
    levels = [read_levels(piece[rows:, :rows], heads) for piece in pieces]
    peak = functools.reduce(jnp.maximum, levels)
    weights = [jnp.exp(level - peak) for level in levels]
    total = functools.reduce(jnp.add, weights)
    weights = [weight / total for weight in weights]
    tiles = []
    for tile in range(heads // 2):
        mixed = None
        for piece, weight in zip(pieces, weights):
            factor = jnp.where(lane < 64, weight[:, 2 * tile : 2 * tile + 1], weight[:, 2 * tile + 1 : 2 * tile + 2])
            term = piece[:rows, tile * 128 : tile * 128 + 128].astype(jnp.float32) * factor
            mixed = term if mixed is None else mixed + term
        tiles.append(mixed)
    return tiles, peak + jnp.log(total)


def layer_kernel(
    lens_ref, tokens_ref, gains_ref, wq_ref, wk_ref, wv_ref, freqs_ref, ids_ref, k_ref, v_ref, w_out_ref, router_ref,
    down_ref, raw_ref,
    attn_ref, out_ref,
    queries, keys, values, mixed, level_tail, sent, held, peer_x, merged, peer_z, parting, half_sum, got_twin, got_across, joined,
    fresh_keys, fresh_values, raw, packed_ref, gate_up_ref, blocks, hidden, other_half, own_half, from_core, from_y, kept, passed, from_x, partial, from_z, final,
    sem_qz, sem_qx, got_q, sem_x, got_x, sem_z, got_z, sem_t, got_t, sem_w, got_w, sem_raw,
    sem_away, sem_side, sem_core, got_link, got_core, sem_lend, got_lend,
    sem_a, got_a, sem_b, got_b, sem_c, got_c, sem_d, got_d, sem_e, got_e,
):
    units = down_ref.shape[0]
    quarter = tokens_ref.shape[1] // 4
    rows, features = tokens_ref.shape[0], wq_ref.shape[0]
    heads = features // 64
    group = heads // k_ref.shape[1]
    pairs = k_ref.shape[2]
    width = tokens_ref.shape[1]
    half = width // 2
    s, t = lax.axis_index("seq"), lax.axis_index("tp")
    z, x = s // 2, s % 2
    y, c = t // 2, t % 2
    mesh_id = pl.DeviceIdType.MESH
    side = (z * 2 + 1 - x, t)
    across = (s, (1 - y) * 2 + c)
    twin = (s, y * 2 + 1 - c)
    mine = pl.ds(pl.multiple_of(c * half, 128), half)
    others = pl.ds(pl.multiple_of((1 - c) * half, 128), half)
    f32, bf16 = jnp.float32, jnp.bfloat16
    nt = (((1,), (1,)), ((), ()))

    barrier = pltpu.get_barrier_semaphore()
    for peer in (side, across, twin):
        pl.semaphore_signal(barrier, inc=1, device_id=peer, device_id_type=mesh_id)
    for step in range(1, 8):
        @pl.when((s + step) % 8 != s // 2 * 2 + 1 - x)
        def _():
            pl.semaphore_signal(barrier, inc=1, device_id=((s + step) % 8, t), device_id_type=mesh_id)

    def fetch(part):
        return pltpu.make_async_copy(
            raw_ref.at[:, :, :, pl.ds(part * 128, 128)], raw.at[part % 2], sem_raw.at[part % 2])

    fetch(0).start()
    fetch(1).start()
    normed = rms_norm(tokens_ref[...].astype(f32), gains_ref[0:1]).astype(bf16)
    quarter_lane = lanes_of(rows) % 64 < 32

    position = lens_ref[z] + x * rows + lax.broadcasted_iota(jnp.int32, (rows, 128), 0)
    angles = position.astype(f32) * freqs_ref[0:1, :]
    cosine = jnp.cos(angles)
    sine = jnp.where(quarter_lane, -jnp.sin(angles), jnp.sin(angles))

    def rotate(tile):
        partner = jnp.where(quarter_lane, pltpu.roll(tile, 96, 1), pltpu.roll(tile, 32, 1))
        return (tile * cosine + partner * sine).astype(bf16)

    projected = lax.dot_general(normed, wq_ref[...], nt, preferred_element_type=f32)
    for tile in range(features // 128):
        queries[s, :rows, tile * 128 : tile * 128 + 128] = rotate(projected[:, tile * 128 : tile * 128 + 128])
    queries[s, rows:, :rows] = ids_ref[...]
    pl.semaphore_wait(barrier, 9)

    def weight_copy(n):
        to = (s + 1 + n % 7) % 8
        cut = n // 7
        depth = packed_ref.shape[1]
        part = depth // 4
        source = pl.ds(pl.multiple_of(cut * part, 16), part)
        target = pl.ds(pl.multiple_of(s * depth + cut * part, 16), part)
        return pltpu.make_async_remote_copy(
            packed_ref.at[to, source], gate_up_ref.at[target], sem_w.at[n], got_w.at[s, cut],
            device_id=(to, t), device_id_type=mesh_id)

    def arrived_w(origin, cut):
        part = packed_ref.shape[1] // 4
        target = pl.ds(pl.multiple_of(origin * packed_ref.shape[1] + cut * part, 16), part)
        return pltpu.make_async_remote_copy(
            packed_ref.at[0, :part], gate_up_ref.at[target], sem_w.at[0], got_w.at[origin, cut],
            device_id=side, device_id_type=mesh_id)

    def pump(first, count):
        for n in range(count):
            weight_copy(first + n).start()

    def query_z(r, direction):
        b = r * 2 + x
        return pltpu.make_async_remote_copy(
            queries.at[b], queries.at[b], sem_qz.at[r, (direction + 1) // 2], got_q.at[b],
            device_id=((z + direction) * 2 + x, t), device_id_type=mesh_id)

    def query_x(r):
        b = r * 2 + x
        return pltpu.make_async_remote_copy(
            queries.at[b], queries.at[b], sem_qx.at[r], got_q.at[b], device_id=side, device_id_type=mesh_id)

    def arrived_q(b):
        return pltpu.make_async_remote_copy(
            queries.at[b], queries.at[b], sem_qx.at[0], got_q.at[b], device_id=side, device_id_type=mesh_id)

    def part_x(i):
        return pltpu.make_async_remote_copy(
            sent.at[i], peer_x.at[i], sem_x.at[i], got_x.at[i], device_id=side, device_id_type=mesh_id)

    def part_z(i):
        return pltpu.make_async_remote_copy(
            merged.at[i], peer_z.at[z], sem_z.at[i], got_z.at[z],
            device_id=(nearest(z, i + 1) * 2 + x, t), device_id_type=mesh_id)

    def arrived_z(z_from):
        return pltpu.make_async_remote_copy(
            merged.at[0], peer_z.at[z_from], sem_z.at[0], got_z.at[z_from], device_id=side, device_id_type=mesh_id)

    for direction in (-1, 1):
        @pl.when((z + direction >= 0) & (z + direction < 4))
        def _():
            query_z(z, direction).start()
    query_x(z).start()

    at_start, at_head, at_tp, at_gather = WEIGHT_PLAN
    after_heads = at_start + 12 * at_head
    after_tp = after_heads + 4 * at_tp
    base = s * (2 * pairs)
    row_lane = lanes_of(rows)
    fresh_keys[...] = rotate(lax.dot_general(normed, wk_ref[...], nt, preferred_element_type=f32))
    fresh_values[...] = lax.dot_general(normed, wv_ref[...], nt, preferred_element_type=f32).astype(bf16)
    low = lanes_of(raw_ref.shape[2]) < 64
    for part in range(4):
        fetch(part).wait()
        for pair in range(raw_ref.shape[0] // 2):
            for which in range(2):
                one = raw[part % 2, 2 * pair, which].astype(f32)
                two = raw[part % 2, 2 * pair + 1, which].astype(f32)
                at = pl.ds(pair * 256 + which * 128, 128)
                packed_ref[2 * part, :, at] = jnp.where(low, one, pltpu.roll(two, 64, 1)).astype(bf16)
                packed_ref[2 * part + 1, :, at] = jnp.where(low, pltpu.roll(one, 64, 1), two).astype(bf16)
        if part < 2:
            fetch(part + 2).start()
    gate_up_ref[pl.ds(pl.multiple_of(s * packed_ref.shape[1], 16), packed_ref.shape[1]), :] = packed_ref[s]
    pump(0, at_start)

    def spread(block, fill, scale):
        plain = block.astype(f32)
        if scale != 1.0:
            plain = plain * scale
        turned = pltpu.roll(plain, 64, 1)
        keep = lanes_of(block.shape[0]) < 64
        return (
            (jnp.where(keep, plain, fill).astype(bf16), jnp.where(keep, turned, fill).astype(bf16)),
            (jnp.where(keep, fill, turned).astype(bf16), jnp.where(keep, fill, plain).astype(bf16)),
        )

    def attend(r, fresh, between, pumped):
        length = lens_ref[r]
        slot = lax.broadcasted_iota(jnp.int32, (1, 2 * pairs), 1)
        position = base + 2 * (slot % pairs) + slot // pairs
        bias = jnp.where(position < length, 0.0, NEGATIVE)
        for j in range(heads // group):
            if j == 1:
                between()
            key_two = spread(k_ref[r, j], 0.0, 0.125)
            value_two = spread(v_ref[r, j], 1.0, 1.0)
            for parity in range(2):
                keys[parity, :pairs] = key_two[parity][0]
                keys[parity, pairs : 2 * pairs] = key_two[parity][1]
                values[parity, :pairs] = value_two[parity][0]
                values[parity, pairs : 2 * pairs] = value_two[parity][1]
            if fresh:
                new_keys = spread(fresh_keys[...], 0.0, 0.125)
                new_values = spread(fresh_values[...], 1.0, 1.0)
            for g in range(j * group, (j + 1) * group):
                parity = g % 2
                for part in range(2):
                    query = queries[r * 2 + part, :rows, g // 2 * 128 : g // 2 * 128 + 128]
                    score = lax.dot_general(query, keys[parity], nt, preferred_element_type=f32) + bias
                    peak = jnp.max(score, axis=1, keepdims=True)
                    if fresh:
                        new_key = new_keys[parity][j]
                        new_value = new_values[parity][j]
                        row_q = part * rows + lax.broadcasted_iota(jnp.int32, (rows, rows), 0)
                        row_k = x * rows + lax.broadcasted_iota(jnp.int32, (rows, rows), 1)
                        new_score = lax.dot_general(query, new_key, nt, preferred_element_type=f32)
                        new_score = new_score + jnp.where(row_k <= row_q, 0.0, NEGATIVE)
                        peak = jnp.maximum(peak, jnp.max(new_score, axis=1, keepdims=True))
                    weight = jnp.exp(score - peak).astype(bf16)
                    total = jnp.dot(weight, values[parity], preferred_element_type=f32)
                    if fresh:
                        weight = jnp.exp(new_score - peak).astype(bf16)
                        total = total + jnp.dot(weight, new_value, preferred_element_type=f32)
                    turned = pltpu.roll(total, 64, 1)
                    if parity == 0:
                        sums = jnp.where(row_lane < 64, turned, total)
                    else:
                        sums = jnp.where(row_lane < 64, total, turned)
                    level = peak + jnp.log(sums)
                    result = total / sums
                    at = pl.ds(part * rows, rows)
                    if g == 0:
                        level_tail[at, :] = level
                    else:
                        level_tail[at, :] = jnp.where(row_lane == g, level, level_tail[at, :])
                    tile = pl.ds(g // 2 * 128, 128)
                    if parity == 0:
                        mixed[at, tile] = result
                    else:
                        mixed[at, tile] = jnp.where(row_lane < 64, mixed[at, tile], result)
                if parity == 1:
                    pump(at_start + (pumped + g // 2) * at_head, at_head)

    def hand_over(i):
        own = pl.ds(pl.multiple_of(x * rows, rows), rows)
        away = pl.ds(pl.multiple_of((1 - x) * rows, rows), rows)
        sent[i, :rows, :] = mixed[away, :].astype(bf16)
        sent[i, rows:, :rows] = write_levels(level_tail[away, :], heads).astype(bf16)
        part_x(i).start()
        held[i, :rows, :] = mixed[own, :].astype(bf16)
        held[i, rows:, :rows] = write_levels(level_tail[own, :], heads).astype(bf16)

    def merge_x(i):
        part_x(i).wait_recv()
        tiles, level = merge([held[i], peer_x[i]], heads)
        for n, tile in enumerate(tiles):
            merged[i, :rows, n * 128 : n * 128 + 128] = tile.astype(bf16)
        merged[i, rows:, :rows] = write_levels(level, heads).astype(bf16)

    def forward(i):
        r = nearest(z, i + 1)
        arrived_q(r * 2 + x).wait_recv()
        for direction in (-1, 1):
            @pl.when(((z - r) * direction > 0) & (z + direction >= 0) & (z + direction < 4))
            def _():
                query_z(r, direction).start()
        query_x(r).start()

    forward(0)
    forward(1)

    def step(i, carry):
        r = nearest(z, i + 1)
        arrived_q(r * 2 + 1 - x).wait_recv()

        def between():
            @pl.when(i == 0)
            def _():
                forward(2)

        attend(r, False, between, 3 * i)
        hand_over(i)

        @pl.when(i > 0)
        def _():
            merge_x(i - 1)
            part_z(i - 1).start()
        return carry

    lax.fori_loop(0, 3, step, 0)
    arrived_q(z * 2 + 1 - x).wait_recv()

    def between():
        merge_x(2)
        part_z(2).start()

    attend(z, True, between, 9)
    hand_over(3)
    merge_x(3)
    pieces = [merged[3]]
    for step_z in range(1, 4):
        z_from = (z + step_z) % 4
        arrived_z(z_from).wait_recv()
        pieces.append(peer_z[z_from])
    tiles, _ = merge(pieces, heads)
    heads_out = jnp.concatenate([tile.astype(bf16) for tile in tiles], axis=1)

    def exchange(n, source, target, to):
        return pltpu.make_async_remote_copy(
            source, target, sem_t.at[n], got_t.at[n], device_id=to, device_id_type=mesh_id)

    parting[...] = jnp.dot(heads_out, w_out_ref[:, others], preferred_element_type=f32).astype(bf16)
    first = exchange(0, parting, got_twin, twin)
    first.start()
    pump(after_heads + 0 * at_tp, at_tp)
    own = jnp.dot(heads_out, w_out_ref[:, mine], preferred_element_type=f32)
    first.wait_recv()
    half_sum[...] = (own + got_twin[...].astype(f32)).astype(bf16)
    second = exchange(1, half_sum, got_across, across)
    second.start()
    pump(after_heads + 1 * at_tp, at_tp)
    pump(after_heads + 2 * at_tp, at_tp)
    second.wait_recv()
    joined[:, mine] = (half_sum[...].astype(f32) + got_across[...].astype(f32)).astype(bf16)
    last = exchange(2, joined.at[:, mine], joined.at[:, mine], twin)
    last.start()
    pump(after_heads + 3 * at_tp, at_tp)
    last.wait_recv()
    attn_ref[...] = joined[...]
    stream = tokens_ref[...].astype(f32) + joined[...].astype(f32)
    normed = rms_norm(stream, gains_ref[1:2])
    blocks[s] = normed.astype(bf16)

    third = half // 3
    duty = pl.ds(pl.multiple_of(c * half + y * third, 128), 2 * third)
    lent = pl.ds(pl.multiple_of(c * half + y * 2 * third, 128), third)
    borrowed = pl.ds(pl.multiple_of(c * half + (1 - y) * 2 * third, 128), third)

    def away(b, direction):
        return pltpu.make_async_remote_copy(
            blocks.at[b, :, duty], blocks.at[b, :, duty], sem_away.at[b, (direction + 1) // 2], got_link.at[b],
            device_id=((z + direction) * 2 + x, t), device_id_type=mesh_id)

    def sideways(b):
        return pltpu.make_async_remote_copy(
            blocks.at[b, :, duty], blocks.at[b, :, duty], sem_side.at[b], got_link.at[b],
            device_id=side, device_id_type=mesh_id)

    def lend(b):
        return pltpu.make_async_remote_copy(
            blocks.at[b, :, lent], blocks.at[b, :, lent], sem_lend.at[b], got_lend.at[b],
            device_id=across, device_id_type=mesh_id)

    def borrow(b):
        return pltpu.make_async_remote_copy(
            blocks.at[b, :, borrowed], blocks.at[b, :, borrowed], sem_lend.at[b], got_lend.at[b],
            device_id=across, device_id_type=mesh_id)

    def to_twin(b):
        return pltpu.make_async_remote_copy(
            blocks.at[b, :, mine], blocks.at[b, :, mine], sem_core.at[b], got_core.at[b],
            device_id=twin, device_id_type=mesh_id)

    def copy_a(i):
        return pltpu.make_async_remote_copy(
            other_half.at[i], from_core.at[i], sem_a.at[i], got_a.at[i], device_id=twin, device_id_type=mesh_id)

    def copy_b(i):
        cut = pl.ds(pl.multiple_of((1 - y) * quarter, 128), quarter)
        return pltpu.make_async_remote_copy(
            own_half.at[i, :, cut], from_y.at[i], sem_b.at[i], got_b.at[i], device_id=across, device_id_type=mesh_id)

    def copy_c(j):
        return pltpu.make_async_remote_copy(
            passed.at[j], from_x.at[j], sem_c.at[j], got_c.at[j], device_id=side, device_id_type=mesh_id)

    def copy_d(j):
        return pltpu.make_async_remote_copy(
            partial.at[j], from_z.at[z], sem_d.at[j], got_d.at[z],
            device_id=(nearest(z, 3 - j) * 2 + x, t), device_id_type=mesh_id)

    def arrive_d(z_from):
        return pltpu.make_async_remote_copy(
            partial.at[0], from_z.at[z_from], sem_d.at[0], got_d.at[z_from],
            device_id=side, device_id_type=mesh_id)

    for direction in (-1, 1):
        @pl.when((z + direction >= 0) & (z + direction < 4))
        def _():
            away(s, direction).start()
    sideways(s).start()

    def block_of(i):
        k = i % 2
        return nearest(z, i // 2) * 2 + jnp.where(k == 0, x, 1 - x)


    def take_z(j):
        b = nearest(z, j) * 2 + x
        sideways(b).wait_recv()
        for direction in (-1, 1):
            @pl.when(((z - nearest(z, j)) * direction > 0) & (z + direction >= 0) & (z + direction < 4))
            def _():
                away(b, direction).start()
        sideways(b).start()
        lend(b).start()

    def take_x(j):
        b = nearest(z, j) * 2 + 1 - x
        sideways(b).wait_recv()
        lend(b).start()

    def finish(b):
        borrow(b).wait_recv()
        to_twin(b).start()

    for j in range(4):
        pump(after_tp + j * at_gather, at_gather)
        if j < 3:
            take_z(j + 1)
        if j > 0:
            finish(nearest(z, j) * 2 + x)
            finish(nearest(z, j - 1) * 2 + 1 - x)
        take_x(j)
    finish(nearest(z, 3) * 2 + 1 - x)
    pump(after_tp + 4 * at_gather, 28 - after_tp - 4 * at_gather)
    for n in range(28):
        weight_copy(n).wait_send()
    for step_s in range(1, 8):
        for cut in range(4):
            arrived_w((s + step_s) % 8, cut).wait_recv()

    expert_of = lanes_of(rows).astype(f32)
    as_columns = jnp.where(lax.broadcasted_iota(jnp.int32, ((queries.shape[1] - rows), 128), 0) == lanes_of((queries.shape[1] - rows)), 1.0, 0.0).astype(jnp.bfloat16)
    expert_lane = lax.broadcasted_iota(jnp.int32, (128, units), 0)
    expert_unit = lax.broadcasted_iota(jnp.int32, (128, units), 1)

    def compute(i, carry):
        @pl.when(i < 8)
        def _():
            b = nearest(z, 3 - i // 2) * 2 + jnp.where(i % 2 == 0, 1 - x, x)

            @pl.when(i < 7)
            def _():
                to_twin(b).wait_recv()

            tokens = blocks[b]
            logits = jnp.dot(tokens, router_ref[...], preferred_element_type=f32)
            named = lax.dot_general(queries[b, rows:, :rows], as_columns, (((0,), (0,)), ((), ())), preferred_element_type=f32)
            chosen = named[:, 0:1] == expert_of
            for k in range(1, 8):
                chosen = chosen | (named[:, k : k + 1] == expert_of)
            logits = jnp.where(chosen, logits, NEGATIVE)
            gates = jnp.where(chosen, jnp.exp(logits - jnp.max(logits, axis=1, keepdims=True)), 0.0)
            share = gates / jnp.sum(gates, axis=1, keepdims=True)
            high = share.astype(jnp.bfloat16)
            low = (share - high.astype(f32)).astype(jnp.bfloat16)
            spread = jnp.where(expert_lane == t * (units // 64) + expert_unit // 64, 1.0, 0.0).astype(jnp.bfloat16)
            shares = jnp.dot(high, spread, preferred_element_type=f32) + jnp.dot(low, spread, preferred_element_type=f32)
            for p in range(units // 128):
                both = jnp.dot(tokens, gate_up_ref[:, p * 256 : p * 256 + 256], preferred_element_type=f32)
                gate, up = both[:, :128], both[:, 128:]
                value = gate / (1.0 + jnp.exp(-gate)) * up * shares[:, p * 128 : p * 128 + 128]
                hidden[:, p * 128 : p * 128 + 128] = value.astype(jnp.bfloat16)
            other_half[i] = jnp.dot(hidden[...], down_ref[:, others], preferred_element_type=f32).astype(jnp.bfloat16)
            copy_a(i).start()
            own_half[i] = jnp.dot(hidden[...], down_ref[:, mine], preferred_element_type=f32).astype(jnp.bfloat16)

        @pl.when((i >= 1) & (i < 9))
        def _():
            n = i - 1
            copy_a(n).wait_recv()
            own_half[n] = (own_half[n].astype(f32) + from_core[n].astype(f32)).astype(jnp.bfloat16)
            copy_b(n).start()

        @pl.when((i >= 4) & (i < 12))
        def _():
            n = i - 4
            copy_b(n).wait_recv()
            cut = pl.ds(pl.multiple_of(y * quarter, 128), quarter)
            total = (own_half[n, :, cut].astype(f32) + from_y[n].astype(f32)).astype(jnp.bfloat16)

            @pl.when(n % 2 == 1)
            def _():
                kept[n // 2] = total

            @pl.when(n % 2 == 0)
            def _():
                passed[n // 2] = total
                copy_c(n // 2).start()

        @pl.when((i >= 6) & (i % 2 == 0))
        def _():
            j = i // 2 - 3
            copy_c(j).wait_recv()
            partial[j] = (kept[j].astype(f32) + from_x[j].astype(f32)).astype(jnp.bfloat16)

            @pl.when(j < 3)
            def _():
                copy_d(j).start()
        return carry

    lax.fori_loop(0, 13, compute, 0)

    total = partial[3].astype(f32)
    for step_z in range(1, 4):
        z_from = (z + step_z) % 4
        arrive_d(z_from).wait_recv()
        total = total + from_z[z_from].astype(f32)

    def copy_e(n, to):
        at = c * half + y * quarter if n == 0 else c * half
        size = quarter if n == 0 else half
        cut = pl.ds(pl.multiple_of(at, 128), size)
        return pltpu.make_async_remote_copy(
            final.at[:, cut], final.at[:, cut], sem_e.at[n], got_e.at[n], device_id=to, device_id_type=mesh_id)

    final[:, pl.ds(pl.multiple_of(c * half + y * quarter, 128), quarter)] = total.astype(jnp.bfloat16)
    copy_e(0, across).start()
    copy_e(0, across).wait_recv()
    copy_e(1, twin).start()
    copy_e(1, twin).wait_recv()
    out_ref[...] = final[...]

    def drain(i, carry):
        b = block_of(i)
        zj = nearest(z, i // 2)

        @pl.when(i > 0)
        def _():
            to_twin(b).wait_send()
            lend(b).wait_send()

        @pl.when(i % 2 == 0)
        def _():
            sideways(b).wait_send()
            for direction in (-1, 1):
                @pl.when(((z - zj) * direction >= 0) & (z + direction >= 0) & (z + direction < 4))
                def _():
                    away(b, direction).wait_send()
            copy_c(i // 2).wait_send()

            @pl.when(i < 6)
            def _():
                copy_d(i // 2).wait_send()

        copy_a(i).wait_send()
        copy_b(i).wait_send()
        return carry

    lax.fori_loop(0, 8, drain, 0)
    copy_e(0, across).wait_send()
    copy_e(1, twin).wait_send()
    for j in range(4):
        query_x(nearest(z, j)).wait_send()
        part_x(j).wait_send()
        for direction in (-1, 1):
            @pl.when(((z - nearest(z, j)) * direction >= 0) & (z + direction >= 0) & (z + direction < 4))
            def _():
                query_z(nearest(z, j), direction).wait_send()
    for j in range(3):
        part_z(j).wait_send()
    first.wait_send()
    second.wait_send()
    last.wait_send()


def layer(lens, tokens, gains, w_query, w_key, w_value, freqs, ids, keys, values, w_out, router, down, gate_up):
    features = w_query.shape[0]
    rows, width = tokens.shape
    extra = ids.shape[0]
    requests, local_kv, pairs, _ = keys.shape
    units = down.shape[0]
    half, quarter = width // 2, width // 4
    bf16, f32 = jnp.bfloat16, jnp.float32
    dma = pltpu.SemaphoreType.DMA
    vmem = pl.BlockSpec(memory_space=pltpu.VMEM)
    scores = requests * FRESH_TOKENS * (features // 64) * 2 * pairs
    return pl.pallas_call(
        layer_kernel,
        out_shape=[jax.ShapeDtypeStruct((rows, width), bf16)] * 2,
        in_specs=[pl.BlockSpec(memory_space=pltpu.SMEM)] + [vmem] * 12 + [pl.BlockSpec(memory_space=pl.ANY)],
        out_specs=[vmem] * 2,
        scratch_shapes=[
            pltpu.VMEM((8, rows + extra, features), bf16),
            pltpu.VMEM((2, 2 * pairs, 128), bf16),
            pltpu.VMEM((2, 2 * pairs, 128), bf16),
            pltpu.VMEM((2 * rows, features), f32),
            pltpu.VMEM((2 * rows, 128), f32),
            pltpu.VMEM((4, rows + 16, features), bf16),
            pltpu.VMEM((4, rows + 16, features), bf16),
            pltpu.VMEM((4, rows + 16, features), bf16),
            pltpu.VMEM((4, rows + 16, features), bf16),
            pltpu.VMEM((4, rows + 16, features), bf16),
            pltpu.VMEM((rows, width // 2), bf16),
            pltpu.VMEM((rows, width // 2), bf16),
            pltpu.VMEM((rows, width // 2), bf16),
            pltpu.VMEM((rows, width // 2), bf16),
            pltpu.VMEM((rows, width), bf16),
            pltpu.VMEM((rows, 128), bf16),
            pltpu.VMEM((rows, 128), bf16),
            pltpu.VMEM((2,) + gate_up.shape[:3] + (128,), bf16),
            pltpu.VMEM((8, gate_up.shape[2], 2 * units), bf16),
            pltpu.VMEM((width, 2 * units), bf16),
            pltpu.VMEM((8, rows, width), bf16),
            pltpu.VMEM((rows, units), bf16),
            pltpu.VMEM((8, rows, half), bf16),
            pltpu.VMEM((8, rows, half), bf16),
            pltpu.VMEM((8, rows, half), bf16),
            pltpu.VMEM((8, rows, quarter), bf16),
            pltpu.VMEM((4, rows, quarter), bf16),
            pltpu.VMEM((4, rows, quarter), bf16),
            pltpu.VMEM((4, rows, quarter), bf16),
            pltpu.VMEM((4, rows, quarter), bf16),
            pltpu.VMEM((4, rows, quarter), bf16),
            pltpu.VMEM((rows, width), bf16),
            dma((4, 2)), dma((4,)), dma((8,)), dma((4,)), dma((4,)), dma((4,)), dma((4,)), dma((3,)), dma((3,)), dma((28,)), dma((8, 4)), dma((2,)),
            dma((8, 2)), dma((8,)), dma((8,)), dma((8,)), dma((8,)), dma((8,)), dma((8,)),
            dma((8,)), dma((8,)), dma((8,)), dma((8,)), dma((4,)), dma((4,)), dma((4,)), dma((4,)), dma((2,)), dma((2,)),
        ],
        compiler_params=pltpu.CompilerParams(
            collective_id=0, has_side_effects=True, vmem_limit_bytes=60 * 1024 * 1024
        ),
        cost_estimate=pl.CostEstimate(flops=64 * 4 * scores, bytes_accessed=16 << 20, transcendentals=scores),
    )(lens, tokens, gains, w_query, w_key, w_value, freqs, ids, keys, values, w_out, router, down, gate_up)


def swap_cores(values):
    count = lax.axis_size("tp")
    return lax.ppermute(values, "tp", [(i, i ^ 1) for i in range(count)])


def sum_halves(mine, others):
    received = swap_cores(others.astype(jnp.bfloat16)).astype(jnp.float32)
    return (mine + received).astype(jnp.bfloat16)


def sum_chips(values):
    count = lax.axis_size("tp")
    step = 2
    total = values.astype(jnp.float32)
    while step < count:
        sent = total.astype(jnp.bfloat16)
        received = lax.ppermute(sent, "tp", [(i, i ^ step) for i in range(count)])
        total = sent.astype(jnp.float32) + received.astype(jnp.float32)
        step = step * 2
    return total.astype(jnp.bfloat16)


def join_halves(values, core):
    other = swap_cores(values)
    first = jnp.where(core == 0, values, other)
    second = jnp.where(core == 0, other, values)
    return jnp.concatenate([first, second], axis=1)


def per_device(
    tokens,
    norm1_gain,
    w_query,
    key_weight,
    value_weight,
    rotated_key_cache,
    stored_value_cache,
    cache_len,
    w_out,
    norm2_gain,
    w_router,
    expert_ids,
    w_gate_up,
    w_down,
):
    tok_rows, width = tokens.shape
    seq_pos = lax.axis_index("seq")
    tp_pos = lax.axis_index("tp")
    local_q = w_query.shape[0] // HEAD_SIZE
    local_kv = key_weight.shape[0] // HEAD_SIZE
    requests = rotated_key_cache.shape[0]
    span = rotated_key_cache.shape[2] // HEAD_SIZE
    inputs = tokens.astype(jnp.float32)
    devices = lax.axis_size("seq")
    local_experts, _, own_width, hidden_size = w_gate_up.shape
    own_hidden = hidden_size // devices
    normalized_input = rms_norm(inputs, norm1_gain).astype(jnp.bfloat16)
    row_ids = seq_pos * tok_rows + jnp.arange(tok_rows, dtype=jnp.int32)
    owners = row_ids // FRESH_TOKENS
    positions = lookup(cache_len, owners) + row_ids % FRESH_TOKENS
    angle_position = positions.astype(jnp.float32)
    query_vector = apply_rotary(
        apply_projection(normalized_input, w_query).reshape(tok_rows, local_q, HEAD_SIZE),
        angle_position,
    ).astype(jnp.bfloat16)
    units = local_experts * own_hidden
    by_owner = jnp.transpose(
        w_gate_up.reshape(local_experts, 2, own_width, devices, own_hidden), (3, 2, 1, 0, 4)
    ).reshape(width, 2 * units)
    fresh_key = apply_rotary(
        apply_projection(normalized_input, key_weight).reshape(tok_rows, local_kv, HEAD_SIZE),
        angle_position,
    ).astype(jnp.bfloat16)
    fresh_value = (
        apply_projection(normalized_input, value_weight)
        .astype(jnp.bfloat16)
        .reshape(tok_rows, local_kv, HEAD_SIZE)
    )
    all_query = lax.all_gather(
        query_vector.reshape(tok_rows, local_q * HEAD_SIZE), "seq", axis=0, tiled=True
    )
    all_query, by_owner = lax.optimization_barrier((all_query, by_owner))
    own_gate_up = lax.all_to_all(by_owner, "seq", 0, 0, tiled=True)
    paired = (requests, local_kv, span // 2, 2 * HEAD_SIZE)
    pad = ((0, 0), (0, 0), (0, HEAD_SIZE))
    parts = attend(
        jnp.concatenate([seq_pos[None].astype(jnp.int32), cache_len]),
        all_query,
        rotated_key_cache.reshape(paired),
        stored_value_cache.reshape(paired),
        jnp.pad(jnp.transpose(fresh_key, (1, 0, 2)), pad),
        jnp.pad(jnp.transpose(fresh_value, (1, 0, 2)), pad),
        tok_rows,
        local_q,
    )
    parts, own_gate_up = lax.optimization_barrier((parts, own_gate_up))
    parts = lax.all_to_all(parts, "seq", 0, 0, tiled=True)
    parts = parts.astype(jnp.float32)
    features = local_q * HEAD_SIZE
    tails = parts.shape[2] - 128
    pieces = parts[:, :, tails : tails + 3 * local_q]
    level = pieces[..., :local_q] + pieces[..., local_q : 2 * local_q] + pieces[..., 2 * local_q :]
    factor = jnp.exp(level - jnp.max(level, axis=0, keepdims=True))
    factor = factor / jnp.sum(factor, axis=0, keepdims=True)
    feature_head = jnp.arange(features, dtype=jnp.int32) // HEAD_SIZE
    widen = (jnp.arange(local_q, dtype=jnp.int32)[:, None] == feature_head[None, :]).astype(jnp.float32)
    factor = jnp.einsum("sth,hf->stf", factor, widen, precision=lax.Precision.HIGHEST)
    heads_out = jnp.sum(parts[:, :, :features] * factor, axis=0).astype(jnp.bfloat16)
    attn_part = jnp.dot(heads_out, w_out, preferred_element_type=jnp.float32)
    core = tp_pos % 2
    half = width // 2
    attn = sum_halves(
        lax.dynamic_slice_in_dim(attn_part, core * half, half, 1),
        lax.dynamic_slice_in_dim(attn_part, (1 - core) * half, half, 1),
    )
    attn = join_halves(sum_chips(attn), core).astype(jnp.float32)
    attn_out = attn.astype(jnp.bfloat16)
    normed2 = rms_norm(inputs + attn, norm2_gain).astype(jnp.bfloat16)
    logits = jnp.dot(normed2, w_router, preferred_element_type=jnp.float32)
    experts_all = w_router.shape[1]
    picked_all = expert_ids[:, :, None] == jnp.arange(experts_all, dtype=jnp.int32)[None, None, :]
    chosen = jnp.sum(jnp.where(picked_all, logits[:, None, :], 0.0), axis=-1)
    gates = jax.nn.softmax(chosen, axis=-1)
    local_ids = tp_pos * local_experts + jnp.arange(local_experts, dtype=jnp.int32)
    picked = expert_ids[:, :, None] == local_ids[None, None, :]
    share = jnp.sum(jnp.where(picked, gates[:, :, None], 0.0), axis=1)
    share_high = lax.reduce_precision(share, 8, 7)
    packed = jnp.concatenate(
        [
            lax.dynamic_slice_in_dim(normed2, core * half, half, 1),
            share_high.astype(jnp.bfloat16),
            (share - share_high).astype(jnp.bfloat16),
            jnp.zeros((tok_rows, 128 - 2 * local_experts), jnp.bfloat16),
        ],
        axis=1,
    )
    packed = lax.all_gather(packed, "seq", axis=0, tiled=True)
    others = swap_cores(packed[:, :half])
    unit_expert = jnp.arange(units, dtype=jnp.int32) // own_hidden
    lanes = jnp.arange(128, dtype=jnp.int32)
    spread = (lanes[:, None] % local_experts == unit_expert[None, :]) & (lanes[:, None] < 2 * local_experts)
    share_all = jnp.dot(packed[:, half:], spread.astype(jnp.bfloat16), preferred_element_type=jnp.float32)
    gate_up_mine = lax.dynamic_slice_in_dim(own_gate_up, core * half, half, 0)
    gate_up_others = lax.dynamic_slice_in_dim(own_gate_up, (1 - core) * half, half, 0)
    both = jnp.dot(packed[:, :half], gate_up_mine, preferred_element_type=jnp.float32)
    both = both + jnp.dot(others, gate_up_others, preferred_element_type=jnp.float32)
    hidden = (jax.nn.silu(both[:, :units]) * both[:, units:] * share_all).astype(jnp.bfloat16)
    down = w_down.reshape(units, width)
    down_mine = lax.dynamic_slice_in_dim(down, core * half, half, 1)
    down_others = lax.dynamic_slice_in_dim(down, (1 - core) * half, half, 1)
    moe_half = sum_halves(
        jnp.dot(hidden, down_mine, preferred_element_type=jnp.float32),
        jnp.dot(hidden, down_others, preferred_element_type=jnp.float32),
    )
    moe_half = lax.psum_scatter(moe_half, "seq", scatter_dimension=0, tiled=True)
    expert_out = join_halves(sum_chips(moe_half.astype(jnp.float32)), core)
    return (attn_out, expert_out)


def per_device_block(
    tokens,
    norm1_gain,
    w_query,
    key_weight,
    value_weight,
    rotated_key_cache,
    stored_value_cache,
    cache_len,
    w_out,
    norm2_gain,
    w_router,
    expert_ids,
    w_gate_up,
    w_down,
):
    tok_rows, width = tokens.shape
    local_kv = key_weight.shape[0] // HEAD_SIZE
    requests = rotated_key_cache.shape[0]
    span = rotated_key_cache.shape[2] // HEAD_SIZE
    devices = lax.axis_size("seq")
    units = w_gate_up.shape[0] * (w_gate_up.shape[3] // devices)
    lane = jnp.arange(128, dtype=jnp.int32)
    freqs = THETA ** (-((lane % 32).astype(jnp.float32) * (2.0 / HEAD_SIZE)))
    paired = (requests, local_kv, span // 2, 2 * HEAD_SIZE)
    return layer(
        cache_len,
        tokens,
        jnp.stack([norm1_gain, norm2_gain]),
        w_query,
        key_weight,
        value_weight,
        jnp.broadcast_to(freqs[None, :], (8, 128)),
        jnp.pad(expert_ids.T.astype(jnp.bfloat16), ((0, 8), (0, 0))),
        rotated_key_cache.reshape(paired),
        stored_value_cache.reshape(paired),
        w_out,
        jnp.pad(w_router, ((0, 0), (0, 128 - w_router.shape[1]))),
        w_down.reshape(units, width),
        w_gate_up,
    )


def solution(mesh):
    block = mesh.shape["seq"] == 8 and mesh.shape["tp"] == 4
    return jax.shard_map(
        per_device_block if block else per_device,
        mesh=mesh,
        in_specs=(
            P("seq", None),
            P(),
            P("tp", None),
            P("tp", None),
            P("tp", None),
            P(None, "tp", "seq"),
            P(None, "tp", "seq"),
            P(),
            P("tp", None),
            P(),
            P(),
            P("seq", None),
            P("tp", None, "seq", None),
            P("tp", "seq", None),
        ),
        out_specs=(P("seq", None), P("seq", None)),
        check_vma=False,
    )
```

```python
import functools

import jax
import jax.numpy as jnp
from jax import lax
from jax.experimental import pallas as pl
from jax.experimental.pallas import tpu as pltpu
from jax.sharding import PartitionSpec as P

HEAD_SIZE = 64
FRESH_TOKENS = 512


EPS = 1e-05
THETA = 10000.0
NEGATIVE = -1e30
WEIGHT_PLAN = (0, 1, 1, 3)


def rms_norm(values, gain):
    mean_square = jnp.mean(values * values, axis=-1, keepdims=True)
    return values * lax.rsqrt(mean_square + EPS) * gain.astype(values.dtype)


def apply_rotary(values, positions):
    half_dim = values.shape[-1] // 2
    exponent = jnp.arange(half_dim, dtype=jnp.float32) * (2.0 / values.shape[-1])
    freqs = THETA ** (-exponent)
    angles = positions[:, None] * freqs[None, :]
    cosine = jnp.cos(angles)[:, None, :]
    sine = jnp.sin(angles)[:, None, :]
    first = values[..., :half_dim]
    second = values[..., half_dim:]
    return jnp.concatenate(
        [first * cosine - second * sine, second * cosine + first * sine], axis=-1
    )


def apply_projection(normalized_input, weight):
    return jnp.einsum("td,fd->tf", normalized_input, weight, preferred_element_type=jnp.float32)


def lookup(table, index):
    hits = index[:, None] == jnp.arange(table.shape[0], dtype=jnp.int32)[None, :]
    return jnp.sum(jnp.where(hits, table[None, :], 0), axis=1)


def attend_kernel(group, info, q_ref, k_ref, v_ref, fk_ref, fv_ref, out_ref, peak_ref, sum_ref, acc_ref):
    heads, rows = acc_ref.shape[0], acc_ref.shape[1]
    pairs = k_ref.shape[2]
    columns = q_ref.shape[1]
    dest = pl.program_id(0)
    me = info[0]
    per = FRESH_TOKENS // rows
    length = info[1 + dest // per]
    base = me * (2 * pairs)
    col = lax.broadcasted_iota(jnp.int32, (columns, 128), 0)
    lane = lax.broadcasted_iota(jnp.int32, (columns, 128), 1)
    out_lane = lax.broadcasted_iota(jnp.int32, (rows, 128), 1)
    has_cache = base < length
    has_fresh = (dest // per == me // per) & (dest >= me)
    nt = (((1,), (1,)), ((), ()))

    def pick(g, odd):
        hit = (col == g * HEAD_SIZE + lane - odd * HEAD_SIZE) & (lane // HEAD_SIZE == odd)
        select = jnp.where(hit, HEAD_SIZE ** (-0.5), 0.0).astype(jnp.bfloat16)
        return jnp.dot(q_ref[...], select, preferred_element_type=jnp.float32).astype(jnp.bfloat16)

    @pl.when(jnp.logical_not(has_cache))
    def _():
        peak_ref[...] = jnp.full_like(peak_ref, NEGATIVE)
        sum_ref[...] = jnp.zeros_like(sum_ref)
        acc_ref[...] = jnp.zeros_like(acc_ref)

    @pl.when(has_cache)
    def _():
        even_pos = base + 2 * lax.broadcasted_iota(jnp.int32, (1, pairs), 1)
        even_bias = jnp.where(even_pos < length, 0.0, NEGATIVE)
        odd_bias = jnp.where(even_pos + 1 < length, 0.0, NEGATIVE)
        @pl.loop(0, heads // group)
        def _(j):
            for i in range(group):
                g = j * group + i
                keys = k_ref[0, j]
                values = v_ref[0, j]
                even = lax.dot_general(pick(g, 0), keys, nt, preferred_element_type=jnp.float32) + even_bias
                odd = lax.dot_general(pick(g, 1), keys, nt, preferred_element_type=jnp.float32) + odd_bias
                peak = jnp.max(jnp.maximum(even, odd), axis=1, keepdims=True)
                even = jnp.exp(even - peak)
                odd = jnp.exp(odd - peak)
                total = jnp.sum(even + odd, axis=1, keepdims=True)
                mix_even = jnp.dot(even.astype(jnp.bfloat16), values, preferred_element_type=jnp.float32)
                mix_odd = jnp.dot(odd.astype(jnp.bfloat16), values, preferred_element_type=jnp.float32)
                mixed = jnp.where(out_lane < HEAD_SIZE, mix_even, mix_odd)
                peak_ref[g] = jnp.broadcast_to(peak, (rows, 128))
                sum_ref[g] = jnp.broadcast_to(total, (rows, 128))
                acc_ref[g] = mixed

    @pl.when(has_fresh)
    def _():
        row_q = dest * rows + lax.broadcasted_iota(jnp.int32, (rows, rows), 0)
        row_k = me * rows + lax.broadcasted_iota(jnp.int32, (rows, rows), 1)
        bias = jnp.where(row_k <= row_q, 0.0, NEGATIVE)
        @pl.loop(0, heads // group)
        def _(j):
            for i in range(group):
                g = j * group + i
                score = lax.dot_general(pick(g, 0), fk_ref[j], nt, preferred_element_type=jnp.float32) + bias
                old = peak_ref[g][:, :1]
                peak = jnp.maximum(old, jnp.max(score, axis=1, keepdims=True))
                weight = jnp.exp(score - peak)
                factor = jnp.exp(old - peak)
                total = sum_ref[g][:, :1] * factor + jnp.sum(weight, axis=1, keepdims=True)
                mix = jnp.dot(weight.astype(jnp.bfloat16), fv_ref[j], preferred_element_type=jnp.float32)
                acc_ref[g] = acc_ref[g] * factor + mix
                peak_ref[g] = jnp.broadcast_to(peak, (rows, 128))
                sum_ref[g] = jnp.broadcast_to(total, (rows, 128))

    tail = jnp.zeros((rows, 128), jnp.float32)
    left = None
    for g in range(heads):
        acc = acc_ref[g]
        acc = acc + pltpu.roll(acc, HEAD_SIZE, 1)
        total = sum_ref[g]
        some = total > 0.0
        safe = jnp.where(some, total, 1.0)
        level = jnp.where(some, peak_ref[g] + jnp.log(safe), NEGATIVE)
        high = level.astype(jnp.bfloat16).astype(jnp.float32)
        middle = (level - high).astype(jnp.bfloat16).astype(jnp.float32)
        low = level - high - middle
        tail = jnp.where(out_lane == g, high, tail)
        tail = jnp.where(out_lane == heads + g, middle, tail)
        tail = jnp.where(out_lane == 2 * heads + g, low, tail)
        result = acc / safe
        if g % 2 == 0:
            left = result
        if g % 2 == 1 or g == heads - 1:
            block = jnp.where(out_lane < HEAD_SIZE, left, result)
            out_ref[0, :, g // 2 * 128 : g // 2 * 128 + 128] = block.astype(out_ref.dtype)
    out_ref[0, :, out_ref.shape[2] - 128 :] = tail.astype(out_ref.dtype)


def attend(info, query, keys, values, fresh_key, fresh_value, rows, local_q):
    local_kv, pairs = keys.shape[1], keys.shape[2]
    group = local_q // local_kv
    per = FRESH_TOKENS // rows
    dests = query.shape[0] // rows
    cache_spec = pl.BlockSpec((1, local_kv, pairs, 128), lambda d, info: (d // per, 0, 0, 0))
    fresh_spec = pl.BlockSpec((local_kv, rows, 128), lambda d, info: (0, 0, 0))
    columns = (local_q + 1) // 2 * 128 + 128
    return pl.pallas_call(
        functools.partial(attend_kernel, group),
        grid_spec=pltpu.PrefetchScalarGridSpec(
            num_scalar_prefetch=1,
            grid=(dests,),
            in_specs=[
                pl.BlockSpec((rows, local_q * HEAD_SIZE), lambda d, info: (d, 0)),
                cache_spec,
                cache_spec,
                fresh_spec,
                fresh_spec,
            ],
            out_specs=pl.BlockSpec((1, rows, columns), lambda d, info: (d, 0, 0)),
            scratch_shapes=[pltpu.VMEM((local_q, rows, 128), jnp.float32)] * 3,
        ),
        out_shape=jax.ShapeDtypeStruct((dests, rows, columns), jnp.bfloat16),
        compiler_params=pltpu.CompilerParams(vmem_limit_bytes=40 * 1024 * 1024),
        cost_estimate=pl.CostEstimate(
            flops=8 * query.size * pairs * 2, bytes_accessed=16 << 20, transcendentals=query.size * pairs // 32
        ),
    )(info, query, keys, values, fresh_key, fresh_value)


def nearest(z, j):
    up = jnp.where(z == 1, jnp.where(j == 0, 1, jnp.where(j == 1, 0, j)), j)
    down = jnp.where(z == 2, jnp.where(j == 0, 2, jnp.where(j == 1, 3, 3 - j)), 3 - j)
    return jnp.where(z < 2, up, down)


def lanes_of(rows):
    return lax.broadcasted_iota(jnp.int32, (rows, 128), 1)


def unit_rows(count):
    return jnp.where(lax.broadcasted_iota(jnp.int32, (count, 128), 0) == lanes_of(count), 1.0, 0.0).astype(jnp.bfloat16)


def read_levels(packed, heads):
    split = lax.dot_general(packed, unit_rows(16), (((0,), (0,)), ((), ())), preferred_element_type=jnp.float32)
    return split + pltpu.roll(split, 128 - heads, 1)


def write_levels(level, heads):
    lane = lanes_of(level.shape[0])
    high = level.astype(jnp.bfloat16).astype(jnp.float32)
    low = level - high
    split = jnp.where(lane < heads, high, jnp.where(lane < 2 * heads, pltpu.roll(low, heads, 1), 0.0))
    nt = (((1,), (1,)), ((), ()))
    return lax.dot_general(unit_rows(16), split.astype(jnp.bfloat16), nt, preferred_element_type=jnp.float32)


def merge(pieces, heads):
    rows = pieces[0].shape[0] - 16
    lane = lanes_of(rows)
    levels = [read_levels(piece[rows:, :rows], heads) for piece in pieces]
    peak = functools.reduce(jnp.maximum, levels)
    weights = [jnp.exp(level - peak) for level in levels]
    total = functools.reduce(jnp.add, weights)
    weights = [weight / total for weight in weights]
    tiles = []
    for tile in range(heads // 2):
        mixed = None
        for piece, weight in zip(pieces, weights):
            factor = jnp.where(lane < 64, weight[:, 2 * tile : 2 * tile + 1], weight[:, 2 * tile + 1 : 2 * tile + 2])
            term = piece[:rows, tile * 128 : tile * 128 + 128].astype(jnp.float32) * factor
            mixed = term if mixed is None else mixed + term
        tiles.append(mixed)
    return tiles, peak + jnp.log(total)


def layer_kernel(
    lens_ref, tokens_ref, gains_ref, wq_ref, wk_ref, wv_ref, freqs_ref, ids_ref, k_ref, v_ref, w_out_ref, router_ref,
    down_ref, raw_ref,
    attn_ref, out_ref,
    queries, keys, values, mixed, level_tail, sent, held, peer_x, merged, peer_z, parting, half_sum, got_twin, got_across, joined,
    fresh_keys, fresh_values, raw, packed_ref, gate_up_ref, blocks, hidden, other_half, own_half, from_core, from_y, kept, passed, from_x, partial, from_z, final,
    sem_qz, sem_qx, got_q, sem_x, got_x, sem_z, got_z, sem_t, got_t, sem_w, got_w, sem_raw,
    sem_away, sem_side, sem_core, got_link, got_core, sem_lend, got_lend,
    sem_a, got_a, sem_b, got_b, sem_c, got_c, sem_d, got_d, sem_e, got_e,
):
    units = down_ref.shape[0]
    quarter = tokens_ref.shape[1] // 4
    rows, features = tokens_ref.shape[0], wq_ref.shape[0]
    heads = features // 64
    group = heads // k_ref.shape[1]
    pairs = k_ref.shape[2]
    width = tokens_ref.shape[1]
    half = width // 2
    s, t = lax.axis_index("seq"), lax.axis_index("tp")
    z, x = s // 2, s % 2
    y, c = t // 2, t % 2
    mesh_id = pl.DeviceIdType.MESH
    side = (z * 2 + 1 - x, t)
    across = (s, (1 - y) * 2 + c)
    twin = (s, y * 2 + 1 - c)
    mine = pl.ds(pl.multiple_of(c * half, 128), half)
    others = pl.ds(pl.multiple_of((1 - c) * half, 128), half)
    f32, bf16 = jnp.float32, jnp.bfloat16
    nt = (((1,), (1,)), ((), ()))

    barrier = pltpu.get_barrier_semaphore()
    for peer in (side, across, twin):
        pl.semaphore_signal(barrier, inc=1, device_id=peer, device_id_type=mesh_id)
    for step in range(1, 8):
        @pl.when((s + step) % 8 != s // 2 * 2 + 1 - x)
        def _():
            pl.semaphore_signal(barrier, inc=1, device_id=((s + step) % 8, t), device_id_type=mesh_id)

    def fetch(part):
        return pltpu.make_async_copy(
            raw_ref.at[:, :, :, pl.ds(part * 128, 128)], raw.at[part % 2], sem_raw.at[part % 2])

    fetch(0).start()
    fetch(1).start()
    normed = rms_norm(tokens_ref[...].astype(f32), gains_ref[0:1]).astype(bf16)
    quarter_lane = lanes_of(rows) % 64 < 32

    position = lens_ref[z] + x * rows + lax.broadcasted_iota(jnp.int32, (rows, 128), 0)
    angles = position.astype(f32) * freqs_ref[0:1, :]
    cosine = jnp.cos(angles)
    sine = jnp.where(quarter_lane, -jnp.sin(angles), jnp.sin(angles))

    def rotate(tile):
        partner = jnp.where(quarter_lane, pltpu.roll(tile, 96, 1), pltpu.roll(tile, 32, 1))
        return (tile * cosine + partner * sine).astype(bf16)

    projected = lax.dot_general(normed, wq_ref[...], nt, preferred_element_type=f32)
    for tile in range(features // 128):
        queries[s, :rows, tile * 128 : tile * 128 + 128] = rotate(projected[:, tile * 128 : tile * 128 + 128])
    queries[s, rows:, :rows] = ids_ref[...]
    pl.semaphore_wait(barrier, 9)

    def weight_copy(n):
        to = (s + 1 + n % 7) % 8
        cut = n // 7
        depth = packed_ref.shape[1]
        part = depth // 4
        source = pl.ds(pl.multiple_of(cut * part, 16), part)
        target = pl.ds(pl.multiple_of(s * depth + cut * part, 16), part)
        return pltpu.make_async_remote_copy(
            packed_ref.at[to, source], gate_up_ref.at[target], sem_w.at[n], got_w.at[s, cut],
            device_id=(to, t), device_id_type=mesh_id)

    def arrived_w(origin, cut):
        part = packed_ref.shape[1] // 4
        target = pl.ds(pl.multiple_of(origin * packed_ref.shape[1] + cut * part, 16), part)
        return pltpu.make_async_remote_copy(
            packed_ref.at[0, :part], gate_up_ref.at[target], sem_w.at[0], got_w.at[origin, cut],
            device_id=side, device_id_type=mesh_id)

    def pump(first, count):
        for n in range(count):
            weight_copy(first + n).start()

    def query_z(r, direction):
        b = r * 2 + x
        return pltpu.make_async_remote_copy(
            queries.at[b], queries.at[b], sem_qz.at[r, (direction + 1) // 2], got_q.at[b],
            device_id=((z + direction) * 2 + x, t), device_id_type=mesh_id)

    def query_x(r):
        b = r * 2 + x
        return pltpu.make_async_remote_copy(
            queries.at[b], queries.at[b], sem_qx.at[r], got_q.at[b], device_id=side, device_id_type=mesh_id)

    def arrived_q(b):
        return pltpu.make_async_remote_copy(
            queries.at[b], queries.at[b], sem_qx.at[0], got_q.at[b], device_id=side, device_id_type=mesh_id)

    def part_x(i):
        return pltpu.make_async_remote_copy(
            sent.at[i], peer_x.at[i], sem_x.at[i], got_x.at[i], device_id=side, device_id_type=mesh_id)

    def part_z(i):
        return pltpu.make_async_remote_copy(
            merged.at[i], peer_z.at[z], sem_z.at[i], got_z.at[z],
            device_id=(nearest(z, i + 1) * 2 + x, t), device_id_type=mesh_id)

    def arrived_z(z_from):
        return pltpu.make_async_remote_copy(
            merged.at[0], peer_z.at[z_from], sem_z.at[0], got_z.at[z_from], device_id=side, device_id_type=mesh_id)

    for direction in (-1, 1):
        @pl.when((z + direction >= 0) & (z + direction < 4))
        def _():
            query_z(z, direction).start()
    query_x(z).start()

    at_start, at_head, at_tp, at_gather = WEIGHT_PLAN
    after_heads = at_start + 12 * at_head
    after_tp = after_heads + 4 * at_tp
    base = s * (2 * pairs)
    row_lane = lanes_of(rows)
    fresh_keys[...] = rotate(lax.dot_general(normed, wk_ref[...], nt, preferred_element_type=f32))
    fresh_values[...] = lax.dot_general(normed, wv_ref[...], nt, preferred_element_type=f32).astype(bf16)
    low = lanes_of(raw_ref.shape[2]) < 64
    for part in range(4):
        fetch(part).wait()
        for pair in range(raw_ref.shape[0] // 2):
            for which in range(2):
                one = raw[part % 2, 2 * pair, which].astype(f32)
                two = raw[part % 2, 2 * pair + 1, which].astype(f32)
                at = pl.ds(pair * 256 + which * 128, 128)
                packed_ref[2 * part, :, at] = jnp.where(low, one, pltpu.roll(two, 64, 1)).astype(bf16)
                packed_ref[2 * part + 1, :, at] = jnp.where(low, pltpu.roll(one, 64, 1), two).astype(bf16)
        if part < 2:
            fetch(part + 2).start()
    gate_up_ref[pl.ds(pl.multiple_of(s * packed_ref.shape[1], 16), packed_ref.shape[1]), :] = packed_ref[s]
    pump(0, at_start)

    def spread(block, fill, scale):
        plain = block.astype(f32)
        if scale != 1.0:
            plain = plain * scale
        turned = pltpu.roll(plain, 64, 1)
        keep = lanes_of(block.shape[0]) < 64
        return (
            (jnp.where(keep, plain, fill).astype(bf16), jnp.where(keep, turned, fill).astype(bf16)),
            (jnp.where(keep, fill, turned).astype(bf16), jnp.where(keep, fill, plain).astype(bf16)),
        )

    def attend(r, fresh, between, pumped):
        length = lens_ref[r]
        slot = lax.broadcasted_iota(jnp.int32, (1, 2 * pairs), 1)
        position = base + 2 * (slot % pairs) + slot // pairs
        bias = jnp.where(position < length, 0.0, NEGATIVE)
        for j in range(heads // group):
            if j == 1:
                between()
            key_two = spread(k_ref[r, j], 0.0, 0.125)
            value_two = spread(v_ref[r, j], 1.0, 1.0)
            for parity in range(2):
                keys[parity, :pairs] = key_two[parity][0]
                keys[parity, pairs : 2 * pairs] = key_two[parity][1]
                values[parity, :pairs] = value_two[parity][0]
                values[parity, pairs : 2 * pairs] = value_two[parity][1]
            if fresh:
                new_keys = spread(fresh_keys[...], 0.0, 0.125)
                new_values = spread(fresh_values[...], 1.0, 1.0)
            for g in range(j * group, (j + 1) * group):
                parity = g % 2
                for part in range(2):
                    query = queries[r * 2 + part, :rows, g // 2 * 128 : g // 2 * 128 + 128]
                    score = lax.dot_general(query, keys[parity], nt, preferred_element_type=f32) + bias
                    peak = jnp.max(score, axis=1, keepdims=True)
                    if fresh:
                        new_key = new_keys[parity][j]
                        new_value = new_values[parity][j]
                        row_q = part * rows + lax.broadcasted_iota(jnp.int32, (rows, rows), 0)
                        row_k = x * rows + lax.broadcasted_iota(jnp.int32, (rows, rows), 1)
                        new_score = lax.dot_general(query, new_key, nt, preferred_element_type=f32)
                        new_score = new_score + jnp.where(row_k <= row_q, 0.0, NEGATIVE)
                        peak = jnp.maximum(peak, jnp.max(new_score, axis=1, keepdims=True))
                    weight = jnp.exp(score - peak).astype(bf16)
                    total = jnp.dot(weight, values[parity], preferred_element_type=f32)
                    if fresh:
                        weight = jnp.exp(new_score - peak).astype(bf16)
                        total = total + jnp.dot(weight, new_value, preferred_element_type=f32)
                    turned = pltpu.roll(total, 64, 1)
                    if parity == 0:
                        sums = jnp.where(row_lane < 64, turned, total)
                    else:
                        sums = jnp.where(row_lane < 64, total, turned)
                    level = peak + jnp.log(sums)
                    result = total / sums
                    at = pl.ds(part * rows, rows)
                    if g == 0:
                        level_tail[at, :] = level
                    else:
                        level_tail[at, :] = jnp.where(row_lane == g, level, level_tail[at, :])
                    tile = pl.ds(g // 2 * 128, 128)
                    if parity == 0:
                        mixed[at, tile] = result
                    else:
                        mixed[at, tile] = jnp.where(row_lane < 64, mixed[at, tile], result)
                if parity == 1:
                    pump(at_start + (pumped + g // 2) * at_head, at_head)

    def hand_over(i):
        own = pl.ds(pl.multiple_of(x * rows, rows), rows)
        away = pl.ds(pl.multiple_of((1 - x) * rows, rows), rows)
        sent[i, :rows, :] = mixed[away, :].astype(bf16)
        sent[i, rows:, :rows] = write_levels(level_tail[away, :], heads).astype(bf16)
        part_x(i).start()
        held[i, :rows, :] = mixed[own, :].astype(bf16)
        held[i, rows:, :rows] = write_levels(level_tail[own, :], heads).astype(bf16)

    def merge_x(i):
        part_x(i).wait_recv()
        tiles, level = merge([held[i], peer_x[i]], heads)
        for n, tile in enumerate(tiles):
            merged[i, :rows, n * 128 : n * 128 + 128] = tile.astype(bf16)
        merged[i, rows:, :rows] = write_levels(level, heads).astype(bf16)

    def forward(i):
        r = nearest(z, i + 1)
        arrived_q(r * 2 + x).wait_recv()
        for direction in (-1, 1):
            @pl.when(((z - r) * direction > 0) & (z + direction >= 0) & (z + direction < 4))
            def _():
                query_z(r, direction).start()
        query_x(r).start()

    forward(0)
    forward(1)

    def step(i, carry):
        r = nearest(z, i + 1)
        arrived_q(r * 2 + 1 - x).wait_recv()

        def between():
            @pl.when(i == 0)
            def _():
                forward(2)

        attend(r, False, between, 3 * i)
        hand_over(i)

        @pl.when(i > 0)
        def _():
            merge_x(i - 1)
            part_z(i - 1).start()
        return carry

    lax.fori_loop(0, 3, step, 0)
    arrived_q(z * 2 + 1 - x).wait_recv()

    def between():
        merge_x(2)
        part_z(2).start()

    attend(z, True, between, 9)
    hand_over(3)
    merge_x(3)
    pieces = [merged[3]]
    for step_z in range(1, 4):
        z_from = (z + step_z) % 4
        arrived_z(z_from).wait_recv()
        pieces.append(peer_z[z_from])
    tiles, _ = merge(pieces, heads)
    heads_out = jnp.concatenate([tile.astype(bf16) for tile in tiles], axis=1)

    def exchange(n, source, target, to):
        return pltpu.make_async_remote_copy(
            source, target, sem_t.at[n], got_t.at[n], device_id=to, device_id_type=mesh_id)

    parting[...] = jnp.dot(heads_out, w_out_ref[:, others], preferred_element_type=f32).astype(bf16)
    first = exchange(0, parting, got_twin, twin)
    first.start()
    pump(after_heads + 0 * at_tp, at_tp)
    own = jnp.dot(heads_out, w_out_ref[:, mine], preferred_element_type=f32)
    first.wait_recv()
    half_sum[...] = (own + got_twin[...].astype(f32)).astype(bf16)
    second = exchange(1, half_sum, got_across, across)
    second.start()
    pump(after_heads + 1 * at_tp, at_tp)
    pump(after_heads + 2 * at_tp, at_tp)
    second.wait_recv()
    joined[:, mine] = (half_sum[...].astype(f32) + got_across[...].astype(f32)).astype(bf16)
    last = exchange(2, joined.at[:, mine], joined.at[:, mine], twin)
    last.start()
    pump(after_heads + 3 * at_tp, at_tp)
    last.wait_recv()
    attn_ref[...] = joined[...]
    stream = tokens_ref[...].astype(f32) + joined[...].astype(f32)
    normed = rms_norm(stream, gains_ref[1:2])
    blocks[s] = normed.astype(bf16)

    third = half // 3
    duty = pl.ds(pl.multiple_of(c * half + y * third, 128), 2 * third)
    lent = pl.ds(pl.multiple_of(c * half + y * 2 * third, 128), third)
    borrowed = pl.ds(pl.multiple_of(c * half + (1 - y) * 2 * third, 128), third)

    def away(b, direction):
        return pltpu.make_async_remote_copy(
            blocks.at[b, :, duty], blocks.at[b, :, duty], sem_away.at[b, (direction + 1) // 2], got_link.at[b],
            device_id=((z + direction) * 2 + x, t), device_id_type=mesh_id)

    def sideways(b):
        return pltpu.make_async_remote_copy(
            blocks.at[b, :, duty], blocks.at[b, :, duty], sem_side.at[b], got_link.at[b],
            device_id=side, device_id_type=mesh_id)

    def lend(b):
        return pltpu.make_async_remote_copy(
            blocks.at[b, :, lent], blocks.at[b, :, lent], sem_lend.at[b], got_lend.at[b],
            device_id=across, device_id_type=mesh_id)

    def borrow(b):
        return pltpu.make_async_remote_copy(
            blocks.at[b, :, borrowed], blocks.at[b, :, borrowed], sem_lend.at[b], got_lend.at[b],
            device_id=across, device_id_type=mesh_id)

    def to_twin(b):
        return pltpu.make_async_remote_copy(
            blocks.at[b, :, mine], blocks.at[b, :, mine], sem_core.at[b], got_core.at[b],
            device_id=twin, device_id_type=mesh_id)

    def copy_a(i):
        return pltpu.make_async_remote_copy(
            other_half.at[i], from_core.at[i], sem_a.at[i], got_a.at[i], device_id=twin, device_id_type=mesh_id)

    def copy_b(i):
        cut = pl.ds(pl.multiple_of((1 - y) * quarter, 128), quarter)
        return pltpu.make_async_remote_copy(
            own_half.at[i, :, cut], from_y.at[i], sem_b.at[i], got_b.at[i], device_id=across, device_id_type=mesh_id)

    def copy_c(j):
        return pltpu.make_async_remote_copy(
            passed.at[j], from_x.at[j], sem_c.at[j], got_c.at[j], device_id=side, device_id_type=mesh_id)

    def copy_d(j):
        return pltpu.make_async_remote_copy(
            partial.at[j], from_z.at[z], sem_d.at[j], got_d.at[z],
            device_id=(nearest(z, 3 - j) * 2 + x, t), device_id_type=mesh_id)

    def arrive_d(z_from):
        return pltpu.make_async_remote_copy(
            partial.at[0], from_z.at[z_from], sem_d.at[0], got_d.at[z_from],
            device_id=side, device_id_type=mesh_id)

    for direction in (-1, 1):
        @pl.when((z + direction >= 0) & (z + direction < 4))
        def _():
            away(s, direction).start()
    sideways(s).start()

    def block_of(i):
        k = i % 2
        return nearest(z, i // 2) * 2 + jnp.where(k == 0, x, 1 - x)


    def take_z(j):
        b = nearest(z, j) * 2 + x
        sideways(b).wait_recv()
        for direction in (-1, 1):
            @pl.when(((z - nearest(z, j)) * direction > 0) & (z + direction >= 0) & (z + direction < 4))
            def _():
                away(b, direction).start()
        sideways(b).start()
        lend(b).start()

    def take_x(j):
        b = nearest(z, j) * 2 + 1 - x
        sideways(b).wait_recv()
        lend(b).start()

    def finish(b):
        borrow(b).wait_recv()
        to_twin(b).start()

    for j in range(4):
        pump(after_tp + j * at_gather, at_gather)
        if j < 3:
            take_z(j + 1)
        if j > 0:
            finish(nearest(z, j) * 2 + x)
            finish(nearest(z, j - 1) * 2 + 1 - x)
        take_x(j)
    finish(nearest(z, 3) * 2 + 1 - x)
    pump(after_tp + 4 * at_gather, 28 - after_tp - 4 * at_gather)
    for n in range(28):
        weight_copy(n).wait_send()
    for step_s in range(1, 8):
        for cut in range(4):
            arrived_w((s + step_s) % 8, cut).wait_recv()

    experts = router_ref.shape[1]
    expert_of = lax.broadcasted_iota(jnp.int32, (rows, experts), 1).astype(f32)
    as_columns = jnp.where(lax.broadcasted_iota(jnp.int32, ((queries.shape[1] - rows), 128), 0) == lanes_of((queries.shape[1] - rows)), 1.0, 0.0).astype(jnp.bfloat16)
    expert_lane = lax.broadcasted_iota(jnp.int32, (experts, units), 0)
    expert_unit = lax.broadcasted_iota(jnp.int32, (experts, units), 1)

    def compute(i, carry):
        @pl.when(i < 8)
        def _():
            b = nearest(z, 3 - i // 2) * 2 + jnp.where(i % 2 == 0, 1 - x, x)

            @pl.when(i < 7)
            def _():
                to_twin(b).wait_recv()

            tokens = blocks[b]
            logits = jnp.dot(tokens, router_ref[...], preferred_element_type=f32)
            named = lax.dot_general(queries[b, rows:, :rows], as_columns, (((0,), (0,)), ((), ())), preferred_element_type=f32)
            chosen = named[:, 0:1] == expert_of
            for k in range(1, 8):
                chosen = chosen | (named[:, k : k + 1] == expert_of)
            logits = jnp.where(chosen, logits, NEGATIVE)
            gates = jnp.where(chosen, jnp.exp(logits - jnp.max(logits, axis=1, keepdims=True)), 0.0)
            share = gates / jnp.sum(gates, axis=1, keepdims=True)
            high = share.astype(jnp.bfloat16)
            low = (share - high.astype(f32)).astype(jnp.bfloat16)
            spread = jnp.where(expert_lane == t * (units // 64) + expert_unit // 64, 1.0, 0.0).astype(jnp.bfloat16)
            shares = jnp.dot(high, spread, preferred_element_type=f32) + jnp.dot(low, spread, preferred_element_type=f32)
            for p in range(units // 128):
                both = jnp.dot(tokens, gate_up_ref[:, p * 256 : p * 256 + 256], preferred_element_type=f32)
                gate, up = both[:, :128], both[:, 128:]
                value = gate / (1.0 + jnp.exp(-gate)) * up * shares[:, p * 128 : p * 128 + 128]
                hidden[:, p * 128 : p * 128 + 128] = value.astype(jnp.bfloat16)
            other_half[i] = jnp.dot(hidden[...], down_ref[:, others], preferred_element_type=f32).astype(jnp.bfloat16)
            copy_a(i).start()
            own_half[i] = jnp.dot(hidden[...], down_ref[:, mine], preferred_element_type=f32).astype(jnp.bfloat16)

        @pl.when((i >= 1) & (i < 9))
        def _():
            n = i - 1
            copy_a(n).wait_recv()
            own_half[n] = (own_half[n].astype(f32) + from_core[n].astype(f32)).astype(jnp.bfloat16)
            copy_b(n).start()

        @pl.when((i >= 4) & (i < 12))
        def _():
            n = i - 4
            copy_b(n).wait_recv()
            cut = pl.ds(pl.multiple_of(y * quarter, 128), quarter)
            total = (own_half[n, :, cut].astype(f32) + from_y[n].astype(f32)).astype(jnp.bfloat16)

            @pl.when(n % 2 == 1)
            def _():
                kept[n // 2] = total

            @pl.when(n % 2 == 0)
            def _():
                passed[n // 2] = total
                copy_c(n // 2).start()

        @pl.when((i >= 6) & (i % 2 == 0))
        def _():
            j = i // 2 - 3
            copy_c(j).wait_recv()
            partial[j] = (kept[j].astype(f32) + from_x[j].astype(f32)).astype(jnp.bfloat16)

            @pl.when(j < 3)
            def _():
                copy_d(j).start()
        return carry

    lax.fori_loop(0, 13, compute, 0)

    total = partial[3].astype(f32)
    for step_z in range(1, 4):
        z_from = (z + step_z) % 4
        arrive_d(z_from).wait_recv()
        total = total + from_z[z_from].astype(f32)

    def copy_e(n, to):
        at = c * half + y * quarter if n == 0 else c * half
        size = quarter if n == 0 else half
        cut = pl.ds(pl.multiple_of(at, 128), size)
        return pltpu.make_async_remote_copy(
            final.at[:, cut], final.at[:, cut], sem_e.at[n], got_e.at[n], device_id=to, device_id_type=mesh_id)

    final[:, pl.ds(pl.multiple_of(c * half + y * quarter, 128), quarter)] = total.astype(jnp.bfloat16)
    copy_e(0, across).start()
    copy_e(0, across).wait_recv()
    copy_e(1, twin).start()
    copy_e(1, twin).wait_recv()
    out_ref[...] = final[...]

    def drain(i, carry):
        b = block_of(i)
        zj = nearest(z, i // 2)

        @pl.when(i > 0)
        def _():
            to_twin(b).wait_send()
            lend(b).wait_send()

        @pl.when(i % 2 == 0)
        def _():
            sideways(b).wait_send()
            for direction in (-1, 1):
                @pl.when(((z - zj) * direction >= 0) & (z + direction >= 0) & (z + direction < 4))
                def _():
                    away(b, direction).wait_send()
            copy_c(i // 2).wait_send()

            @pl.when(i < 6)
            def _():
                copy_d(i // 2).wait_send()

        copy_a(i).wait_send()
        copy_b(i).wait_send()
        return carry

    lax.fori_loop(0, 8, drain, 0)
    copy_e(0, across).wait_send()
    copy_e(1, twin).wait_send()
    for j in range(4):
        query_x(nearest(z, j)).wait_send()
        part_x(j).wait_send()
        for direction in (-1, 1):
            @pl.when(((z - nearest(z, j)) * direction >= 0) & (z + direction >= 0) & (z + direction < 4))
            def _():
                query_z(nearest(z, j), direction).wait_send()
    for j in range(3):
        part_z(j).wait_send()
    first.wait_send()
    second.wait_send()
    last.wait_send()


def layer(lens, tokens, gains, w_query, w_key, w_value, freqs, ids, keys, values, w_out, router, down, gate_up):
    features = w_query.shape[0]
    rows, width = tokens.shape
    extra = ids.shape[0]
    requests, local_kv, pairs, _ = keys.shape
    units = down.shape[0]
    half, quarter = width // 2, width // 4
    bf16, f32 = jnp.bfloat16, jnp.float32
    dma = pltpu.SemaphoreType.DMA
    vmem = pl.BlockSpec(memory_space=pltpu.VMEM)
    scores = requests * FRESH_TOKENS * (features // 64) * 2 * pairs
    return pl.pallas_call(
        layer_kernel,
        out_shape=[jax.ShapeDtypeStruct((rows, width), bf16)] * 2,
        in_specs=[pl.BlockSpec(memory_space=pltpu.SMEM)] + [vmem] * 12 + [pl.BlockSpec(memory_space=pl.ANY)],
        out_specs=[vmem] * 2,
        scratch_shapes=[
            pltpu.VMEM((8, rows + extra, features), bf16),
            pltpu.VMEM((2, 2 * pairs, 128), bf16),
            pltpu.VMEM((2, 2 * pairs, 128), bf16),
            pltpu.VMEM((2 * rows, features), f32),
            pltpu.VMEM((2 * rows, 128), f32),
            pltpu.VMEM((4, rows + 16, features), bf16),
            pltpu.VMEM((4, rows + 16, features), bf16),
            pltpu.VMEM((4, rows + 16, features), bf16),
            pltpu.VMEM((4, rows + 16, features), bf16),
            pltpu.VMEM((4, rows + 16, features), bf16),
            pltpu.VMEM((rows, width // 2), bf16),
            pltpu.VMEM((rows, width // 2), bf16),
            pltpu.VMEM((rows, width // 2), bf16),
            pltpu.VMEM((rows, width // 2), bf16),
            pltpu.VMEM((rows, width), bf16),
            pltpu.VMEM((rows, 128), bf16),
            pltpu.VMEM((rows, 128), bf16),
            pltpu.VMEM((2,) + gate_up.shape[:3] + (128,), bf16),
            pltpu.VMEM((8, gate_up.shape[2], 2 * units), bf16),
            pltpu.VMEM((width, 2 * units), bf16),
            pltpu.VMEM((8, rows, width), bf16),
            pltpu.VMEM((rows, units), bf16),
            pltpu.VMEM((8, rows, half), bf16),
            pltpu.VMEM((8, rows, half), bf16),
            pltpu.VMEM((8, rows, half), bf16),
            pltpu.VMEM((8, rows, quarter), bf16),
            pltpu.VMEM((4, rows, quarter), bf16),
            pltpu.VMEM((4, rows, quarter), bf16),
            pltpu.VMEM((4, rows, quarter), bf16),
            pltpu.VMEM((4, rows, quarter), bf16),
            pltpu.VMEM((4, rows, quarter), bf16),
            pltpu.VMEM((rows, width), bf16),
            dma((4, 2)), dma((4,)), dma((8,)), dma((4,)), dma((4,)), dma((4,)), dma((4,)), dma((3,)), dma((3,)), dma((28,)), dma((8, 4)), dma((2,)),
            dma((8, 2)), dma((8,)), dma((8,)), dma((8,)), dma((8,)), dma((8,)), dma((8,)),
            dma((8,)), dma((8,)), dma((8,)), dma((8,)), dma((4,)), dma((4,)), dma((4,)), dma((4,)), dma((2,)), dma((2,)),
        ],
        compiler_params=pltpu.CompilerParams(
            collective_id=0, has_side_effects=True, vmem_limit_bytes=60 * 1024 * 1024
        ),
        cost_estimate=pl.CostEstimate(flops=64 * 4 * scores, bytes_accessed=16 << 20, transcendentals=scores),
    )(lens, tokens, gains, w_query, w_key, w_value, freqs, ids, keys, values, w_out, router, down, gate_up)


def swap_cores(values):
    count = lax.axis_size("tp")
    return lax.ppermute(values, "tp", [(i, i ^ 1) for i in range(count)])


def sum_halves(mine, others):
    received = swap_cores(others.astype(jnp.bfloat16)).astype(jnp.float32)
    return (mine + received).astype(jnp.bfloat16)


def sum_chips(values):
    count = lax.axis_size("tp")
    step = 2
    total = values.astype(jnp.float32)
    while step < count:
        sent = total.astype(jnp.bfloat16)
        received = lax.ppermute(sent, "tp", [(i, i ^ step) for i in range(count)])
        total = sent.astype(jnp.float32) + received.astype(jnp.float32)
        step = step * 2
    return total.astype(jnp.bfloat16)


def join_halves(values, core):
    other = swap_cores(values)
    first = jnp.where(core == 0, values, other)
    second = jnp.where(core == 0, other, values)
    return jnp.concatenate([first, second], axis=1)


def per_device(
    tokens,
    norm1_gain,
    w_query,
    key_weight,
    value_weight,
    rotated_key_cache,
    stored_value_cache,
    cache_len,
    w_out,
    norm2_gain,
    w_router,
    expert_ids,
    w_gate_up,
    w_down,
):
    tok_rows, width = tokens.shape
    seq_pos = lax.axis_index("seq")
    tp_pos = lax.axis_index("tp")
    local_q = w_query.shape[0] // HEAD_SIZE
    local_kv = key_weight.shape[0] // HEAD_SIZE
    requests = rotated_key_cache.shape[0]
    span = rotated_key_cache.shape[2] // HEAD_SIZE
    inputs = tokens.astype(jnp.float32)
    devices = lax.axis_size("seq")
    local_experts, _, own_width, hidden_size = w_gate_up.shape
    own_hidden = hidden_size // devices
    normalized_input = rms_norm(inputs, norm1_gain).astype(jnp.bfloat16)
    row_ids = seq_pos * tok_rows + jnp.arange(tok_rows, dtype=jnp.int32)
    owners = row_ids // FRESH_TOKENS
    positions = lookup(cache_len, owners) + row_ids % FRESH_TOKENS
    angle_position = positions.astype(jnp.float32)
    query_vector = apply_rotary(
        apply_projection(normalized_input, w_query).reshape(tok_rows, local_q, HEAD_SIZE),
        angle_position,
    ).astype(jnp.bfloat16)
    units = local_experts * own_hidden
    by_owner = jnp.transpose(
        w_gate_up.reshape(local_experts, 2, own_width, devices, own_hidden), (3, 2, 1, 0, 4)
    ).reshape(width, 2 * units)
    fresh_key = apply_rotary(
        apply_projection(normalized_input, key_weight).reshape(tok_rows, local_kv, HEAD_SIZE),
        angle_position,
    ).astype(jnp.bfloat16)
    fresh_value = (
        apply_projection(normalized_input, value_weight)
        .astype(jnp.bfloat16)
        .reshape(tok_rows, local_kv, HEAD_SIZE)
    )
    all_query = lax.all_gather(
        query_vector.reshape(tok_rows, local_q * HEAD_SIZE), "seq", axis=0, tiled=True
    )
    all_query, by_owner = lax.optimization_barrier((all_query, by_owner))
    own_gate_up = lax.all_to_all(by_owner, "seq", 0, 0, tiled=True)
    paired = (requests, local_kv, span // 2, 2 * HEAD_SIZE)
    pad = ((0, 0), (0, 0), (0, HEAD_SIZE))
    parts = attend(
        jnp.concatenate([seq_pos[None].astype(jnp.int32), cache_len]),
        all_query,
        rotated_key_cache.reshape(paired),
        stored_value_cache.reshape(paired),
        jnp.pad(jnp.transpose(fresh_key, (1, 0, 2)), pad),
        jnp.pad(jnp.transpose(fresh_value, (1, 0, 2)), pad),
        tok_rows,
        local_q,
    )
    parts, own_gate_up = lax.optimization_barrier((parts, own_gate_up))
    parts = lax.all_to_all(parts, "seq", 0, 0, tiled=True)
    parts = parts.astype(jnp.float32)
    features = local_q * HEAD_SIZE
    tails = parts.shape[2] - 128
    pieces = parts[:, :, tails : tails + 3 * local_q]
    level = pieces[..., :local_q] + pieces[..., local_q : 2 * local_q] + pieces[..., 2 * local_q :]
    factor = jnp.exp(level - jnp.max(level, axis=0, keepdims=True))
    factor = factor / jnp.sum(factor, axis=0, keepdims=True)
    feature_head = jnp.arange(features, dtype=jnp.int32) // HEAD_SIZE
    widen = (jnp.arange(local_q, dtype=jnp.int32)[:, None] == feature_head[None, :]).astype(jnp.float32)
    factor = jnp.einsum("sth,hf->stf", factor, widen, precision=lax.Precision.HIGHEST)
    heads_out = jnp.sum(parts[:, :, :features] * factor, axis=0).astype(jnp.bfloat16)
    attn_part = jnp.dot(heads_out, w_out, preferred_element_type=jnp.float32)
    core = tp_pos % 2
    half = width // 2
    attn = sum_halves(
        lax.dynamic_slice_in_dim(attn_part, core * half, half, 1),
        lax.dynamic_slice_in_dim(attn_part, (1 - core) * half, half, 1),
    )
    attn = join_halves(sum_chips(attn), core).astype(jnp.float32)
    attn_out = attn.astype(jnp.bfloat16)
    normed2 = rms_norm(inputs + attn, norm2_gain).astype(jnp.bfloat16)
    logits = jnp.dot(normed2, w_router, preferred_element_type=jnp.float32)
    experts_all = w_router.shape[1]
    picked_all = expert_ids[:, :, None] == jnp.arange(experts_all, dtype=jnp.int32)[None, None, :]
    chosen = jnp.sum(jnp.where(picked_all, logits[:, None, :], 0.0), axis=-1)
    gates = jax.nn.softmax(chosen, axis=-1)
    local_ids = tp_pos * local_experts + jnp.arange(local_experts, dtype=jnp.int32)
    picked = expert_ids[:, :, None] == local_ids[None, None, :]
    share = jnp.sum(jnp.where(picked, gates[:, :, None], 0.0), axis=1)
    share_high = lax.reduce_precision(share, 8, 7)
    packed = jnp.concatenate(
        [
            lax.dynamic_slice_in_dim(normed2, core * half, half, 1),
            share_high.astype(jnp.bfloat16),
            (share - share_high).astype(jnp.bfloat16),
            jnp.zeros((tok_rows, 128 - 2 * local_experts), jnp.bfloat16),
        ],
        axis=1,
    )
    packed = lax.all_gather(packed, "seq", axis=0, tiled=True)
    others = swap_cores(packed[:, :half])
    unit_expert = jnp.arange(units, dtype=jnp.int32) // own_hidden
    lanes = jnp.arange(128, dtype=jnp.int32)
    spread = (lanes[:, None] % local_experts == unit_expert[None, :]) & (lanes[:, None] < 2 * local_experts)
    share_all = jnp.dot(packed[:, half:], spread.astype(jnp.bfloat16), preferred_element_type=jnp.float32)
    gate_up_mine = lax.dynamic_slice_in_dim(own_gate_up, core * half, half, 0)
    gate_up_others = lax.dynamic_slice_in_dim(own_gate_up, (1 - core) * half, half, 0)
    both = jnp.dot(packed[:, :half], gate_up_mine, preferred_element_type=jnp.float32)
    both = both + jnp.dot(others, gate_up_others, preferred_element_type=jnp.float32)
    hidden = (jax.nn.silu(both[:, :units]) * both[:, units:] * share_all).astype(jnp.bfloat16)
    down = w_down.reshape(units, width)
    down_mine = lax.dynamic_slice_in_dim(down, core * half, half, 1)
    down_others = lax.dynamic_slice_in_dim(down, (1 - core) * half, half, 1)
    moe_half = sum_halves(
        jnp.dot(hidden, down_mine, preferred_element_type=jnp.float32),
        jnp.dot(hidden, down_others, preferred_element_type=jnp.float32),
    )
    moe_half = lax.psum_scatter(moe_half, "seq", scatter_dimension=0, tiled=True)
    expert_out = join_halves(sum_chips(moe_half.astype(jnp.float32)), core)
    return (attn_out, expert_out)


def per_device_block(
    tokens,
    norm1_gain,
    w_query,
    key_weight,
    value_weight,
    rotated_key_cache,
    stored_value_cache,
    cache_len,
    w_out,
    norm2_gain,
    w_router,
    expert_ids,
    w_gate_up,
    w_down,
):
    tok_rows, width = tokens.shape
    local_kv = key_weight.shape[0] // HEAD_SIZE
    requests = rotated_key_cache.shape[0]
    span = rotated_key_cache.shape[2] // HEAD_SIZE
    devices = lax.axis_size("seq")
    units = w_gate_up.shape[0] * (w_gate_up.shape[3] // devices)
    lane = jnp.arange(128, dtype=jnp.int32)
    freqs = THETA ** (-((lane % 32).astype(jnp.float32) * (2.0 / HEAD_SIZE)))
    paired = (requests, local_kv, span // 2, 2 * HEAD_SIZE)
    return layer(
        cache_len,
        tokens,
        jnp.stack([norm1_gain, norm2_gain]),
        w_query,
        key_weight,
        value_weight,
        jnp.broadcast_to(freqs[None, :], (8, 128)),
        jnp.pad(expert_ids.T.astype(jnp.bfloat16), ((0, 8), (0, 0))),
        rotated_key_cache.reshape(paired),
        stored_value_cache.reshape(paired),
        w_out,
        w_router,
        w_down.reshape(units, width),
        w_gate_up,
    )


def solution(mesh):
    block = mesh.shape["seq"] == 8 and mesh.shape["tp"] == 4
    return jax.shard_map(
        per_device_block if block else per_device,
        mesh=mesh,
        in_specs=(
            P("seq", None),
            P(),
            P("tp", None),
            P("tp", None),
            P("tp", None),
            P(None, "tp", "seq"),
            P(None, "tp", "seq"),
            P(),
            P("tp", None),
            P(),
            P(),
            P("seq", None),
            P("tp", None, "seq", None),
            P("tp", "seq", None),
        ),
        out_specs=(P("seq", None), P("seq", None)),
        check_vma=False,
    )
```
